32 devices in a mesh: seq: 4 (over y, x), rows: 8 (over z, core).
Axes of the slice: x: 2, y: 2, z: 4, core: 2. Of those that a mesh axis runs over, the one named last changes fastest.
Arguments:
- frames: bfloat16 [8, 1024, 768], P('rows', 'seq'), may hold values from -6 to 6
- text_tokens: bfloat16 [8, 308, 768], P('rows'), may hold values from -6 to 6
- step_embed: bfloat16 [8, 4, 768], P('rows'), may hold values from -6 to 6
- segments: int32 [8, 1024], P('rows'), may hold values from 0 to 3, as said below
- cotangent: bfloat16 [8, 1024, 768], P('rows', 'seq'), may hold values from -6 to 6
- w_ada: bfloat16 [768, 4608], replicated, may hold values from -0.21875 to 0.21875
- b_ada: bfloat16 [4608], replicated, may hold values from -1.5 to 1.5
- w_qkv: bfloat16 [768, 2304], replicated, may hold values from -0.21875 to 0.21875
- w_out: bfloat16 [768, 768], replicated, may hold values from -1.75 to 1.75
- g_cross: bfloat16 [768], replicated, may hold values from 0.25 to 1.75
- w_cq: bfloat16 [768, 768], replicated, may hold values from -0.21875 to 0.21875
- w_ckv: bfloat16 [768, 1536], replicated, may hold values from -0.21875 to 0.21875
- w_co: bfloat16 [768, 768], replicated, may hold values from -0.875 to 0.875
- w_up: bfloat16 [768, 3072], replicated, may hold values from -0.21875 to 0.21875
- b_up: bfloat16 [3072], replicated, may hold values from -2.5 to 2.5
- w_down: bfloat16 [3072, 768], replicated, may hold values from -0.109375 to 0.109375
- b_down: bfloat16 [768], replicated, may hold values from -1.5 to 1.5
Outputs:
- output: bfloat16 [8, 1024, 768], P('rows', 'seq')
- d_frames: float32 [8, 1024, 768], P('rows', 'seq')
- d_text: float32 [8, 308, 768], P('rows', 'seq')
- d_step: float32 [8, 4, 768], P('rows', 'seq')
- d_w_ada: float32 [768, 4608], P('rows', 'seq')
- d_b_ada: float32 [4608], P('rows')
- d_w_qkv: float32 [768, 2304], P('rows', 'seq')
- d_w_out: float32 [768, 768], P('rows', 'seq')
- d_g_cross: float32 [768], P('rows')
- d_w_cq: float32 [768, 768], P('rows', 'seq')
- d_w_ckv: float32 [768, 1536], P('rows', 'seq')
- d_w_co: float32 [768, 768], P('rows', 'seq')
- d_w_up: float32 [768, 3072], P('rows', 'seq')
- d_b_up: float32 [3072], P('rows')
- d_w_down: float32 [3072, 768], P('rows', 'seq')
- d_b_down: float32 [768], P('rows')
The draws below stay inside these ranges and needn't reach their ends.
Inputs may be any that keep to these rules, and one draw needn't show every extreme that they name: `segments`: in each row the slot numbers start at 0, never fall and rise by one from item to item; each item covers a quarter, a half or all of the 1024 frames; some row holds four items.
All inputs are finite; a program needn't handle non-finite values.
Results may differ from the reference program's by a relative error of at most 0.02.
Values may be sent and summed in bfloat16 or wider, within the bound.
A program may use at most 192 MiB of HBM per device.

```python
import jax
import jax.numpy as jnp
from jax import lax

D = 768
HEADS = 12
HEAD = 64
FF = 3072
TXT = 77
ITEMS = 4
L = 1024
ROWS = 8


def draw_segments(key, part):
    ends_table = jnp.array([[1, 2, 3], [2, 4, 4], [4, 4, 4], [2, 3, 4], [1, 2, 4]], jnp.int32)
    pattern = jax.random.randint(key, (ROWS,), 0, 5, dtype=jnp.int32)
    pattern = jnp.where(jnp.arange(ROWS, dtype=jnp.int32) == 0, 0, pattern)
    row_ends = ends_table[pattern] * (L // ITEMS)
    frame_pos = jnp.arange(L, dtype=jnp.int32)
    return jnp.sum((frame_pos[None, :, None] >= row_ends[:, None, :]).astype(jnp.int32), axis=-1)


def block_scale(stream_key, extent, cuts, least, high):
    factor_of = 1.0
    for axis_at, parts in cuts:
        heights = jax.random.uniform(jax.random.fold_in(jax.random.fold_in(stream_key, 6), axis_at), (parts,), jnp.float32, least / len(cuts), high / len(cuts))
        factor_of = factor_of * jnp.repeat(jnp.exp(heights), extent[axis_at] // parts).reshape((-1,) + (1,) * (len(extent) - 1 - axis_at))
    return factor_of


def normal_values(key, shape, deviation, most, shards=(), held_as=jnp.bfloat16):
    values = deviation * jax.random.normal(key, shape, jnp.float32)
    if shards:
        values = values * block_scale(key, shape, shards, -0.22, 0.18)
    return jnp.clip(values, -most, most).astype(held_as)


def setup_inputs(seed: int = 0) -> dict:
    splits = jax.random.split(jax.random.key(seed), 18)
    return {
        "frames": normal_values(splits[0], (ROWS, L, D), 1.0, 6.0, ((0, 8), (1, 4))),
        "text_tokens": normal_values(splits[1], (ROWS, ITEMS * TXT, D), 1.0, 6.0, ((0, 8),)),
        "step_embed": normal_values(splits[2], (ROWS, ITEMS, D), 1.0, 6.0, ((0, 8),)),
        "segments": draw_segments(jax.random.fold_in(splits[17], 71), 0),
        "cotangent": normal_values(splits[4], (ROWS, L, D), 1.0, 6.0, ((0, 8), (1, 4))),
        "w_ada": normal_values(splits[5], (D, 6 * D), D ** -0.5, 0.21875),
        "b_ada": normal_values(splits[6], (6 * D,), 0.3, 1.5),
        "w_qkv": normal_values(splits[7], (D, 3 * D), D ** -0.5, 0.21875),
        "w_out": normal_values(splits[8], (D, D), (D // 64) ** -0.5, 1.75),
        "g_cross": jnp.clip(1.0 + 0.15 * jax.random.normal(splits[9], (D,), jnp.float32), 0.25, 1.75).astype(jnp.bfloat16),
        "w_cq": normal_values(splits[10], (D, D), D ** -0.5, 0.21875),
        "w_ckv": normal_values(splits[11], (D, 2 * D), D ** -0.5, 0.21875),
        "w_co": normal_values(splits[12], (D, D), (D // 16) ** -0.5, 0.875),
        "w_up": normal_values(splits[13], (D, FF), D ** -0.5, 0.21875),
        "b_up": normal_values(splits[14], (FF,), 0.5, 2.5),
        "w_down": normal_values(splits[15], (FF, D), FF ** -0.5, 0.109375),
        "b_down": normal_values(splits[16], (D,), 0.3, 1.5),
    }


EPSILON = 1e-06
NEG_FILL = -1e+30
PRECISE = lax.Precision.HIGHEST

@jax.custom_vjp
def low(v):
    return lax.optimization_barrier(v.astype(jnp.bfloat16)).astype(jnp.float32)

@jax.custom_vjp
def low_back(v):
    return v

def low_keep(v):
    return (low(v), None)

def low_pass(kept, grad):
    return (grad,)

def back_keep(v):
    return (v, None)

def back_low(kept, grad):
    return (low(grad),)
low.defvjp(low_keep, low_pass)
low_back.defvjp(back_keep, back_low)

def norm_rows(values):
    center = values - lax.optimization_barrier(jnp.mean(values, axis=-1, keepdims=True))
    return center * lax.rsqrt(lax.optimization_barrier(jnp.mean(center * center, axis=-1, keepdims=True)) + EPSILON)

def exact_dot(left, right):
    return jnp.dot(left, right, precision=PRECISE)

def attend(queries, keyset, valueset, allowed):
    query_heads = queries.reshape(queries.shape[0], HEADS, HEAD)
    key_heads = keyset.reshape(keyset.shape[0], HEADS, HEAD)
    value_heads = valueset.reshape(valueset.shape[0], HEADS, HEAD)
    scores = jnp.einsum('qhd,khd->hqk', query_heads, key_heads, precision=PRECISE) * HEAD ** (-0.5)
    scores = low_back(scores)
    scores = jnp.where(allowed[None], scores, NEG_FILL)
    prob_rows = low(jax.nn.softmax(scores, axis=-1))
    mixed_out = jnp.einsum('hqk,khd->qhd', prob_rows, value_heads, precision=PRECISE)
    return mixed_out.reshape(queries.shape[0], HEADS * HEAD)

def block_row(frames_f, text_f, step_f, item_of, slot_ids, params):
    w_ada, b_ada, w_qkv, w_out, g_cross, w_cq, w_ckv, w_co, w_up, b_up, w_down, b_down = params
    ada_in = low(jax.nn.silu(step_f))
    item_mod = exact_dot(ada_in, w_ada) + b_ada
    frame_mod = item_mod[item_of]
    shift_a, scale_a, gate_a, shift_b, scale_b, gate_b = jnp.split(frame_mod, 6, axis=-1)
    h_one = low(norm_rows(frames_f) * (1.0 + scale_a) + shift_a)
    proj_all = low(low_back(exact_dot(h_one, w_qkv)))
    query_a, key_a, value_a = jnp.split(proj_all, 3, axis=-1)
    allowed_self = item_of[:, None] == item_of[None, :]
    attn_low = low(low_back(attend(query_a, key_a, value_a, allowed_self)))
    branch_a = low_back(exact_dot(attn_low, w_out))
    x_one = frames_f + gate_a * branch_a
    h_two = low(norm_rows(x_one) * g_cross)
    query_c = low(low_back(exact_dot(h_two, w_cq)))
    text_kv = low(low_back(exact_dot(text_f, w_ckv)))
    key_c, value_c = jnp.split(text_kv, 2, axis=-1)
    allowed_cross = item_of[:, None] == slot_ids[None, :]
    cross_low = low(low_back(attend(query_c, key_c, value_c, allowed_cross)))
    branch_c = low_back(exact_dot(cross_low, w_co))
    x_two = x_one + branch_c
    h_three = low(norm_rows(x_two) * (1.0 + scale_b) + shift_b)
    pre_act = low_back(exact_dot(h_three, w_up) + b_up)
    act_low = low(jax.nn.gelu(pre_act, approximate=True))
    branch_m = low_back(exact_dot(act_low, w_down) + b_down)
    return x_two + gate_b * branch_m

def reference(frames, text_tokens, step_embed, segments, cotangent, w_ada, b_ada, w_qkv, w_out, g_cross, w_cq, w_ckv, w_co, w_up, b_up, w_down, b_down):
    weights = tuple((member.astype(jnp.float32) for member in (w_ada, b_ada, w_qkv, w_out, g_cross, w_cq, w_ckv, w_co, w_up, b_up, w_down, b_down)))
    slot_ids = (jnp.arange(ITEMS * TXT) // TXT).astype(jnp.int32)

    def one_row(totals, row_in):
        row_frames, row_text, row_step, row_items, row_cot = row_in

        def forward(frames_f, text_f, step_f, *params):
            return block_row(frames_f, text_f, step_f, row_items, slot_ids, params)
        result, pullback = jax.vjp(forward, row_frames, row_text, row_step, *weights)
        gradients = pullback(row_cot)
        new_totals = tuple((running + addend for running, addend in zip(totals, gradients[3:])))
        return (new_totals, (result.astype(jnp.bfloat16), gradients[0], gradients[1], gradients[2]))
    start_totals = tuple((jnp.zeros(member.shape, jnp.float32) for member in weights))
    row_inputs = (frames.astype(jnp.float32), text_tokens.astype(jnp.float32), step_embed.astype(jnp.float32), segments.astype(jnp.int32), cotangent.astype(jnp.float32))
    totals, stacked = lax.scan(one_row, start_totals, row_inputs)
    output, d_frames, d_text, d_step = stacked
    return (output, d_frames, d_text, d_step, totals[0], totals[1], totals[2], totals[3], totals[4], totals[5], totals[6], totals[7], totals[8], totals[9], totals[10], totals[11])
```

```python
import functools

import jax
import jax.numpy as jnp
from jax import lax
from jax.experimental import pallas as pl
from jax.experimental.pallas import tpu as pltpu
from jax.sharding import PartitionSpec as P

HEADS = 12
HEAD = 64
TXT = 77
ITEMS = 4

EPSILON = 1e-06
NEG_FILL = -1e30
PRECISE = lax.Precision.HIGHEST
F32 = jnp.float32
BF16 = jnp.bfloat16
MESH = pl.DeviceIdType.MESH
CHUNKS = 8
VMEM_MOST = 66_000_000


def dot(left, right):
    return jnp.dot(left, right, preferred_element_type=F32)


def dot_t(left, right):
    return lax.dot_general(left, right, (((1,), (1,)), ((), ())), preferred_element_type=F32)


def t_dot(left, right):
    return lax.dot_general(left, right, (((0,), (0,)), ((), ())), preferred_element_type=F32)


def norm_parts(values):
    center = values - jnp.mean(values, axis=-1, keepdims=True)
    inverse = lax.rsqrt(jnp.mean(center * center, axis=-1, keepdims=True) + EPSILON)
    return center * inverse, inverse


def norm_back(normed, inverse, upstream):
    return inverse * (
        upstream
        - jnp.mean(upstream, axis=-1, keepdims=True)
        - normed * jnp.mean(upstream * normed, axis=-1, keepdims=True)
    )


def gelu_tanh(values):
    return jax.nn.gelu(values, approximate=True)


def split_heads(matrix):
    return matrix.reshape(matrix.shape[0], HEADS, HEAD)


def scores_of(queries, keyset, allowed):
    raw = jnp.einsum(
        "qhd,khd->hqk", split_heads(queries), split_heads(keyset), preferred_element_type=F32
    )
    raw = raw * HEAD ** (-0.5)
    return raw if allowed is None else jnp.where(allowed[None, None, :], raw, NEG_FILL)


def attend_forward(queries, keyset, valueset, allowed):
    scores = scores_of(queries, keyset, allowed)
    top_score = jnp.max(scores, axis=-1, keepdims=True)
    exp_scores = jnp.exp(scores - top_score)
    totals = jnp.sum(exp_scores, axis=-1, keepdims=True)
    probs_low = (exp_scores / totals).astype(BF16)
    mixed = jnp.einsum(
        "hqk,khd->qhd", probs_low, split_heads(valueset), preferred_element_type=F32
    )
    return mixed.reshape(queries.shape).astype(BF16), top_score + jnp.log(totals)


def attend_backward(queries, keyset, valueset, allowed, log_total, upstream):
    probs = jnp.exp(scores_of(queries, keyset, allowed) - log_total)
    up_heads = split_heads(upstream)
    grad_probs = jnp.einsum(
        "qhd,khd->hqk", up_heads, split_heads(valueset), preferred_element_type=F32
    )
    inner = jnp.sum(probs * grad_probs, axis=-1, keepdims=True)
    grad_scores = (probs * (grad_probs - inner)).astype(BF16)
    grad_query = jnp.einsum(
        "hqk,khd->qhd", grad_scores, split_heads(keyset), preferred_element_type=F32
    )
    grad_key = jnp.einsum(
        "hqk,qhd->khd", grad_scores, split_heads(queries), preferred_element_type=F32
    )
    grad_value = jnp.einsum(
        "hqk,qhd->khd", probs.astype(BF16), up_heads, preferred_element_type=F32
    )
    return (
        (grad_query.reshape(queries.shape) * HEAD ** (-0.5)).astype(BF16),
        (grad_key.reshape(keyset.shape) * HEAD ** (-0.5)).astype(BF16),
        grad_value.reshape(valueset.shape).astype(BF16),
    )


def reduce_kernel(
    act, gm_t, h3, gpre, lc, gc, text, gkv, lq, gq0, gq1,
    out,
    G, R0, R1, R2, R3,
    s0, r0, s1, r1, s2, r2, s3, r3,
):
    seq = lax.axis_index("seq")
    rows = lax.axis_index("rows")
    y, x = seq // 2, seq % 2
    z, c = rows // 2, rows % 2
    core_peer = {"rows": z * 2 + (1 - c)}
    x_peer = {"seq": y * 2 + (1 - x)}
    y_peer = {"seq": (1 - y) * 2 + x}
    z_peers = [{"rows": lax.rem(z + d, 4) * 2 + c} for d in (1, 2, 3)]

    barrier = pltpu.get_barrier_semaphore()
    for peer in [core_peer, x_peer, y_peer] + z_peers:
        pl.semaphore_signal(barrier, inc=1, device_id=peer, device_id_type=MESH)
    pl.semaphore_wait(barrier, 6)

    width = G.shape[-1]
    tall = G.shape[-2]

    def put(k, s, block):
        low = block.astype(BF16)
        for zz in range(4):
            for cc in range(2):
                at = (zz * 2 + cc) * tall
                G[k, cc, zz, s // 2, s % 2] = low[at : at + tall]

    def compute(k):
        @pl.loop(0, 4)
        def _(s):
            if k < 2:
                left = gm_t[pl.ds(pl.multiple_of(s * 2 * tall + k * tall, 16), tall), :]
                for r in range(8):
                    G[k, r % 2, r // 2, s // 2, s % 2] = dot(
                        left, act[:, r * width : (r + 1) * width]
                    ).astype(BF16)
            elif k < 4:
                at = pl.multiple_of(s * 2 * width + (k - 2) * width, 128)
                put(k, s, t_dot(h3[...], gpre[:, pl.ds(at, width)]))
            elif k == 4:
                put(k, s, t_dot(lc[...], gc[s]))
            elif k == 5:
                at = pl.multiple_of(s * width, 128)
                put(k, s, t_dot(text[...], gkv[:, pl.ds(at, width)]))
            elif k == 6:
                put(k, s, t_dot(lq[: gq0.shape[1], :], gq0[s]))
            else:
                put(k, s, t_dot(lq[...], gq1[s]))

    def remote(src, dst, send, recv, peer):
        return pltpu.make_async_remote_copy(
            src_ref=src, dst_ref=dst, send_sem=send, recv_sem=recv,
            device_id=peer, device_id_type=MESH,
        )

    def core_copy(k):
        return remote(G.at[k, 1 - c], R0.at[k], s0.at[k], r0.at[k], core_peer)

    def first_copies(k):
        return (
            remote(G.at[k, c, 0:2, :, 1 - x], R1.at[k, 0], s1.at[k, 0], r1.at[k, 0], x_peer),
            remote(G.at[k, c, 2:4, 1 - y], R1.at[k, 1], s1.at[k, 1], r1.at[k, 1], y_peer),
        )

    def second_copies(k):
        return (
            remote(G.at[k, c, 0:2, 1 - y, x], R2.at[k, 0], s2.at[k, 0], r2.at[k, 0], y_peer),
            remote(G.at[k, c, 2:4, y, 1 - x], R2.at[k, 1], s2.at[k, 1], r2.at[k, 1], x_peer),
        )

    def z_copies(k):
        return [
            remote(
                G.at[k, c, lax.rem(z + d, 4), y, x], R3.at[k, d - 1],
                s3.at[k, d - 1], r3.at[k, d - 1], z_peers[d - 1],
            )
            for d in (1, 2, 3)
        ]

    def add(one, two):
        return (one.astype(F32) + two.astype(F32)).astype(BF16)

    def phase0(k):
        compute(k)
        core_copy(k).start()

    def phase1(k):
        core_copy(k).wait_recv()

        @pl.loop(0, 4)
        def _(zz):
            for yy in range(2):
                for xx in range(2):
                    G[k, c, zz, yy, xx] = add(G[k, c, zz, yy, xx], R0[k, zz, yy, xx])

        for copy in first_copies(k):
            copy.start()

    def phase2(k):
        for copy in first_copies(k):
            copy.wait_recv()
        for zz in range(2):
            for other in range(2):
                G[k, c, zz, other, x] = add(G[k, c, zz, other, x], R1[k, 0, zz, other])
                G[k, c, 2 + zz, y, other] = add(G[k, c, 2 + zz, y, other], R1[k, 1, zz, other])
        for copy in second_copies(k):
            copy.start()

    def phase3(k):
        for copy in second_copies(k):
            copy.wait_recv()
        for zz in range(2):
            G[k, c, zz, y, x] = add(G[k, c, zz, y, x], R2[k, 0, zz])
            G[k, c, 2 + zz, y, x] = add(G[k, c, 2 + zz, y, x], R2[k, 1, zz])
        for copy in z_copies(k):
            copy.start()

    def phase4(k):
        for copy in z_copies(k):
            copy.wait_recv()
        total = G[k, c, z, y, x].astype(F32)
        for d in range(3):
            total = total + R3[k, d].astype(F32)
        out[k] = total

    phases = (phase0, phase1, phase2, phase3, phase4)
    for wave in range(CHUNKS + 4):
        for depth in (4, 3, 2, 1, 0):
            if 0 <= wave - depth < CHUNKS:
                phases[depth](wave - depth)
    for k in range(CHUNKS):
        core_copy(k).wait_send()
        for copy in (*first_copies(k), *second_copies(k), *z_copies(k)):
            copy.wait_send()


def reduce_weights(ops, model):
    tall, width = model // 8, model // 2
    block = (CHUNKS, 2, 4, 2, 2, tall, width)
    dma = pltpu.SemaphoreType.DMA
    return pl.pallas_call(
        reduce_kernel,
        out_shape=jax.ShapeDtypeStruct((CHUNKS, tall, width), F32),
        in_specs=[pl.BlockSpec(memory_space=pltpu.VMEM)] * len(ops),
        out_specs=pl.BlockSpec(memory_space=pltpu.VMEM),
        scratch_shapes=[
            pltpu.VMEM(block, BF16),
            pltpu.VMEM((CHUNKS, 4, 2, 2, tall, width), BF16),
            pltpu.VMEM((CHUNKS, 2, 2, 2, tall, width), BF16),
            pltpu.VMEM((CHUNKS, 2, 2, tall, width), BF16),
            pltpu.VMEM((CHUNKS, 3, tall, width), BF16),
            dma((CHUNKS,)), dma((CHUNKS,)),
            dma((CHUNKS, 2)), dma((CHUNKS, 2)),
            dma((CHUNKS, 2)), dma((CHUNKS, 2)),
            dma((CHUNKS, 3)), dma((CHUNKS, 3)),
        ],
        compiler_params=pltpu.CompilerParams(
            collective_id=0, has_side_effects=True, vmem_limit_bytes=VMEM_MOST
        ),
        name="reduce_weights",
    )(*ops)


def scatter_plain(matrix):
    part = lax.psum_scatter(matrix.astype(BF16), "rows", scatter_dimension=0, tiled=True)
    part = lax.psum_scatter(part, "seq", scatter_dimension=1, tiled=True)
    return part.astype(F32)


def per_device(
    frames, text_tokens, step_embed, segments, cotangent,
    w_ada, b_ada, w_qkv, w_out, g_cross, w_cq, w_ckv, w_co, w_up, b_up, w_down, b_down,
):
    seq_count = lax.axis_size("seq")
    rows_count = lax.axis_size("rows")
    seq_index = lax.axis_index("seq")
    rows_index = lax.axis_index("rows")
    frames, text_tokens, step_embed = frames[0], text_tokens[0], step_embed[0]
    segments, cotangent = segments[0], cotangent[0]
    here, model = frames.shape
    length = segments.shape[0]
    assert (length // ITEMS) % here == 0
    block_slots = segments[::here]
    slot = lax.dynamic_index_in_dim(block_slots, seq_index, 0, keepdims=False)
    allowed = segments == slot
    text_mine = lax.dynamic_slice_in_dim(text_tokens, slot * TXT, TXT, axis=0)

    frames_all = lax.all_gather(frames, "seq", axis=0, tiled=True)
    ada_in = jax.nn.silu(step_embed.astype(F32)).astype(BF16)
    item_mod = dot(ada_in, w_ada) + b_ada.astype(F32)
    mine = lax.dynamic_slice_in_dim(item_mod, slot, 1, axis=0)
    shift_a, scale_a, gate_a, shift_b, scale_b, gate_b = jnp.split(mine, 6, axis=-1)

    normed_all, inverse_all = norm_parts(frames_all.astype(F32))
    hot = (block_slots[:, None] == jnp.arange(ITEMS)[None, :]).astype(F32)
    block_mod = jnp.dot(hot, item_mod[:, : 2 * model], precision=PRECISE)
    frame_mod = jnp.repeat(block_mod, here, axis=0)
    h_all = (normed_all * (1.0 + frame_mod[:, model:]) + frame_mod[:, :model]).astype(BF16)
    frames_f32 = frames.astype(F32)
    normed_0, inverse_0 = norm_parts(frames_f32)
    h_one = (normed_0 * (1.0 + scale_a) + shift_a).astype(BF16)
    query_a = dot(h_one, w_qkv[:, :model]).astype(BF16)
    kv_all = dot(h_all, w_qkv[:, model:]).astype(BF16)
    key_all, value_all = kv_all[:, :model], kv_all[:, model:]
    attn_low, lse_self = attend_forward(query_a, key_all, value_all, allowed)
    branch_a = dot(attn_low, w_out)
    x_one = frames_f32 + gate_a * branch_a
    gain = g_cross.astype(F32)[None]
    normed_1, inverse_1 = norm_parts(x_one)
    h_two = (normed_1 * gain).astype(BF16)
    query_c = dot(h_two, w_cq).astype(BF16)
    text_kv = dot(text_mine, w_ckv).astype(BF16)
    key_c, value_c = text_kv[:, :model], text_kv[:, model:]
    cross_low, lse_cross = attend_forward(query_c, key_c, value_c, None)
    x_two = x_one + dot(cross_low, w_co)
    normed_2, inverse_2 = norm_parts(x_two)
    h_three = (normed_2 * (1.0 + scale_b) + shift_b).astype(BF16)
    pre_act = dot(h_three, w_up) + b_up.astype(F32)
    act_low = gelu_tanh(pre_act).astype(BF16)
    branch_m = dot(act_low, w_down) + b_down.astype(F32)
    output = (x_two + gate_b * branch_m).astype(BF16)

    grad_out = cotangent.astype(F32)
    grad_m = (gate_b * grad_out).astype(BF16)
    grad_act = dot_t(grad_m, w_down)
    unused_act, gelu_back = jax.vjp(gelu_tanh, pre_act)
    grad_pre = gelu_back(grad_act)[0].astype(BF16)
    up_three = dot_t(grad_pre, w_up)
    grad_x2 = grad_out + norm_back(normed_2, inverse_2, up_three * (1.0 + scale_b))
    grad_c = grad_x2.astype(BF16)
    grad_cross = dot_t(grad_c, w_co).astype(BF16)
    grad_qc, grad_kc, grad_vc = attend_backward(
        query_c, key_c, value_c, None, lse_cross, grad_cross
    )
    grad_kvc = jnp.concatenate([grad_kc, grad_vc], axis=-1)
    up_two = dot_t(grad_qc, w_cq)
    grad_x1 = grad_x2 + norm_back(normed_1, inverse_1, up_two * gain)
    grad_a = (gate_a * grad_x1).astype(BF16)
    grad_attn = dot_t(grad_a, w_out).astype(BF16)
    grad_qa, grad_ka, grad_va = attend_backward(
        query_a, key_all, value_all, allowed, lse_self, grad_attn
    )
    grad_kva = jnp.concatenate([grad_ka, grad_va], axis=-1)
    up_kv = dot_t(grad_kva, w_qkv[:, model:]).astype(BF16)
    up_one = dot_t(grad_qa, w_qkv[:, :model]) + lax.psum_scatter(
        up_kv, "seq", scatter_dimension=0, tiled=True
    ).astype(F32)
    d_frames = grad_x1 + norm_back(normed_0, inverse_0, up_one * (1.0 + scale_a))

    small = jnp.concatenate(
        [
            jnp.sum(up_one, axis=0),
            jnp.sum(up_one * normed_0, axis=0),
            jnp.sum(grad_x1 * branch_a, axis=0),
            jnp.sum(up_three, axis=0),
            jnp.sum(up_three * normed_2, axis=0),
            jnp.sum(grad_out * branch_m, axis=0),
            jnp.sum(up_two * normed_1, axis=0),
            jnp.sum(grad_pre.astype(F32), axis=0),
            jnp.sum(grad_m.astype(F32), axis=0),
            lax.dynamic_index_in_dim(ada_in, slot, 0, keepdims=False).astype(F32),
        ]
    )
    small_all = lax.all_gather(small, ("rows", "seq"), axis=0, tiled=False)
    small_all = small_all.reshape(rows_count * seq_count, -1)
    item_all = small_all[:, : 6 * model]
    bias_all = small_all[:, 6 * model : -model]
    ada_all = small_all[:, -model:]

    def share(table, count, index):
        size = table.shape[-1] // count
        return lax.dynamic_slice_in_dim(table, index * size, size, axis=-1)

    def bias_sum(table):
        return jnp.sum(share(table, rows_count, rows_index), axis=0)

    d_b_ada = bias_sum(item_all)
    d_g_cross = bias_sum(bias_all[:, :model])
    d_b_up = bias_sum(bias_all[:, model:-model])
    d_b_down = bias_sum(bias_all[:, -model:])
    d_w_ada = lax.dot_general(
        share(ada_all, rows_count, rows_index),
        share(item_all, seq_count, seq_index),
        (((0,), (0,)), ((), ())),
        precision=PRECISE,
        preferred_element_type=F32,
    )
    item_share = ITEMS // seq_count
    row_items = lax.dynamic_slice_in_dim(item_all, rows_index * seq_count, seq_count, axis=0)
    owned = seq_index * item_share + jnp.arange(item_share)
    pick = (owned[:, None] == block_slots[None, :]).astype(F32)
    item_mine = jnp.dot(pick, row_items, precision=PRECISE)
    d_ada = lax.dot_general(
        item_mine, w_ada.astype(F32), (((1,), (1,)), ((), ())), precision=PRECISE
    )
    my_step = lax.dynamic_slice_in_dim(
        step_embed, seq_index * item_share, item_share, axis=0
    ).astype(F32)
    unused_step, silu_back = jax.vjp(jax.nn.silu, my_step)
    d_step = silu_back(d_ada)[0]
    text_part = dot_t(grad_kvc, w_ckv).astype(BF16)
    text_full = lax.dynamic_update_slice_in_dim(
        jnp.zeros(text_tokens.shape, BF16), text_part, slot * TXT, axis=0
    )
    d_text = lax.psum_scatter(text_full, "seq", scatter_dimension=0, tiled=True).astype(F32)

    if rows_count == 8 and seq_count == 4:
        half = model // 2

        def by_seq(table):
            return table.reshape(table.shape[0], 4, -1).transpose(1, 0, 2)

        pad_text = (-TXT) % 16
        zero_c = jnp.zeros((4, here, model // 4), BF16)
        gc = jnp.concatenate(
            [
                jnp.concatenate([by_seq(grad_qc), zero_c], axis=2),
                jnp.concatenate([zero_c, by_seq(grad_c)], axis=2),
            ],
            axis=1,
        )
        query_full = lax.dynamic_update_slice_in_dim(
            jnp.zeros((length, model), BF16), grad_qa, seq_index * here, axis=0
        )
        gqkv = by_seq(jnp.concatenate([query_full, grad_kva], axis=1))
        rest = gqkv[:, :, half:]
        gq1 = jnp.concatenate(
            [
                jnp.pad(rest, ((0, 0), (0, 0), (0, half - rest.shape[2]))),
                jnp.pad(by_seq(grad_a), ((0, 0), (0, 0), (rest.shape[2], 0))),
            ],
            axis=1,
        )
        ops = (
            act_low, grad_m.T, h_three, grad_pre,
            jnp.concatenate([h_two, cross_low], axis=0), gc,
            jnp.pad(text_mine, ((0, pad_text), (0, 0))),
            jnp.pad(grad_kvc, ((0, pad_text), (0, 0))),
            jnp.concatenate([h_all, attn_low], axis=0), gqkv[:, :, :half], gq1,
        )
        done = reduce_weights(ops, model)
        d_w_down = jnp.concatenate([done[0], done[1]], axis=0).T
        d_w_up = jnp.concatenate([done[2], done[3]], axis=1)
        d_w_cq, d_w_co = done[4][:, : model // 4], done[4][:, model // 4 :]
        d_w_ckv = done[5]
        last = done[7]
        d_w_qkv = jnp.concatenate([done[6], last[:, : rest.shape[2]]], axis=1)
        d_w_out = last[:, rest.shape[2] :]
    else:
        d_w_down = scatter_plain(t_dot(act_low, grad_m))
        d_w_up = scatter_plain(t_dot(h_three, grad_pre))
        d_w_cq = scatter_plain(t_dot(h_two, grad_qc))
        d_w_co = scatter_plain(t_dot(cross_low, grad_c))
        d_w_ckv = scatter_plain(t_dot(text_mine, grad_kvc))
        d_w_out = scatter_plain(t_dot(attn_low, grad_a))
        d_w_qkv = scatter_plain(
            jnp.concatenate([t_dot(h_one, grad_qa), t_dot(h_all, grad_kva)], axis=1)
        )
    return (
        output[None], d_frames[None], d_text[None], d_step[None],
        d_w_ada, d_b_ada, d_w_qkv, d_w_out, d_g_cross, d_w_cq, d_w_ckv, d_w_co,
        d_w_up, d_b_up, d_w_down, d_b_down,
    )


def solution(mesh):
    row_seq = P("rows", "seq", None)
    in_specs = (
        row_seq, P("rows", None, None), P("rows", None, None), P("rows", None), row_seq,
    ) + (P(),) * 12
    out_specs = (row_seq,) * 4 + (
        P("rows", "seq"), P("rows"), P("rows", "seq"), P("rows", "seq"), P("rows"),
        P("rows", "seq"), P("rows", "seq"), P("rows", "seq"), P("rows", "seq"), P("rows"),
        P("rows", "seq"), P("rows"),
    )
    return jax.shard_map(
        per_device, mesh=mesh, in_specs=in_specs, out_specs=out_specs, check_vma=False
    )
```

```python
import functools

import jax
import jax.numpy as jnp
from jax import lax
from jax.experimental import pallas as pl
from jax.experimental.pallas import tpu as pltpu
from jax.sharding import PartitionSpec as P

HEADS = 12
HEAD = 64
TXT = 77
ITEMS = 4

EPSILON = 1e-06
NEG_FILL = -1e30
PRECISE = lax.Precision.HIGHEST
F32 = jnp.float32
BF16 = jnp.bfloat16
MESH = pl.DeviceIdType.MESH
CHUNKS = 8
VMEM_MOST = 67_043_328


def dot(left, right):
    return jnp.dot(left, right, preferred_element_type=F32)


def dot_t(left, right):
    return lax.dot_general(left, right, (((1,), (1,)), ((), ())), preferred_element_type=F32)


def t_dot(left, right):
    return lax.dot_general(left, right, (((0,), (0,)), ((), ())), preferred_element_type=F32)


def norm_parts(values):
    center = values - jnp.mean(values, axis=-1, keepdims=True)
    inverse = lax.rsqrt(jnp.mean(center * center, axis=-1, keepdims=True) + EPSILON)
    return center * inverse, inverse


def norm_back(normed, inverse, upstream):
    return inverse * (
        upstream
        - jnp.mean(upstream, axis=-1, keepdims=True)
        - normed * jnp.mean(upstream * normed, axis=-1, keepdims=True)
    )


def gelu_tanh(values):
    return jax.nn.gelu(values, approximate=True)


def split_heads(matrix):
    return matrix.reshape(matrix.shape[0], HEADS, HEAD)


def scores_of(queries, keyset, allowed):
    raw = jnp.einsum(
        "qhd,khd->hqk", split_heads(queries), split_heads(keyset), preferred_element_type=F32
    )
    raw = raw * HEAD ** (-0.5)
    return raw if allowed is None else jnp.where(allowed[None, None, :], raw, NEG_FILL)


def attend_forward(queries, keyset, valueset, allowed):
    scores = scores_of(queries, keyset, allowed)
    top_score = jnp.max(scores, axis=-1, keepdims=True)
    exp_scores = jnp.exp(scores - top_score)
    totals = jnp.sum(exp_scores, axis=-1, keepdims=True)
    probs_low = (exp_scores / totals).astype(BF16)
    mixed = jnp.einsum(
        "hqk,khd->qhd", probs_low, split_heads(valueset), preferred_element_type=F32
    )
    return mixed.reshape(queries.shape).astype(BF16), top_score + jnp.log(totals)


def attend_backward(queries, keyset, valueset, allowed, log_total, upstream):
    probs = jnp.exp(scores_of(queries, keyset, allowed) - log_total)
    up_heads = split_heads(upstream)
    grad_probs = jnp.einsum(
        "qhd,khd->hqk", up_heads, split_heads(valueset), preferred_element_type=F32
    )
    inner = jnp.sum(probs * grad_probs, axis=-1, keepdims=True)
    grad_scores = (probs * (grad_probs - inner)).astype(BF16)
    grad_query = jnp.einsum(
        "hqk,khd->qhd", grad_scores, split_heads(keyset), preferred_element_type=F32
    )
    grad_key = jnp.einsum(
        "hqk,qhd->khd", grad_scores, split_heads(queries), preferred_element_type=F32
    )
    grad_value = jnp.einsum(
        "hqk,qhd->khd", probs.astype(BF16), up_heads, preferred_element_type=F32
    )
    return (
        (grad_query.reshape(queries.shape) * HEAD ** (-0.5)).astype(BF16),
        (grad_key.reshape(keyset.shape) * HEAD ** (-0.5)).astype(BF16),
        grad_value.reshape(valueset.shape).astype(BF16),
    )


def scatter_plain(matrix):
    part = lax.psum_scatter(matrix.astype(BF16), "rows", scatter_dimension=0, tiled=True)
    part = lax.psum_scatter(part, "seq", scatter_dimension=1, tiled=True)
    return part.astype(F32)


def per_device_plain(
    frames, text_tokens, step_embed, segments, cotangent,
    w_ada, b_ada, w_qkv, w_out, g_cross, w_cq, w_ckv, w_co, w_up, b_up, w_down, b_down,
):
    seq_count = lax.axis_size("seq")
    rows_count = lax.axis_size("rows")
    seq_index = lax.axis_index("seq")
    rows_index = lax.axis_index("rows")
    frames, text_tokens, step_embed = frames[0], text_tokens[0], step_embed[0]
    segments, cotangent = segments[0], cotangent[0]
    here, model = frames.shape
    length = segments.shape[0]
    assert (length // ITEMS) % here == 0
    block_slots = segments[::here]
    slot = lax.dynamic_index_in_dim(block_slots, seq_index, 0, keepdims=False)
    allowed = segments == slot
    text_mine = lax.dynamic_slice_in_dim(text_tokens, slot * TXT, TXT, axis=0)

    frames_all = lax.all_gather(frames, "seq", axis=0, tiled=True)
    ada_in = jax.nn.silu(step_embed.astype(F32)).astype(BF16)
    item_mod = dot(ada_in, w_ada) + b_ada.astype(F32)
    mine = lax.dynamic_slice_in_dim(item_mod, slot, 1, axis=0)
    shift_a, scale_a, gate_a, shift_b, scale_b, gate_b = jnp.split(mine, 6, axis=-1)

    normed_all, inverse_all = norm_parts(frames_all.astype(F32))
    hot = (block_slots[:, None] == jnp.arange(ITEMS)[None, :]).astype(F32)
    block_mod = jnp.dot(hot, item_mod[:, : 2 * model], precision=PRECISE)
    frame_mod = jnp.repeat(block_mod, here, axis=0)
    h_all = (normed_all * (1.0 + frame_mod[:, model:]) + frame_mod[:, :model]).astype(BF16)
    frames_f32 = frames.astype(F32)
    normed_0, inverse_0 = norm_parts(frames_f32)
    h_one = (normed_0 * (1.0 + scale_a) + shift_a).astype(BF16)
    query_a = dot(h_one, w_qkv[:, :model]).astype(BF16)
    kv_all = dot(h_all, w_qkv[:, model:]).astype(BF16)
    key_all, value_all = kv_all[:, :model], kv_all[:, model:]
    attn_low, lse_self = attend_forward(query_a, key_all, value_all, allowed)
    branch_a = dot(attn_low, w_out)
    x_one = frames_f32 + gate_a * branch_a
    gain = g_cross.astype(F32)[None]
    normed_1, inverse_1 = norm_parts(x_one)
    h_two = (normed_1 * gain).astype(BF16)
    query_c = dot(h_two, w_cq).astype(BF16)
    text_kv = dot(text_mine, w_ckv).astype(BF16)
    key_c, value_c = text_kv[:, :model], text_kv[:, model:]
    cross_low, lse_cross = attend_forward(query_c, key_c, value_c, None)
    x_two = x_one + dot(cross_low, w_co)
    normed_2, inverse_2 = norm_parts(x_two)
    h_three = (normed_2 * (1.0 + scale_b) + shift_b).astype(BF16)
    pre_act = dot(h_three, w_up) + b_up.astype(F32)
    act_low = gelu_tanh(pre_act).astype(BF16)
    branch_m = dot(act_low, w_down) + b_down.astype(F32)
    output = (x_two + gate_b * branch_m).astype(BF16)

    grad_out = cotangent.astype(F32)
    grad_m = (gate_b * grad_out).astype(BF16)
    grad_act = dot_t(grad_m, w_down)
    unused_act, gelu_back = jax.vjp(gelu_tanh, pre_act)
    grad_pre = gelu_back(grad_act)[0].astype(BF16)
    up_three = dot_t(grad_pre, w_up)
    grad_x2 = grad_out + norm_back(normed_2, inverse_2, up_three * (1.0 + scale_b))
    grad_c = grad_x2.astype(BF16)
    grad_cross = dot_t(grad_c, w_co).astype(BF16)
    grad_qc, grad_kc, grad_vc = attend_backward(
        query_c, key_c, value_c, None, lse_cross, grad_cross
    )
    grad_kvc = jnp.concatenate([grad_kc, grad_vc], axis=-1)
    up_two = dot_t(grad_qc, w_cq)
    grad_x1 = grad_x2 + norm_back(normed_1, inverse_1, up_two * gain)
    grad_a = (gate_a * grad_x1).astype(BF16)
    grad_attn = dot_t(grad_a, w_out).astype(BF16)
    grad_qa, grad_ka, grad_va = attend_backward(
        query_a, key_all, value_all, allowed, lse_self, grad_attn
    )
    grad_kva = jnp.concatenate([grad_ka, grad_va], axis=-1)
    up_kv = dot_t(grad_kva, w_qkv[:, model:]).astype(BF16)
    up_one = dot_t(grad_qa, w_qkv[:, :model]) + lax.psum_scatter(
        up_kv, "seq", scatter_dimension=0, tiled=True
    ).astype(F32)
    d_frames = grad_x1 + norm_back(normed_0, inverse_0, up_one * (1.0 + scale_a))

    small = jnp.concatenate(
        [
            jnp.sum(up_one, axis=0),
            jnp.sum(up_one * normed_0, axis=0),
            jnp.sum(grad_x1 * branch_a, axis=0),
            jnp.sum(up_three, axis=0),
            jnp.sum(up_three * normed_2, axis=0),
            jnp.sum(grad_out * branch_m, axis=0),
            jnp.sum(up_two * normed_1, axis=0),
            jnp.sum(grad_pre.astype(F32), axis=0),
            jnp.sum(grad_m.astype(F32), axis=0),
            lax.dynamic_index_in_dim(ada_in, slot, 0, keepdims=False).astype(F32),
        ]
    )
    small_all = lax.all_gather(small, ("rows", "seq"), axis=0, tiled=False)
    small_all = small_all.reshape(rows_count * seq_count, -1)
    item_all = small_all[:, : 6 * model]
    bias_all = small_all[:, 6 * model : -model]
    ada_all = small_all[:, -model:]

    def share(table, count, index):
        size = table.shape[-1] // count
        return lax.dynamic_slice_in_dim(table, index * size, size, axis=-1)

    def bias_sum(table):
        return jnp.sum(share(table, rows_count, rows_index), axis=0)

    d_b_ada = bias_sum(item_all)
    d_g_cross = bias_sum(bias_all[:, :model])
    d_b_up = bias_sum(bias_all[:, model:-model])
    d_b_down = bias_sum(bias_all[:, -model:])
    d_w_ada = lax.dot_general(
        share(ada_all, rows_count, rows_index),
        share(item_all, seq_count, seq_index),
        (((0,), (0,)), ((), ())),
        precision=PRECISE,
        preferred_element_type=F32,
    )
    item_share = ITEMS // seq_count
    row_items = lax.dynamic_slice_in_dim(item_all, rows_index * seq_count, seq_count, axis=0)
    owned = seq_index * item_share + jnp.arange(item_share)
    pick = (owned[:, None] == block_slots[None, :]).astype(F32)
    item_mine = jnp.dot(pick, row_items, precision=PRECISE)
    d_ada = lax.dot_general(
        item_mine, w_ada.astype(F32), (((1,), (1,)), ((), ())), precision=PRECISE
    )
    my_step = lax.dynamic_slice_in_dim(
        step_embed, seq_index * item_share, item_share, axis=0
    ).astype(F32)
    unused_step, silu_back = jax.vjp(jax.nn.silu, my_step)
    d_step = silu_back(d_ada)[0]
    text_part = dot_t(grad_kvc, w_ckv).astype(BF16)
    text_full = lax.dynamic_update_slice_in_dim(
        jnp.zeros(text_tokens.shape, BF16), text_part, slot * TXT, axis=0
    )
    d_text = lax.psum_scatter(text_full, "seq", scatter_dimension=0, tiled=True).astype(F32)

    d_w_down = scatter_plain(t_dot(act_low, grad_m))
    d_w_up = scatter_plain(t_dot(h_three, grad_pre))
    d_w_cq = scatter_plain(t_dot(h_two, grad_qc))
    d_w_co = scatter_plain(t_dot(cross_low, grad_c))
    d_w_ckv = scatter_plain(t_dot(text_mine, grad_kvc))
    d_w_out = scatter_plain(t_dot(attn_low, grad_a))
    d_w_qkv = scatter_plain(
        jnp.concatenate([t_dot(h_one, grad_qa), t_dot(h_all, grad_kva)], axis=1)
    )
    return (
        output[None], d_frames[None], d_text[None], d_step[None],
        d_w_ada, d_b_ada, d_w_qkv, d_w_out, d_g_cross, d_w_cq, d_w_ckv, d_w_co,
        d_w_up, d_b_up, d_w_down, d_b_down,
    )


def remote(src, dst, send, recv, peer):
    return pltpu.make_async_remote_copy(
        src_ref=src, dst_ref=dst, send_sem=send, recv_sem=recv,
        device_id=peer, device_id_type=MESH,
    )


def enter(peers):
    barrier = pltpu.get_barrier_semaphore()
    for peer in peers:
        pl.semaphore_signal(barrier, inc=1, device_id=peer, device_id_type=MESH)
    pl.semaphore_wait(barrier, len(peers))


def low_half(shape):
    return lax.broadcasted_iota(jnp.int32, shape, len(shape) - 1) < HEAD


def pick_half(pair, half):
    lower = low_half(pair.shape)
    return jnp.where(lower if half == 0 else ~lower, pair, jnp.zeros_like(pair))


def join_halves(first, second):
    return jnp.where(low_half(first.shape), first, second)


def lanes(index, count=1):
    return pl.ds(pl.multiple_of(index * 128, 128), 128 * count)


def col_sum(values):
    return jnp.sum(values, axis=0, keepdims=True)


def softmax_rows(scores):
    top = jnp.max(scores, axis=-1, keepdims=True)
    raised = jnp.exp(scores - top)
    total = jnp.sum(raised, axis=-1, keepdims=True)
    return raised / total, top + jnp.log(total)


def forward_kernel(
    frames, cot, text, step, picks, mask,
    w_ada, b_ada, w_qkv, w_out, g_cross, w_cq, w_ckv, w_co, w_up, b_up, w_down, b_down,
    output, act, gm_t, h3, gpre, h2, cross, gqc, gc, gkvc, attn, ga, gattn, gx1, query,
    kv, h_all, lse, mods, text_part, early,
    fr, ada_v, qkv_v, out_v, cq_v, ckv_v, co_v, up_v, down_v, prob_c, acc_m, acc_u,
    item, local, send, recv,
):
    seq = lax.axis_index("seq")
    y, x = seq // 2, seq % 2
    x_id, y_id, d_id = y * 2 + 1 - x, (1 - y) * 2 + x, (1 - y) * 2 + 1 - x
    x_peer, y_peer = {"seq": x_id}, {"seq": y_id}
    model = frames.shape[1]
    here = frames.shape[0]
    part = here // 2
    loads = [
        pltpu.make_async_copy(src, dst, local.at[i])
        for i, (src, dst) in enumerate(
            [
                (frames, fr.at[seq]), (w_ada, ada_v), (w_qkv, qkv_v), (w_out, out_v),
                (w_ckv, ckv_v), (w_cq, cq_v), (w_co, co_v), (w_up, up_v), (w_down, down_v),
            ]
        )
    ]
    for load in loads:
        load.start()
    enter([x_peer, y_peer])
    to_x = remote(frames, fr.at[seq], send.at[0], recv.at[0], x_peer)
    to_y = remote(frames, fr.at[seq], send.at[1], recv.at[1], y_peer)
    to_x.start()
    to_y.start()

    def row(at):
        return mods[at : at + 1, :]

    step_f32 = step[...].astype(F32)
    ada = (step_f32 / (1.0 + jnp.exp(-step_f32))).astype(BF16)
    loads[1].wait()
    item[...] = dot(ada, ada_v[...]) + b_ada[...].astype(F32)
    for part_at in range(6):
        mods[part_at : part_at + 1, :] = col_sum(
            item[:, part_at * model : (part_at + 1) * model] * picks[4]
        )
    early[10:11, :] = col_sum(ada.astype(F32) * picks[4])

    def take(block):
        chosen = picks[block]
        shift = col_sum(item[:, :model] * chosen)
        scale = col_sum(item[:, model : 2 * model] * chosen)
        normed, unused = norm_parts(fr[block].astype(F32))
        rows_at = pl.ds(pl.multiple_of(block * here, here), here)
        h_block = (normed * (1.0 + scale) + shift).astype(BF16)
        h_all[rows_at, :] = h_block
        kv[rows_at, :] = dot(h_block, qkv_v[:, model:]).astype(BF16)
        return h_block

    loads[0].wait()
    loads[2].wait()
    h_one = take(seq)
    query[...] = dot(h_one, qkv_v[:, :model]).astype(BF16)
    to_x.wait_recv()
    fwd_y = remote(
        fr.at[x_id, pl.ds(0, part)], fr.at[x_id, pl.ds(0, part)], send.at[2], recv.at[2], y_peer
    )
    fwd_y.start()
    to_y.wait_recv()
    fwd_x = remote(
        fr.at[y_id, pl.ds(part, part)], fr.at[y_id, pl.ds(part, part)],
        send.at[3], recv.at[3], x_peer,
    )
    fwd_x.start()
    take(x_id)
    take(y_id)
    loads[4].wait()
    text_kv = dot(text[...], ckv_v[...]).astype(BF16)
    gkvc[...] = text_kv
    fwd_y.wait_recv()
    fwd_x.wait_recv()
    take(d_id)

    lse[...] = jnp.zeros_like(lse)
    lane_of = lax.broadcasted_iota(jnp.int32, lse.shape, 1)

    @pl.loop(0, HEADS // 2)
    def _(p):
        at = lanes(p)
        value_at = lanes(p + HEADS // 2)
        pair = query[:, at] * jnp.asarray(HEAD ** (-0.5), BF16)
        outs = []
        for half in range(2):
            scores = dot_t(pick_half(pair, half), kv[:, at])
            scores = jnp.where(mask[...] > 0.5, scores, NEG_FILL)
            probs, log_total = softmax_rows(scores)
            lse[...] = jnp.where(lane_of == 2 * p + half, log_total, lse[...])
            outs.append(dot(probs.astype(BF16), kv[:, value_at]))
        attn[:, at] = join_halves(*outs).astype(BF16)

    loads[3].wait()
    branch_a = dot(attn[...], out_v[...])
    x_one = frames_f32(fr[seq]) + row(2) * branch_a
    gx1[...] = branch_a
    gain = g_cross[...].astype(F32)
    normed_1, inverse_1 = norm_parts(x_one)
    h2[...] = (normed_1 * gain).astype(BF16)
    loads[5].wait()
    query_c = dot(h2[...], cq_v[...]).astype(BF16)
    gqc[...] = query_c

    text_rows = text.shape[0]
    key_lane = lax.broadcasted_iota(jnp.int32, (here, text_rows), 1)

    @pl.loop(0, HEADS // 2)
    def _(p):
        at = lanes(p)
        value_at = lanes(p + HEADS // 2)
        pair = gqc[:, at] * jnp.asarray(HEAD ** (-0.5), BF16)
        outs = []
        for half in range(2):
            scores = dot_t(pick_half(pair, half), gkvc[:, at])
            probs, unused = softmax_rows(jnp.where(key_lane < TXT, scores, NEG_FILL))
            prob_c[2 * p + half] = probs
            outs.append(dot(probs.astype(BF16), gkvc[:, value_at]))
        cross[:, at] = join_halves(*outs).astype(BF16)

    loads[6].wait()
    x_two = x_one + dot(cross[...], co_v[...])
    normed_2, inverse_2 = norm_parts(x_two)
    h3[...] = (normed_2 * (1.0 + row(4)) + row(3)).astype(BF16)
    grad_out = cot[...].astype(F32)
    grad_m = row(5) * grad_out
    gm_low = grad_m.astype(BF16)
    gm_t[...] = gm_low.astype(F32).T.astype(BF16)
    early[9:10, :] = col_sum(gm_low.astype(F32))
    gc[...] = gm_low
    acc_m[...] = jnp.zeros_like(acc_m)
    acc_u[...] = jnp.zeros_like(acc_u)
    loads[7].wait()
    loads[8].wait()
    slab = model // 2

    @pl.loop(0, w_up.shape[1] // slab)
    def _(j):
        at = pl.ds(pl.multiple_of(j * slab, slab), slab)
        pre = dot(h3[...], up_v[:, at]) + b_up[:, at].astype(F32)
        inner = GELU_SCALE * (pre + 0.044715 * pre * pre * pre)
        tanh = jnp.tanh(inner)
        act_low = (0.5 * pre * (1.0 + tanh)).astype(BF16)
        act[:, at] = act_low
        acc_m[...] += dot(act_low, down_v[at, :])
        slope = 0.5 * (1.0 + tanh) + 0.5 * pre * (1.0 - tanh * tanh) * (
            GELU_SCALE * (1.0 + 3.0 * 0.044715 * pre * pre)
        )
        grad_pre = (dot_t(gc[...], down_v[at, :]) * slope).astype(BF16)
        gpre[:, at] = grad_pre
        acc_u[...] += dot_t(grad_pre, up_v[:, at])

    for quarter in range(4):
        at = slice(quarter * model, (quarter + 1) * model)
        early[5 + quarter : 6 + quarter, :] = col_sum(gpre[:, at].astype(F32))
    branch_m = acc_m[...] + b_down[...].astype(F32)
    output[...] = (x_two + row(5) * branch_m).astype(BF16)
    early[3:4, :] = col_sum(grad_out * branch_m)
    up_three = acc_u[...]
    early[1:2, :] = col_sum(up_three)
    early[2:3, :] = col_sum(up_three * normed_2)
    grad_x2 = grad_out + norm_back(normed_2, inverse_2, up_three * (1.0 + row(4)))
    acc_m[...] = grad_x2
    gc[...] = grad_x2.astype(BF16)
    ga[...] = dot_t(gc[...], co_v[...]).astype(BF16)

    @pl.loop(0, HEADS // 2)
    def _(p):
        at = lanes(p)
        value_at = lanes(p + HEADS // 2)
        key_pair, value_pair = gkvc[:, at], gkvc[:, value_at]
        query_pair, up_pair = gqc[:, at], ga[:, at]
        d_q, d_k, d_v = [], [], []
        for half in range(2):
            probs = prob_c[2 * p + half]
            grad_probs = dot_t(pick_half(up_pair, half), value_pair)
            inner = jnp.sum(probs * grad_probs, axis=-1, keepdims=True)
            grad_scores = (probs * (grad_probs - inner)).astype(BF16)
            d_q.append(dot(grad_scores, key_pair))
            d_k.append(t_dot(grad_scores, query_pair))
            d_v.append(t_dot(probs.astype(BF16), up_pair))
        gqc[:, at] = (join_halves(*d_q) * HEAD ** (-0.5)).astype(BF16)
        gkvc[:, at] = (join_halves(*d_k) * HEAD ** (-0.5)).astype(BF16)
        gkvc[:, value_at] = join_halves(*d_v).astype(BF16)

    text_part[...] = dot_t(gkvc[...], ckv_v[...]).astype(BF16)
    up_two = dot_t(gqc[...], cq_v[...])
    early[4:5, :] = col_sum(up_two * normed_1)
    grad_x1 = acc_m[...] + norm_back(normed_1, inverse_1, up_two * gain)
    early[0:1, :] = col_sum(grad_x1 * gx1[...])
    early[11:16, :] = jnp.zeros((5, model), F32)
    gx1[...] = grad_x1
    ga[...] = (row(2) * grad_x1).astype(BF16)
    gattn[...] = dot_t(ga[...], out_v[...]).astype(BF16)
    for copy in (to_x, to_y, fwd_x, fwd_y):
        copy.wait_send()


def frames_f32(block):
    return block.astype(F32)


GELU_SCALE = 0.7978845608028654


def backward_kernel(
    act, gm_t, h3, gpre, h2, cross, gqc, gc, gkvc, attn, ga, gattn, gx1, query,
    kv, h_all, lse, mods, text_part, early, text, mask, frames, w_qkv, text_pick,
    out, d_frames, d_text, e_all, l_all,
    G, R0, R1, R2, R3, R4, dqkv, up_low, T, late,
    s0, r0, s1, r1, s2, r2, s3, r3, s4, r4, se, re, sl, rl, st, rt, free,
):
    seq = lax.axis_index("seq")
    rows = lax.axis_index("rows")
    y, x = seq // 2, seq % 2
    z, c = rows // 2, rows % 2
    core_peer = {"rows": z * 2 + (1 - c)}
    x_id, y_id, d_id = y * 2 + 1 - x, (1 - y) * 2 + x, (1 - y) * 2 + 1 - x
    x_peer, y_peer, d_peer = {"seq": x_id}, {"seq": y_id}, {"seq": d_id}
    z_peers = [{"rows": lax.rem(z + d, 4) * 2 + c} for d in (1, 2, 3)]
    enter([core_peer, x_peer, y_peer, d_peer] + z_peers)

    tall, width = G.shape[-2:]
    here, model = frames.shape

    def gather_copies(table, send, recv):
        mine = table.at[c, z, y, x]
        pair = table.at[c, z, y]
        plane = table.at[c, z]
        return (
            [remote(mine, mine, send.at[0], recv.at[0], x_peer)],
            [remote(pair, pair, send.at[1], recv.at[1], y_peer)],
            [
                remote(plane, plane, send.at[1 + d], recv.at[1 + d], z_peers[d - 1])
                for d in (1, 2, 3)
            ],
            [remote(table.at[c], table.at[c], send.at[5], recv.at[5], core_peer)],
        )

    early_steps = gather_copies(e_all, se, re)
    late_steps = gather_copies(l_all, sl, rl)
    text_steps = (
        [remote(T.at[y, x], T.at[y, x], st.at[0], rt.at[0], x_peer)],
        [remote(T.at[y], T.at[y], st.at[1], rt.at[1], y_peer)],
    )

    def advance(steps, at):
        if at:
            for copy in steps[at - 1]:
                copy.wait_recv()
        if at < len(steps):
            for copy in steps[at]:
                copy.start()

    def put(k, s, block):
        low = block.astype(BF16)
        for zz in range(4):
            for cc in range(2):
                at = (zz * 2 + cc) * tall
                G[k, cc, zz, s // 2, s % 2] = low[at : at + tall]

    def put_lanes(k, s, lane, block):
        low = block.astype(BF16)
        for zz in range(4):
            for cc in range(2):
                at = (zz * 2 + cc) * tall
                G[k, cc, zz, s // 2, s % 2, :, lane : lane + 128] = low[at : at + tall]

    def shared(s, first_left, first, second_left, second):
        parity = s % 2
        half_of = (~low_half(first.shape)).astype(jnp.int32)
        first = jnp.where(half_of == parity, first, jnp.zeros_like(first))
        turned = pltpu.roll(second.astype(F32), HEAD, 1)
        half_of = (~low_half(turned.shape)).astype(jnp.int32)
        turned = jnp.where(half_of == parity, 0.0, turned).astype(BF16)
        return t_dot(first_left, first) + t_dot(second_left, turned)

    def compute(k):
        @pl.loop(0, 4)
        def _(s):
            full = s + (s + 1) // 2
            split = 1 + 3 * (s // 2)
            wide = 4 * s + (s + 1) // 2
            if k < 2:
                left = gm_t[pl.ds(pl.multiple_of(s * 2 * tall + k * tall, 16), tall), :]
                for r in range(8):
                    G[k, r % 2, r // 2, s // 2, s % 2] = dot(
                        left, act[:, r * width : (r + 1) * width]
                    ).astype(BF16)
            elif k < 4:
                put(k, s, t_dot(h3[...], gpre[:, lanes(s * 6 + (k - 2) * 3, 3)]))
            elif k == 4:
                put_lanes(k, s, 0, t_dot(h2[...], gqc[:, lanes(full)]))
                put_lanes(k, s, 128, t_dot(cross[...], gc[:, lanes(full)]))
                put_lanes(
                    k, s, 256,
                    shared(s, h2[...], gqc[:, lanes(split)], cross[...], gc[:, lanes(split)]),
                )
            elif k == 5:
                put(k, s, t_dot(text[...], gkvc[:, lanes(s * 3, 3)]))
            elif k == 6:
                put(k, s, t_dot(h_all[...], dqkv[:, lanes(wide, 3)]))
            else:
                put_lanes(k, s, 0, t_dot(h_all[...], dqkv[:, lanes(wide + 3)]))
                put_lanes(
                    k, s, 128,
                    shared(
                        s, h_all[...], dqkv[:, lanes(4 + 9 * (s // 2))],
                        attn[...], ga[:, lanes(split)],
                    ),
                )
                put_lanes(k, s, 256, t_dot(attn[...], ga[:, lanes(full)]))

    def core_copy(k):
        slot = k % 2
        return remote(G.at[k, 1 - c], R0.at[slot], s0.at[k], r0.at[k], core_peer)

    def first_copies(k):
        return (
            remote(G.at[k, c, 0:2, :, 1 - x], R1.at[k, 0], s1.at[k, 0], r1.at[k, 0], x_peer),
            remote(G.at[k, c, 2:4, 1 - y], R1.at[k, 1], s1.at[k, 1], r1.at[k, 1], y_peer),
        )

    def second_copies(k):
        return (
            remote(G.at[k, c, 0:2, 1 - y, x], R2.at[k, 0], s2.at[k, 0], r2.at[k, 0], y_peer),
            remote(G.at[k, c, 2:4, y, 1 - x], R2.at[k, 1], s2.at[k, 1], r2.at[k, 1], x_peer),
        )

    def z_copies(k):
        return [
            remote(
                G.at[k, c, lax.rem(z + d, 4), y, x], R3.at[k, d - 1],
                s3.at[k, d - 1], r3.at[k, d - 1], z_peers[d - 1],
            )
            for d in (1, 2, 3)
        ]

    def add(one, two):
        return (one.astype(F32) + two.astype(F32)).astype(BF16)

    def phase0(k):
        compute(k)
        if k >= 2:
            pl.semaphore_wait(free, 1)
        core_copy(k).start()

    def phase1(k):
        core_copy(k).wait_recv()

        @pl.loop(0, 4)
        def _(zz):
            for yy in range(2):
                for xx in range(2):
                    G[k, c, zz, yy, xx] = add(G[k, c, zz, yy, xx], R0[k % 2, zz, yy, xx])

        if k < CHUNKS - 2:
            pl.semaphore_signal(free, inc=1, device_id=core_peer, device_id_type=MESH)
        for copy in first_copies(k):
            copy.start()

    def phase2(k):
        for copy in first_copies(k):
            copy.wait_recv()
        for zz in range(2):
            for other in range(2):
                G[k, c, zz, other, x] = add(G[k, c, zz, other, x], R1[k, 0, zz, other])
                G[k, c, 2 + zz, y, other] = add(G[k, c, 2 + zz, y, other], R1[k, 1, zz, other])
        for copy in second_copies(k):
            copy.start()

    def phase3(k):
        for copy in second_copies(k):
            copy.wait_recv()
        for zz in range(2):
            G[k, c, zz, y, x] = add(G[k, c, zz, y, x], R2[k, 0, zz])
            G[k, c, 2 + zz, y, x] = add(G[k, c, 2 + zz, y, x], R2[k, 1, zz])
        for copy in z_copies(k):
            copy.start()

    def phase4(k):
        for copy in z_copies(k):
            copy.wait_recv()
        total = G[k, c, z, y, x].astype(F32)
        for d in range(3):
            total = total + R3[k, d].astype(F32)
        out[k] = total

    e_all[c, z, y, x] = early[...]
    T[y, x] = text_part[...]
    phase0(0)
    advance(early_steps, 0)
    advance(text_steps, 0)
    phase0(1)
    phase1(0)
    phase0(2)
    phase1(1)
    phase0(3)
    phase1(2)
    phase0(4)
    phase1(3)
    phase0(5)
    phase1(4)
    phase1(5)
    advance(early_steps, 1)
    advance(text_steps, 1)

    own = pl.ds(pl.multiple_of(seq * here, here), here)
    dqkv[:, :model] = jnp.zeros((dqkv.shape[0], model), BF16)
    lane_of = lax.broadcasted_iota(jnp.int32, lse.shape, 1)

    @pl.loop(0, HEADS // 2)
    def _(p):
        at = lanes(p)
        key_at = lanes(p + HEADS // 2)
        value_at = lanes(p + HEADS)
        key_pair, value_pair = kv[:, at], kv[:, key_at]
        query_pair, up_pair = query[:, at], gattn[:, at]
        scaled = query_pair * jnp.asarray(HEAD ** (-0.5), BF16)
        d_q, d_k, d_v = [], [], []
        for half in range(2):
            scores = dot_t(pick_half(scaled, half), key_pair)
            log_total = jnp.sum(
                jnp.where(lane_of == 2 * p + half, lse[...], 0.0), axis=-1, keepdims=True
            )
            scores = jnp.where(mask[...] > 0.5, scores, NEG_FILL)
            probs = jnp.exp(scores - log_total)
            grad_probs = dot_t(pick_half(up_pair, half), value_pair)
            inner = jnp.sum(probs * grad_probs, axis=-1, keepdims=True)
            grad_scores = (probs * (grad_probs - inner)).astype(BF16)
            d_q.append(dot(grad_scores, key_pair))
            d_k.append(t_dot(grad_scores, query_pair))
            d_v.append(t_dot(probs.astype(BF16), up_pair))
        dqkv[own, at] = (join_halves(*d_q) * HEAD ** (-0.5)).astype(BF16)
        dqkv[:, key_at] = (join_halves(*d_k) * HEAD ** (-0.5)).astype(BF16)
        dqkv[:, value_at] = join_halves(*d_v).astype(BF16)
        phase2(p)

    def up_block(block):
        rows_at = pl.ds(pl.multiple_of(block * here, here), here)
        return dot_t(dqkv[rows_at, model:], w_qkv[:, model:])

    up_copies = []
    for i, (block, peer) in enumerate(((d_id, d_peer), (x_id, x_peer), (y_id, y_peer))):
        up_low[i] = up_block(block).astype(BF16)
        copy = remote(up_low.at[i], R4.at[i], s4.at[i], r4.at[i], peer)
        copy.start()
        up_copies.append(copy)
    phase0(6)
    phase0(7)
    phase1(6)
    phase1(7)
    advance(early_steps, 2)
    advance(text_steps, 2)

    @pl.loop(0, 6)
    def _(k):
        phase3(k)

    for copy in up_copies:
        copy.wait_recv()
    up_one = dot_t(dqkv[own, :], w_qkv[...])
    for i in range(3):
        up_one = up_one + R4[i].astype(F32)
    normed, inverse = norm_parts(frames[...].astype(F32))
    late[0:1, :] = col_sum(up_one)
    late[1:2, :] = col_sum(up_one * normed)
    late[2:8, :] = jnp.zeros((6, model), F32)
    d_frames[...] = gx1[...] + norm_back(normed, inverse, up_one * (1.0 + mods[1:2, :]))
    l_all[c, z, y, x] = late[...]
    advance(late_steps, 0)
    total = jnp.zeros(d_text.shape, F32)
    for i in range(4):
        total = total + T[i // 2, i % 2].astype(F32) * text_pick[i]
    d_text[...] = total
    phase2(6)
    advance(late_steps, 1)
    phase2(7)
    advance(early_steps, 3)

    @pl.loop(0, 6)
    def _(k):
        phase4(k)

    advance(late_steps, 2)
    phase3(6)
    phase3(7)
    advance(late_steps, 3)
    phase4(6)
    phase4(7)
    advance(early_steps, 4)
    advance(late_steps, 4)

    @pl.loop(0, CHUNKS)
    def _(k):
        core_copy(k).wait_send()
        for copy in (*first_copies(k), *second_copies(k), *z_copies(k)):
            copy.wait_send()

    for copy in up_copies:
        copy.wait_send()
    for steps in (early_steps, late_steps, text_steps):
        for step in steps:
            for copy in step:
                copy.wait_send()


def in_vmem(count):
    return [pl.BlockSpec(memory_space=pltpu.VMEM)] * count


def in_any(count):
    return [pl.BlockSpec(memory_space=pl.ANY)] * count


def per_device(
    frames, text_tokens, step_embed, segments, cotangent,
    w_ada, b_ada, w_qkv, w_out, g_cross, w_cq, w_ckv, w_co, w_up, b_up, w_down, b_down,
):
    seq_count = lax.axis_size("seq")
    rows_count = lax.axis_size("rows")
    seq_index = lax.axis_index("seq")
    rows_index = lax.axis_index("rows")
    frames, text_tokens, step_embed = frames[0], text_tokens[0], step_embed[0]
    segments, cotangent = segments[0], cotangent[0]
    here, model = frames.shape
    length = segments.shape[0]
    hidden = w_up.shape[1]
    assert (length // ITEMS) % here == 0
    block_slots = segments[::here]
    slot = lax.dynamic_index_in_dim(block_slots, seq_index, 0, keepdims=False)
    mask = (segments == slot).astype(F32)[None]
    text_rows = 128
    text_mine = jnp.pad(
        lax.dynamic_slice_in_dim(text_tokens, slot * TXT, TXT, axis=0),
        ((0, text_rows - TXT), (0, 0)),
    )
    step_rows = 16
    step_pad = jnp.pad(step_embed, ((0, step_rows - ITEMS), (0, 0)))
    wanted = jnp.concatenate([block_slots, slot[None]])
    picks = (wanted[:, None] == jnp.arange(step_rows)[None, :]).astype(F32)[:, :, None]
    text_pick = (block_slots == seq_index).astype(F32)[:, None, None]

    def like(shape, dtype=BF16):
        return jax.ShapeDtypeStruct(shape, dtype)

    square = like((here, model))
    dma = pltpu.SemaphoreType.DMA
    vmem = pltpu.VMEM
    (
        output, act, gm_t, h3, gpre, h2, cross, gqc, gc, gkvc, attn, ga, gattn, gx1, query,
        kv, h_all, lse, mods, text_part, early,
    ) = pl.pallas_call(
        forward_kernel,
        out_shape=(
            square, like((here, hidden)), like((model, here)), square, like((here, hidden)),
            square, square, square, square, like((text_rows, 2 * model)), square, square,
            square, like((here, model), F32), square, like((length, 2 * model)),
            like((length, model)), like((here, 128), F32), like((8, model), F32),
            like((text_rows, model)), like((16, model), F32),
        ),
        in_specs=in_any(1) + in_vmem(5)
        + in_any(1) + in_vmem(1) + in_any(2) + in_vmem(1) + in_any(4) + in_vmem(1)
        + in_any(1) + in_vmem(1),
        out_specs=tuple(in_vmem(21)),
        scratch_shapes=[
            vmem((seq_count, here, model), BF16),
            vmem(w_ada.shape, BF16), vmem(w_qkv.shape, BF16), vmem(w_out.shape, BF16),
            vmem(w_cq.shape, BF16), vmem(w_ckv.shape, BF16), vmem(w_co.shape, BF16),
            vmem(w_up.shape, BF16), vmem(w_down.shape, BF16),
            vmem((HEADS, here, text_rows), F32),
            vmem((here, model), F32), vmem((here, model), F32),
            vmem((step_rows, 6 * model), F32),
            dma((9,)), dma((4,)), dma((4,)),
        ],
        compiler_params=pltpu.CompilerParams(
            collective_id=0, has_side_effects=True, vmem_limit_bytes=VMEM_MOST
        ),
        name="forward_layer",
    )(
        frames, cotangent, text_mine, step_pad, picks, mask,
        w_ada, b_ada[None], w_qkv, w_out, g_cross[None], w_cq, w_ckv, w_co, w_up,
        b_up[None], w_down, b_down[None],
    )

    tall, width = model // rows_count, model // 2
    table = (2, 4, 2, 2)
    done, d_frames, d_text, e_all, l_all = pl.pallas_call(
        backward_kernel,
        out_shape=(
            like((CHUNKS, tall, width), F32), like((here, model), F32),
            like((text_rows, model), F32), like(table + (16, model), F32),
            like(table + (8, model), F32),
        ),
        in_specs=in_vmem(25),
        out_specs=tuple(in_vmem(5)),
        scratch_shapes=[
            vmem((CHUNKS,) + table + (tall, width), BF16),
            vmem((2, 4, 2, 2, tall, width), BF16),
            vmem((CHUNKS, 2, 2, 2, tall, width), BF16),
            vmem((CHUNKS, 2, 2, tall, width), BF16),
            vmem((CHUNKS, 3, tall, width), BF16),
            vmem((3, here, model), BF16),
            vmem((length, 3 * model), BF16),
            vmem((3, here, model), BF16),
            vmem((2, 2, text_rows, model), BF16),
            vmem((8, model), F32),
            dma((CHUNKS,)), dma((CHUNKS,)),
            dma((CHUNKS, 2)), dma((CHUNKS, 2)),
            dma((CHUNKS, 2)), dma((CHUNKS, 2)),
            dma((CHUNKS, 3)), dma((CHUNKS, 3)),
            dma((3,)), dma((3,)), dma((6,)), dma((6,)), dma((6,)), dma((6,)),
            dma((2,)), dma((2,)), pltpu.SemaphoreType.REGULAR,
        ],
        compiler_params=pltpu.CompilerParams(
            collective_id=1, has_side_effects=True, vmem_limit_bytes=VMEM_MOST
        ),
        name="backward_layer",
    )(
        act, gm_t, h3, gpre, h2, cross, gqc, gc, gkvc, attn, ga, gattn, gx1, query,
        kv, h_all, lse, mods, text_part, early, text_mine, mask, frames, w_qkv, text_pick,
    )

    def by_device(entries):
        return entries.transpose(1, 0, 2, 3, 4, 5).reshape(
            (rows_count * seq_count,) + entries.shape[4:]
        )

    e_all, l_all = by_device(e_all), by_device(l_all)
    item_all = jnp.concatenate([l_all[:, :2], e_all[:, :4]], axis=1).reshape(
        rows_count * seq_count, 6 * model
    )
    ada_all = e_all[:, 10]

    def share(vector, count, index):
        size = vector.shape[-1] // count
        return lax.dynamic_slice_in_dim(vector, index * size, size, axis=-1)

    d_b_ada = share(jnp.sum(item_all, axis=0), rows_count, rows_index)
    d_g_cross = share(jnp.sum(e_all[:, 4], axis=0), rows_count, rows_index)
    d_b_up = share(jnp.sum(e_all[:, 5:9], axis=0).reshape(-1), rows_count, rows_index)
    d_b_down = share(jnp.sum(e_all[:, 9], axis=0), rows_count, rows_index)
    d_w_ada = lax.dot_general(
        share(ada_all, rows_count, rows_index),
        share(item_all, seq_count, seq_index),
        (((0,), (0,)), ((), ())),
        precision=PRECISE,
        preferred_element_type=F32,
    )
    row_items = lax.dynamic_slice_in_dim(item_all, rows_index * seq_count, seq_count, axis=0)
    item_mine = jnp.sum(row_items * text_pick[:, 0], axis=0, keepdims=True)
    item_high = item_mine.astype(BF16)
    item_low = (item_mine - item_high.astype(F32)).astype(BF16)
    d_ada = jnp.sum(
        dot_t(jnp.concatenate([item_high, item_low], axis=0), w_ada), axis=0, keepdims=True
    )
    my_step = lax.dynamic_slice_in_dim(step_embed, seq_index, 1, axis=0).astype(F32)
    unused_step, silu_back = jax.vjp(jax.nn.silu, my_step)
    d_step = silu_back(d_ada)[0]

    odd = seq_index % 2 == 1

    def place(full, mixed, first):
        even = mixed[:, :HEAD] if first else mixed[:, HEAD:]
        other = mixed[:, HEAD:] if first else mixed[:, :HEAD]
        return jnp.where(
            odd,
            jnp.concatenate([other, full], axis=1),
            jnp.concatenate([full, even], axis=1),
        )

    d_w_down = jnp.concatenate([done[0], done[1]], axis=0).T
    d_w_up = jnp.concatenate([done[2], done[3]], axis=1)
    d_w_cq = place(done[4][:, :128], done[4][:, 256:], True)
    d_w_co = place(done[4][:, 128:256], done[4][:, 256:], False)
    d_w_ckv = done[5]
    d_w_qkv = place(
        jnp.concatenate([done[6], done[7][:, :128]], axis=1), done[7][:, 128:256], True
    )
    d_w_out = place(done[7][:, 256:], done[7][:, 128:256], False)
    return (
        output[None], d_frames[None], d_text[None, :TXT], d_step[None],
        d_w_ada, d_b_ada, d_w_qkv, d_w_out, d_g_cross, d_w_cq, d_w_ckv, d_w_co,
        d_w_up, d_b_up, d_w_down, d_b_down,
    )


def solution(mesh):
    row_seq = P("rows", "seq", None)
    in_specs = (
        row_seq, P("rows", None, None), P("rows", None, None), P("rows", None), row_seq,
    ) + (P(),) * 12
    out_specs = (row_seq,) * 4 + (
        P("rows", "seq"), P("rows"), P("rows", "seq"), P("rows", "seq"), P("rows"),
        P("rows", "seq"), P("rows", "seq"), P("rows", "seq"), P("rows", "seq"), P("rows"),
        P("rows", "seq"), P("rows"),
    )
    fused = mesh.shape["rows"] == 8 and mesh.shape["seq"] == 4
    return jax.shard_map(
        per_device if fused else per_device_plain, mesh=mesh, in_specs=in_specs, out_specs=out_specs, check_vma=False
    )
```

```python
import functools

import jax
import jax.numpy as jnp
from jax import lax
from jax.experimental import pallas as pl
from jax.experimental.pallas import tpu as pltpu
from jax.sharding import PartitionSpec as P

HEADS = 12
HEAD = 64
TXT = 77
ITEMS = 4

EPSILON = 1e-06
NEG_FILL = -1e30
PRECISE = lax.Precision.HIGHEST
F32 = jnp.float32
BF16 = jnp.bfloat16
MESH = pl.DeviceIdType.MESH
CHUNKS = 8
VMEM_MOST = 67_043_328


def dot(left, right):
    return jnp.dot(left, right, preferred_element_type=F32)


def dot_t(left, right):
    return lax.dot_general(left, right, (((1,), (1,)), ((), ())), preferred_element_type=F32)


def t_dot(left, right):
    return lax.dot_general(left, right, (((0,), (0,)), ((), ())), preferred_element_type=F32)


def norm_parts(values):
    center = values - jnp.mean(values, axis=-1, keepdims=True)
    inverse = lax.rsqrt(jnp.mean(center * center, axis=-1, keepdims=True) + EPSILON)
    return center * inverse, inverse


def norm_back(normed, inverse, upstream):
    return inverse * (
        upstream
        - jnp.mean(upstream, axis=-1, keepdims=True)
        - normed * jnp.mean(upstream * normed, axis=-1, keepdims=True)
    )


def gelu_tanh(values):
    return jax.nn.gelu(values, approximate=True)


def split_heads(matrix):
    return matrix.reshape(matrix.shape[0], HEADS, HEAD)


def scores_of(queries, keyset, allowed):
    raw = jnp.einsum(
        "qhd,khd->hqk", split_heads(queries), split_heads(keyset), preferred_element_type=F32
    )
    raw = raw * HEAD ** (-0.5)
    return raw if allowed is None else jnp.where(allowed[None, None, :], raw, NEG_FILL)


def attend_forward(queries, keyset, valueset, allowed):
    scores = scores_of(queries, keyset, allowed)
    top_score = jnp.max(scores, axis=-1, keepdims=True)
    exp_scores = jnp.exp(scores - top_score)
    totals = jnp.sum(exp_scores, axis=-1, keepdims=True)
    probs_low = (exp_scores / totals).astype(BF16)
    mixed = jnp.einsum(
        "hqk,khd->qhd", probs_low, split_heads(valueset), preferred_element_type=F32
    )
    return mixed.reshape(queries.shape).astype(BF16), top_score + jnp.log(totals)


def attend_backward(queries, keyset, valueset, allowed, log_total, upstream):
    probs = jnp.exp(scores_of(queries, keyset, allowed) - log_total)
    up_heads = split_heads(upstream)
    grad_probs = jnp.einsum(
        "qhd,khd->hqk", up_heads, split_heads(valueset), preferred_element_type=F32
    )
    inner = jnp.sum(probs * grad_probs, axis=-1, keepdims=True)
    grad_scores = (probs * (grad_probs - inner)).astype(BF16)
    grad_query = jnp.einsum(
        "hqk,khd->qhd", grad_scores, split_heads(keyset), preferred_element_type=F32
    )
    grad_key = jnp.einsum(
        "hqk,qhd->khd", grad_scores, split_heads(queries), preferred_element_type=F32
    )
    grad_value = jnp.einsum(
        "hqk,qhd->khd", probs.astype(BF16), up_heads, preferred_element_type=F32
    )
    return (
        (grad_query.reshape(queries.shape) * HEAD ** (-0.5)).astype(BF16),
        (grad_key.reshape(keyset.shape) * HEAD ** (-0.5)).astype(BF16),
        grad_value.reshape(valueset.shape).astype(BF16),
    )


def scatter_plain(matrix):
    part = lax.psum_scatter(matrix.astype(BF16), "rows", scatter_dimension=0, tiled=True)
    part = lax.psum_scatter(part, "seq", scatter_dimension=1, tiled=True)
    return part.astype(F32)


def per_device_plain(
    frames, text_tokens, step_embed, segments, cotangent,
    w_ada, b_ada, w_qkv, w_out, g_cross, w_cq, w_ckv, w_co, w_up, b_up, w_down, b_down,
):
    seq_count = lax.axis_size("seq")
    rows_count = lax.axis_size("rows")
    seq_index = lax.axis_index("seq")
    rows_index = lax.axis_index("rows")
    frames, text_tokens, step_embed = frames[0], text_tokens[0], step_embed[0]
    segments, cotangent = segments[0], cotangent[0]
    here, model = frames.shape
    length = segments.shape[0]
    assert (length // ITEMS) % here == 0
    block_slots = segments[::here]
    slot = lax.dynamic_index_in_dim(block_slots, seq_index, 0, keepdims=False)
    allowed = segments == slot
    text_mine = lax.dynamic_slice_in_dim(text_tokens, slot * TXT, TXT, axis=0)

    frames_all = lax.all_gather(frames, "seq", axis=0, tiled=True)
    ada_in = jax.nn.silu(step_embed.astype(F32)).astype(BF16)
    item_mod = dot(ada_in, w_ada) + b_ada.astype(F32)
    mine = lax.dynamic_slice_in_dim(item_mod, slot, 1, axis=0)
    shift_a, scale_a, gate_a, shift_b, scale_b, gate_b = jnp.split(mine, 6, axis=-1)

    normed_all, inverse_all = norm_parts(frames_all.astype(F32))
    hot = (block_slots[:, None] == jnp.arange(ITEMS)[None, :]).astype(F32)
    block_mod = jnp.dot(hot, item_mod[:, : 2 * model], precision=PRECISE)
    frame_mod = jnp.repeat(block_mod, here, axis=0)
    h_all = (normed_all * (1.0 + frame_mod[:, model:]) + frame_mod[:, :model]).astype(BF16)
    frames_f32 = frames.astype(F32)
    normed_0, inverse_0 = norm_parts(frames_f32)
    h_one = (normed_0 * (1.0 + scale_a) + shift_a).astype(BF16)
    query_a = dot(h_one, w_qkv[:, :model]).astype(BF16)
    kv_all = dot(h_all, w_qkv[:, model:]).astype(BF16)
    key_all, value_all = kv_all[:, :model], kv_all[:, model:]
    attn_low, lse_self = attend_forward(query_a, key_all, value_all, allowed)
    branch_a = dot(attn_low, w_out)
    x_one = frames_f32 + gate_a * branch_a
    gain = g_cross.astype(F32)[None]
    normed_1, inverse_1 = norm_parts(x_one)
    h_two = (normed_1 * gain).astype(BF16)
    query_c = dot(h_two, w_cq).astype(BF16)
    text_kv = dot(text_mine, w_ckv).astype(BF16)
    key_c, value_c = text_kv[:, :model], text_kv[:, model:]
    cross_low, lse_cross = attend_forward(query_c, key_c, value_c, None)
    x_two = x_one + dot(cross_low, w_co)
    normed_2, inverse_2 = norm_parts(x_two)
    h_three = (normed_2 * (1.0 + scale_b) + shift_b).astype(BF16)
    pre_act = dot(h_three, w_up) + b_up.astype(F32)
    act_low = gelu_tanh(pre_act).astype(BF16)
    branch_m = dot(act_low, w_down) + b_down.astype(F32)
    output = (x_two + gate_b * branch_m).astype(BF16)

    grad_out = cotangent.astype(F32)
    grad_m = (gate_b * grad_out).astype(BF16)
    grad_act = dot_t(grad_m, w_down)
    unused_act, gelu_back = jax.vjp(gelu_tanh, pre_act)
    grad_pre = gelu_back(grad_act)[0].astype(BF16)
    up_three = dot_t(grad_pre, w_up)
    grad_x2 = grad_out + norm_back(normed_2, inverse_2, up_three * (1.0 + scale_b))
    grad_c = grad_x2.astype(BF16)
    grad_cross = dot_t(grad_c, w_co).astype(BF16)
    grad_qc, grad_kc, grad_vc = attend_backward(
        query_c, key_c, value_c, None, lse_cross, grad_cross
    )
    grad_kvc = jnp.concatenate([grad_kc, grad_vc], axis=-1)
    up_two = dot_t(grad_qc, w_cq)
    grad_x1 = grad_x2 + norm_back(normed_1, inverse_1, up_two * gain)
    grad_a = (gate_a * grad_x1).astype(BF16)
    grad_attn = dot_t(grad_a, w_out).astype(BF16)
    grad_qa, grad_ka, grad_va = attend_backward(
        query_a, key_all, value_all, allowed, lse_self, grad_attn
    )
    grad_kva = jnp.concatenate([grad_ka, grad_va], axis=-1)
    up_kv = dot_t(grad_kva, w_qkv[:, model:]).astype(BF16)
    up_one = dot_t(grad_qa, w_qkv[:, :model]) + lax.psum_scatter(
        up_kv, "seq", scatter_dimension=0, tiled=True
    ).astype(F32)
    d_frames = grad_x1 + norm_back(normed_0, inverse_0, up_one * (1.0 + scale_a))

    small = jnp.concatenate(
        [
            jnp.sum(up_one, axis=0),
            jnp.sum(up_one * normed_0, axis=0),
            jnp.sum(grad_x1 * branch_a, axis=0),
            jnp.sum(up_three, axis=0),
            jnp.sum(up_three * normed_2, axis=0),
            jnp.sum(grad_out * branch_m, axis=0),
            jnp.sum(up_two * normed_1, axis=0),
            jnp.sum(grad_pre.astype(F32), axis=0),
            jnp.sum(grad_m.astype(F32), axis=0),
            lax.dynamic_index_in_dim(ada_in, slot, 0, keepdims=False).astype(F32),
        ]
    )
    small_all = lax.all_gather(small, ("rows", "seq"), axis=0, tiled=False)
    small_all = small_all.reshape(rows_count * seq_count, -1)
    item_all = small_all[:, : 6 * model]
    bias_all = small_all[:, 6 * model : -model]
    ada_all = small_all[:, -model:]

    def share(table, count, index):
        size = table.shape[-1] // count
        return lax.dynamic_slice_in_dim(table, index * size, size, axis=-1)

    def bias_sum(table):
        return jnp.sum(share(table, rows_count, rows_index), axis=0)

    d_b_ada = bias_sum(item_all)
    d_g_cross = bias_sum(bias_all[:, :model])
    d_b_up = bias_sum(bias_all[:, model:-model])
    d_b_down = bias_sum(bias_all[:, -model:])
    d_w_ada = lax.dot_general(
        share(ada_all, rows_count, rows_index),
        share(item_all, seq_count, seq_index),
        (((0,), (0,)), ((), ())),
        precision=PRECISE,
        preferred_element_type=F32,
    )
    item_share = ITEMS // seq_count
    row_items = lax.dynamic_slice_in_dim(item_all, rows_index * seq_count, seq_count, axis=0)
    owned = seq_index * item_share + jnp.arange(item_share)
    pick = (owned[:, None] == block_slots[None, :]).astype(F32)
    item_mine = jnp.dot(pick, row_items, precision=PRECISE)
    d_ada = lax.dot_general(
        item_mine, w_ada.astype(F32), (((1,), (1,)), ((), ())), precision=PRECISE
    )
    my_step = lax.dynamic_slice_in_dim(
        step_embed, seq_index * item_share, item_share, axis=0
    ).astype(F32)
    unused_step, silu_back = jax.vjp(jax.nn.silu, my_step)
    d_step = silu_back(d_ada)[0]
    text_part = dot_t(grad_kvc, w_ckv).astype(BF16)
    text_full = lax.dynamic_update_slice_in_dim(
        jnp.zeros(text_tokens.shape, BF16), text_part, slot * TXT, axis=0
    )
    d_text = lax.psum_scatter(text_full, "seq", scatter_dimension=0, tiled=True).astype(F32)

    d_w_down = scatter_plain(t_dot(act_low, grad_m))
    d_w_up = scatter_plain(t_dot(h_three, grad_pre))
    d_w_cq = scatter_plain(t_dot(h_two, grad_qc))
    d_w_co = scatter_plain(t_dot(cross_low, grad_c))
    d_w_ckv = scatter_plain(t_dot(text_mine, grad_kvc))
    d_w_out = scatter_plain(t_dot(attn_low, grad_a))
    d_w_qkv = scatter_plain(
        jnp.concatenate([t_dot(h_one, grad_qa), t_dot(h_all, grad_kva)], axis=1)
    )
    return (
        output[None], d_frames[None], d_text[None], d_step[None],
        d_w_ada, d_b_ada, d_w_qkv, d_w_out, d_g_cross, d_w_cq, d_w_ckv, d_w_co,
        d_w_up, d_b_up, d_w_down, d_b_down,
    )


def remote(src, dst, send, recv, peer):
    return pltpu.make_async_remote_copy(
        src_ref=src, dst_ref=dst, send_sem=send, recv_sem=recv,
        device_id=peer, device_id_type=MESH,
    )


def enter(peers):
    barrier = pltpu.get_barrier_semaphore()
    for peer in peers:
        pl.semaphore_signal(barrier, inc=1, device_id=peer, device_id_type=MESH)
    pl.semaphore_wait(barrier, len(peers))


def low_half(shape):
    return lax.broadcasted_iota(jnp.int32, shape, len(shape) - 1) < HEAD


def pick_half(pair, half):
    lower = low_half(pair.shape)
    return jnp.where(lower if half == 0 else ~lower, pair, jnp.zeros_like(pair))


def join_halves(first, second):
    return jnp.where(low_half(first.shape), first, second)


def lanes(index, count=1):
    return pl.ds(pl.multiple_of(index * 128, 128), 128 * count)


def col_sum(values):
    return jnp.sum(values, axis=0, keepdims=True)


def softmax_rows(scores):
    top = jnp.max(scores, axis=-1, keepdims=True)
    raised = jnp.exp(scores - top)
    total = jnp.sum(raised, axis=-1, keepdims=True)
    return raised / total, top + jnp.log(total)


def forward_kernel(
    frames, cot, text, step, seg_s, seg,
    w_ada, b_ada, w_qkv, w_out, g_cross, w_cq, w_ckv, w_co, w_up, b_up, w_down, b_down,
    output, act, gm_t, h3, gpre, h2, cross, gqc, gc, gkvc, attn, ga, gattn, gx1, query,
    kv, h_all, lse, mods, text_part, early, text_mine,
    fr, ada_v, qkv_v, out_v, cq_v, ckv_v, co_v, up_v, down_v, prob_c, acc_m, acc_u,
    item, up_bias, local, send, recv,
):
    seq = lax.axis_index("seq")
    y, x = seq // 2, seq % 2
    x_id, y_id, d_id = y * 2 + 1 - x, (1 - y) * 2 + x, (1 - y) * 2 + 1 - x
    x_peer, y_peer = {"seq": x_id}, {"seq": y_id}
    frames = frames.at[0]
    here, model = frames.shape
    part = here // 2
    slot = seg_s[0, seq * here]
    mask = seg[...] == slot
    loads = [
        pltpu.make_async_copy(src, dst, local.at[i])
        for i, (src, dst) in enumerate(
            [
                (frames, fr.at[seq]), (w_ada, ada_v), (w_qkv, qkv_v), (w_out, out_v),
                (w_ckv, ckv_v), (w_cq, cq_v), (w_co, co_v), (w_up, up_v), (w_down, down_v),
            ]
        )
    ]
    for load in loads:
        load.start()
    enter([x_peer, y_peer])
    to_x = remote(frames, fr.at[seq], send.at[0], recv.at[0], x_peer)
    to_y = remote(frames, fr.at[seq], send.at[1], recv.at[1], y_peer)
    to_x.start()
    to_y.start()

    def row(at):
        return mods[at : at + 1, :]

    step_f32 = jnp.concatenate(
        [step[0].astype(F32), jnp.zeros((item.shape[0] - ITEMS, model), F32)], axis=0
    )
    ada = (step_f32 / (1.0 + jnp.exp(-step_f32))).astype(BF16)
    loads[1].wait()
    item[...] = dot(ada, ada_v[...]) + b_ada[...].astype(F32)[None]
    slot_row = lax.broadcasted_iota(jnp.int32, (item.shape[0], model), 0)
    chosen_mine = (slot_row == slot).astype(F32)
    for part_at in range(6):
        mods[part_at : part_at + 1, :] = col_sum(
            item[:, part_at * model : (part_at + 1) * model] * chosen_mine
        )
    early[10:11, :] = col_sum(ada.astype(F32) * chosen_mine)
    up_bias[...] = b_up[...].astype(F32)[None]

    def take(block):
        chosen = (slot_row == seg_s[0, block * here]).astype(F32)
        shift = col_sum(item[:, :model] * chosen)
        scale = col_sum(item[:, model : 2 * model] * chosen)
        normed, unused = norm_parts(fr[block].astype(F32))
        rows_at = pl.ds(pl.multiple_of(block * here, here), here)
        h_block = (normed * (1.0 + scale) + shift).astype(BF16)
        h_all[rows_at, :] = h_block
        kv[rows_at, :] = dot(h_block, qkv_v[:, model:]).astype(BF16)
        return h_block

    loads[0].wait()
    loads[2].wait()
    h_one = take(seq)
    query[...] = dot(h_one, qkv_v[:, :model]).astype(BF16)
    to_x.wait_recv()
    fwd_y = remote(
        fr.at[x_id, pl.ds(0, part)], fr.at[x_id, pl.ds(0, part)], send.at[2], recv.at[2], y_peer
    )
    fwd_y.start()
    to_y.wait_recv()
    fwd_x = remote(
        fr.at[y_id, pl.ds(part, part)], fr.at[y_id, pl.ds(part, part)],
        send.at[3], recv.at[3], x_peer,
    )
    fwd_x.start()
    take(x_id)
    take(y_id)
    loads[4].wait()
    picked = (text_mine.shape[0], text.shape[1])
    text_at = lax.broadcasted_iota(jnp.int32, picked, 0)
    token = lax.broadcasted_iota(jnp.int32, picked, 1)
    hot = jnp.where((token == text_at + TXT * slot) & (text_at < TXT), 1.0, 0.0).astype(BF16)
    text_mine[...] = dot(hot, text[0]).astype(BF16)
    text_kv = dot(text_mine[...], ckv_v[...]).astype(BF16)
    gkvc[...] = text_kv
    fwd_y.wait_recv()
    fwd_x.wait_recv()
    take(d_id)

    lse[...] = jnp.zeros_like(lse)
    lane_of = lax.broadcasted_iota(jnp.int32, lse.shape, 1)

    @pl.loop(0, HEADS // 2)
    def _(p):
        at = lanes(p)
        value_at = lanes(p + HEADS // 2)
        pair = query[:, at] * jnp.asarray(HEAD ** (-0.5), BF16)
        outs = []
        for half in range(2):
            scores = dot_t(pick_half(pair, half), kv[:, at])
            scores = jnp.where(mask, scores, NEG_FILL)
            probs, log_total = softmax_rows(scores)
            lse[...] = jnp.where(lane_of == 2 * p + half, log_total, lse[...])
            outs.append(dot(probs.astype(BF16), kv[:, value_at]))
        attn[:, at] = join_halves(*outs).astype(BF16)

    loads[3].wait()
    branch_a = dot(attn[...], out_v[...])
    x_one = frames_f32(fr[seq]) + row(2) * branch_a
    gx1[...] = branch_a
    gain = g_cross[...].astype(F32)[None]
    normed_1, inverse_1 = norm_parts(x_one)
    h2[...] = (normed_1 * gain).astype(BF16)
    loads[5].wait()
    query_c = dot(h2[...], cq_v[...]).astype(BF16)
    gqc[...] = query_c

    text_rows = text_mine.shape[0]
    key_lane = lax.broadcasted_iota(jnp.int32, (here, text_rows), 1)

    @pl.loop(0, HEADS // 2)
    def _(p):
        at = lanes(p)
        value_at = lanes(p + HEADS // 2)
        pair = gqc[:, at] * jnp.asarray(HEAD ** (-0.5), BF16)
        outs = []
        for half in range(2):
            scores = dot_t(pick_half(pair, half), gkvc[:, at])
            probs, unused = softmax_rows(jnp.where(key_lane < TXT, scores, NEG_FILL))
            prob_c[2 * p + half] = probs
            outs.append(dot(probs.astype(BF16), gkvc[:, value_at]))
        cross[:, at] = join_halves(*outs).astype(BF16)

    loads[6].wait()
    x_two = x_one + dot(cross[...], co_v[...])
    normed_2, inverse_2 = norm_parts(x_two)
    h3[...] = (normed_2 * (1.0 + row(4)) + row(3)).astype(BF16)
    grad_out = cot[0].astype(F32)
    grad_m = row(5) * grad_out
    gm_low = grad_m.astype(BF16)
    gm_t[...] = gm_low.astype(F32).T.astype(BF16)
    early[9:10, :] = col_sum(gm_low.astype(F32))
    gc[...] = gm_low
    acc_m[...] = jnp.zeros_like(acc_m)
    acc_u[...] = jnp.zeros_like(acc_u)
    loads[7].wait()
    loads[8].wait()
    slab = model // 2

    @pl.loop(0, w_up.shape[1] // slab)
    def _(j):
        at = pl.ds(pl.multiple_of(j * slab, slab), slab)
        pre = dot(h3[...], up_v[:, at]) + up_bias[:, at]
        inner = GELU_SCALE * (pre + 0.044715 * pre * pre * pre)
        tanh = jnp.tanh(inner)
        act_low = (0.5 * pre * (1.0 + tanh)).astype(BF16)
        act[:, at] = act_low
        acc_m[...] += dot(act_low, down_v[at, :])
        slope = 0.5 * (1.0 + tanh) + 0.5 * pre * (1.0 - tanh * tanh) * (
            GELU_SCALE * (1.0 + 3.0 * 0.044715 * pre * pre)
        )
        grad_pre = (dot_t(gc[...], down_v[at, :]) * slope).astype(BF16)
        gpre[:, at] = grad_pre
        acc_u[...] += dot_t(grad_pre, up_v[:, at])

    for quarter in range(4):
        at = slice(quarter * model, (quarter + 1) * model)
        early[5 + quarter : 6 + quarter, :] = col_sum(gpre[:, at].astype(F32))
    branch_m = acc_m[...] + b_down[...].astype(F32)[None]
    output[...] = (x_two + row(5) * branch_m).astype(BF16)
    early[3:4, :] = col_sum(grad_out * branch_m)
    up_three = acc_u[...]
    early[1:2, :] = col_sum(up_three)
    early[2:3, :] = col_sum(up_three * normed_2)
    grad_x2 = grad_out + norm_back(normed_2, inverse_2, up_three * (1.0 + row(4)))
    acc_m[...] = grad_x2
    gc[...] = grad_x2.astype(BF16)
    ga[...] = dot_t(gc[...], co_v[...]).astype(BF16)

    @pl.loop(0, HEADS // 2)
    def _(p):
        at = lanes(p)
        value_at = lanes(p + HEADS // 2)
        key_pair, value_pair = gkvc[:, at], gkvc[:, value_at]
        query_pair, up_pair = gqc[:, at], ga[:, at]
        d_q, d_k, d_v = [], [], []
        for half in range(2):
            probs = prob_c[2 * p + half]
            grad_probs = dot_t(pick_half(up_pair, half), value_pair)
            inner = jnp.sum(probs * grad_probs, axis=-1, keepdims=True)
            grad_scores = (probs * (grad_probs - inner)).astype(BF16)
            d_q.append(dot(grad_scores, key_pair))
            d_k.append(t_dot(grad_scores, query_pair))
            d_v.append(t_dot(probs.astype(BF16), up_pair))
        gqc[:, at] = (join_halves(*d_q) * HEAD ** (-0.5)).astype(BF16)
        gkvc[:, at] = (join_halves(*d_k) * HEAD ** (-0.5)).astype(BF16)
        gkvc[:, value_at] = join_halves(*d_v).astype(BF16)

    text_part[...] = dot_t(gkvc[...], ckv_v[...]).astype(BF16)
    up_two = dot_t(gqc[...], cq_v[...])
    early[4:5, :] = col_sum(up_two * normed_1)
    grad_x1 = acc_m[...] + norm_back(normed_1, inverse_1, up_two * gain)
    early[0:1, :] = col_sum(grad_x1 * gx1[...])
    early[11:16, :] = jnp.zeros((5, model), F32)
    gx1[...] = grad_x1
    ga[...] = (row(2) * grad_x1).astype(BF16)
    gattn[...] = dot_t(ga[...], out_v[...]).astype(BF16)
    for copy in (to_x, to_y, fwd_x, fwd_y):
        copy.wait_send()


def frames_f32(block):
    return block.astype(F32)


GELU_SCALE = 0.7978845608028654


def backward_kernel(
    act, gm_t, h3, gpre, h2, cross, gqc, gc, gkvc, attn, ga, mods, text_part, early, text,
    seg_s, seg, gattn_h, gx1_h, query_h, kv_h, h_all_h, lse_h, frames_h, w_qkv_h,
    out, d_frames, d_text, e_all, l_all,
    G, R0, R1, R2, R3, R4, dqkv, up_low, T, late,
    gattn, gx1, query, kv, h_all, lse, frames, w_qkv, local,
    s0, r0, s1, r1, s2, r2, s3, r3, s4, r4, se, re, sl, rl, st, rt, free,
):
    seq = lax.axis_index("seq")
    rows = lax.axis_index("rows")
    y, x = seq // 2, seq % 2
    z, c = rows // 2, rows % 2
    core_peer = {"rows": z * 2 + (1 - c)}
    x_id, y_id, d_id = y * 2 + 1 - x, (1 - y) * 2 + x, (1 - y) * 2 + 1 - x
    x_peer, y_peer, d_peer = {"seq": x_id}, {"seq": y_id}, {"seq": d_id}
    z_peers = [{"rows": lax.rem(z + d, 4) * 2 + c} for d in (1, 2, 3)]
    loads = [
        pltpu.make_async_copy(src, dst, local.at[i])
        for i, (src, dst) in enumerate(
            [
                (query_h, query), (kv_h, kv), (gattn_h, gattn), (lse_h, lse),
                (w_qkv_h, w_qkv), (h_all_h, h_all), (gx1_h, gx1), (frames_h.at[0], frames),
            ]
        )
    ]
    for load in loads:
        load.start()
    enter([core_peer, x_peer, y_peer, d_peer] + z_peers)

    tall, width = G.shape[-2:]
    here, model = frames.shape
    mask = seg[...] == seg_s[0, seq * here]

    def gather_copies(table, send, recv):
        mine = table.at[c, z, y, x]
        pair = table.at[c, z, y]
        plane = table.at[c, z]
        return (
            [remote(mine, mine, send.at[0], recv.at[0], x_peer)],
            [remote(pair, pair, send.at[1], recv.at[1], y_peer)],
            [
                remote(plane, plane, send.at[1 + d], recv.at[1 + d], z_peers[d - 1])
                for d in (1, 2, 3)
            ],
            [remote(table.at[c], table.at[c], send.at[5], recv.at[5], core_peer)],
        )

    early_steps = gather_copies(e_all, se, re)
    late_steps = gather_copies(l_all, sl, rl)
    text_steps = (
        [remote(T.at[y, x], T.at[y, x], st.at[0], rt.at[0], x_peer)],
        [remote(T.at[y], T.at[y], st.at[1], rt.at[1], y_peer)],
    )

    def advance(steps, at):
        if at:
            for copy in steps[at - 1]:
                copy.wait_recv()
        if at < len(steps):
            for copy in steps[at]:
                copy.start()

    def put(k, s, block):
        low = block.astype(BF16)
        for zz in range(4):
            for cc in range(2):
                at = (zz * 2 + cc) * tall
                G[k, cc, zz, s // 2, s % 2] = low[at : at + tall]

    def put_lanes(k, s, lane, block):
        low = block.astype(BF16)
        for zz in range(4):
            for cc in range(2):
                at = (zz * 2 + cc) * tall
                G[k, cc, zz, s // 2, s % 2, :, lane : lane + 128] = low[at : at + tall]

    def shared(s, first_left, first, second_left, second):
        parity = s % 2
        half_of = (~low_half(first.shape)).astype(jnp.int32)
        first = jnp.where(half_of == parity, first, jnp.zeros_like(first))
        turned = pltpu.roll(second.astype(F32), HEAD, 1)
        half_of = (~low_half(turned.shape)).astype(jnp.int32)
        turned = jnp.where(half_of == parity, 0.0, turned).astype(BF16)
        return t_dot(first_left, first) + t_dot(second_left, turned)

    def compute(k):
        @pl.loop(0, 4)
        def _(s):
            full = s + (s + 1) // 2
            split = 1 + 3 * (s // 2)
            wide = 4 * s + (s + 1) // 2
            if k < 2:
                left = gm_t[pl.ds(pl.multiple_of(s * 2 * tall + k * tall, 16), tall), :]
                for r in range(8):
                    G[k, r % 2, r // 2, s // 2, s % 2] = dot(
                        left, act[:, r * width : (r + 1) * width]
                    ).astype(BF16)
            elif k < 4:
                put(k, s, t_dot(h3[...], gpre[:, lanes(s * 6 + (k - 2) * 3, 3)]))
            elif k == 4:
                put_lanes(k, s, 0, t_dot(h2[...], gqc[:, lanes(full)]))
                put_lanes(k, s, 128, t_dot(cross[...], gc[:, lanes(full)]))
                put_lanes(
                    k, s, 256,
                    shared(s, h2[...], gqc[:, lanes(split)], cross[...], gc[:, lanes(split)]),
                )
            elif k == 5:
                put(k, s, t_dot(text[...], gkvc[:, lanes(s * 3, 3)]))
            elif k == 6:
                put(k, s, t_dot(h_all[...], dqkv[:, lanes(wide, 3)]))
            else:
                put_lanes(k, s, 0, t_dot(h_all[...], dqkv[:, lanes(wide + 3)]))
                put_lanes(
                    k, s, 128,
                    shared(
                        s, h_all[...], dqkv[:, lanes(4 + 9 * (s // 2))],
                        attn[...], ga[:, lanes(split)],
                    ),
                )
                put_lanes(k, s, 256, t_dot(attn[...], ga[:, lanes(full)]))

    def core_copy(k):
        slot = k % 2
        return remote(G.at[k, 1 - c], R0.at[slot], s0.at[k], r0.at[k], core_peer)

    def first_copies(k):
        return (
            remote(G.at[k, c, 0:2, :, 1 - x], R1.at[k, 0], s1.at[k, 0], r1.at[k, 0], x_peer),
            remote(G.at[k, c, 2:4, 1 - y], R1.at[k, 1], s1.at[k, 1], r1.at[k, 1], y_peer),
        )

    def second_copies(k):
        return (
            remote(G.at[k, c, 0:2, 1 - y, x], R2.at[k, 0], s2.at[k, 0], r2.at[k, 0], y_peer),
            remote(G.at[k, c, 2:4, y, 1 - x], R2.at[k, 1], s2.at[k, 1], r2.at[k, 1], x_peer),
        )

    def z_copies(k):
        return [
            remote(
                G.at[k, c, lax.rem(z + d, 4), y, x], R3.at[k, d - 1],
                s3.at[k, d - 1], r3.at[k, d - 1], z_peers[d - 1],
            )
            for d in (1, 2, 3)
        ]

    def add(one, two):
        return (one.astype(F32) + two.astype(F32)).astype(BF16)

    def phase0(k):
        compute(k)
        if k >= 2:
            pl.semaphore_wait(free, 1)
        core_copy(k).start()

    def phase1(k):
        core_copy(k).wait_recv()

        @pl.loop(0, 4)
        def _(zz):
            for yy in range(2):
                for xx in range(2):
                    G[k, c, zz, yy, xx] = add(G[k, c, zz, yy, xx], R0[k % 2, zz, yy, xx])

        if k < CHUNKS - 2:
            pl.semaphore_signal(free, inc=1, device_id=core_peer, device_id_type=MESH)
        for copy in first_copies(k):
            copy.start()

    def phase2(k):
        for copy in first_copies(k):
            copy.wait_recv()
        for zz in range(2):
            for other in range(2):
                G[k, c, zz, other, x] = add(G[k, c, zz, other, x], R1[k, 0, zz, other])
                G[k, c, 2 + zz, y, other] = add(G[k, c, 2 + zz, y, other], R1[k, 1, zz, other])
        for copy in second_copies(k):
            copy.start()

    def phase3(k):
        for copy in second_copies(k):
            copy.wait_recv()
        for zz in range(2):
            G[k, c, zz, y, x] = add(G[k, c, zz, y, x], R2[k, 0, zz])
            G[k, c, 2 + zz, y, x] = add(G[k, c, 2 + zz, y, x], R2[k, 1, zz])
        for copy in z_copies(k):
            copy.start()

    def phase4(k):
        for copy in z_copies(k):
            copy.wait_recv()
        total = G[k, c, z, y, x].astype(F32)
        for d in range(3):
            total = total + R3[k, d].astype(F32)
        out[k] = total

    e_all[c, z, y, x] = early[...].astype(BF16)
    T[y, x] = text_part[: T.shape[2], :]
    phase0(0)
    advance(early_steps, 0)
    advance(text_steps, 0)
    phase0(1)
    phase1(0)
    phase0(2)
    phase1(1)
    advance(early_steps, 1)
    advance(text_steps, 1)
    phase0(3)
    phase1(2)
    phase0(4)
    phase1(3)
    advance(early_steps, 2)
    phase0(5)
    phase1(4)
    phase1(5)

    own = pl.ds(pl.multiple_of(seq * here, here), here)
    dqkv[:, :model] = jnp.zeros((dqkv.shape[0], model), BF16)
    lane_of = lax.broadcasted_iota(jnp.int32, lse.shape, 1)
    for load in loads:
        load.wait()

    @pl.loop(0, HEADS // 2)
    def _(p):
        at = lanes(p)
        key_at = lanes(p + HEADS // 2)
        value_at = lanes(p + HEADS)
        key_pair, value_pair = kv[:, at], kv[:, key_at]
        query_pair, up_pair = query[:, at], gattn[:, at]
        scaled = query_pair * jnp.asarray(HEAD ** (-0.5), BF16)
        d_q, d_k, d_v = [], [], []
        for half in range(2):
            scores = dot_t(pick_half(scaled, half), key_pair)
            log_total = jnp.sum(
                jnp.where(lane_of == 2 * p + half, lse[...], 0.0), axis=-1, keepdims=True
            )
            scores = jnp.where(mask, scores, NEG_FILL)
            probs = jnp.exp(scores - log_total)
            grad_probs = dot_t(pick_half(up_pair, half), value_pair)
            inner = jnp.sum(probs * grad_probs, axis=-1, keepdims=True)
            grad_scores = (probs * (grad_probs - inner)).astype(BF16)
            d_q.append(dot(grad_scores, key_pair))
            d_k.append(t_dot(grad_scores, query_pair))
            d_v.append(t_dot(probs.astype(BF16), up_pair))
        dqkv[own, at] = (join_halves(*d_q) * HEAD ** (-0.5)).astype(BF16)
        dqkv[:, key_at] = (join_halves(*d_k) * HEAD ** (-0.5)).astype(BF16)
        dqkv[:, value_at] = join_halves(*d_v).astype(BF16)

    def up_block(block):
        rows_at = pl.ds(pl.multiple_of(block * here, here), here)
        return dot_t(dqkv[rows_at, model:], w_qkv[:, model:])

    up_copies = []
    for i, (block, peer) in enumerate(((d_id, d_peer), (x_id, x_peer), (y_id, y_peer))):
        up_low[i] = up_block(block).astype(BF16)
        copy = remote(up_low.at[i], R4.at[i], s4.at[i], r4.at[i], peer)
        copy.start()
        up_copies.append(copy)
    phase0(6)
    phase2(0)
    phase0(7)
    phase2(1)
    phase1(6)
    phase3(0)
    phase2(2)
    phase1(7)
    phase3(1)
    advance(early_steps, 3)
    advance(text_steps, 2)

    @pl.loop(3, 6)
    def _(k):
        phase2(k)
        phase3(k - 1)

    for copy in up_copies:
        copy.wait_recv()
    up_one = dot_t(dqkv[own, :], w_qkv[...])
    for i in range(3):
        up_one = up_one + R4[i].astype(F32)
    normed, inverse = norm_parts(frames[...].astype(F32))
    for i, total in enumerate((col_sum(up_one), col_sum(up_one * normed))):
        for j in range(model // 128):
            at = i * (model // 128) + j
            late[at : at + 1, :] = total[:, j * 128 : (j + 1) * 128]
    late[2 * (model // 128) :, :] = jnp.zeros((16 - 2 * (model // 128), 128), F32)
    d_frames[...] = gx1[...] + norm_back(normed, inverse, up_one * (1.0 + mods[1:2, :]))
    l_all[c, z, y, x] = late[...].astype(BF16)
    advance(late_steps, 0)
    total = jnp.zeros(d_text.shape, F32)
    for i in range(4):
        total = total + T[i // 2, i % 2].astype(F32) * jnp.where(
            seg_s[0, i * here] == seq, 1.0, 0.0
        )
    d_text[...] = total
    phase2(6)
    phase3(5)
    advance(late_steps, 1)
    phase2(7)
    phase3(6)
    advance(late_steps, 2)
    phase3(7)
    advance(late_steps, 3)

    @pl.loop(0, CHUNKS)
    def _(k):
        phase4(k)

    advance(early_steps, 4)
    advance(late_steps, 4)

    @pl.loop(0, CHUNKS)
    def _(k):
        core_copy(k).wait_send()
        for copy in (*first_copies(k), *second_copies(k), *z_copies(k)):
            copy.wait_send()

    for copy in up_copies:
        copy.wait_send()
    for steps in (early_steps, late_steps, text_steps):
        for step in steps:
            for copy in step:
                copy.wait_send()


def in_vmem(count):
    return [pl.BlockSpec(memory_space=pltpu.VMEM)] * count


def in_any(count):
    return [pl.BlockSpec(memory_space=pl.ANY)] * count


def finish_kernel(
    done, d_frames_in, d_text_in, output_in, e_all, l_all, step, seg_s, w_ada,
    output, d_frames, d_text, d_step, d_w_ada, d_b_ada, d_w_qkv, d_w_out, d_g_cross,
    d_w_cq, d_w_ckv, d_w_co, d_w_up, d_b_up, d_w_down, d_b_down,
    item, ada, ada_t,
):
    seq = lax.axis_index("seq")
    rows = lax.axis_index("rows")
    here, model = output_in.shape
    parts = model // 128
    output[0] = output_in[...]
    d_frames[0] = d_frames_in[...]
    d_text[0] = d_text_in[: d_text.shape[1], :]
    bias_sum = jnp.zeros((16, model), F32)
    for r in range(8):
        for s in range(4):
            entry = e_all[r % 2, r // 2, s // 2, s % 2].astype(F32)
            tail = l_all[r % 2, r // 2, s // 2, s % 2].astype(F32)
            bias_sum = bias_sum + entry
            at = slice(r * 4 + s, r * 4 + s + 1)
            ada[at, :] = entry[10:11]
            for j in range(4):
                item[at, (2 + j) * model : (3 + j) * model] = entry[j : j + 1]
            for j in range(2 * parts):
                item[at, j * 128 : (j + 1) * 128] = tail[j : j + 1]
    item_sum = jnp.sum(item[...], axis=0, keepdims=True)

    def share(pieces):
        total = jnp.zeros_like(pieces[0])
        for r, piece in enumerate(pieces):
            total = total + jnp.where(rows == r, piece, jnp.zeros_like(piece))
        return total

    def cut(row, size):
        return [row[:, at * size : (at + 1) * size] for at in range(row.shape[1] // size)]

    d_b_ada[...] = share(cut(item_sum, 6 * model // 8)).reshape(6 * model // 8)
    d_g_cross[...] = share(cut(bias_sum[4:5], model // 8)).reshape(model // 8)
    d_b_down[...] = share(cut(bias_sum[9:10], model // 8)).reshape(model // 8)
    d_b_up[...] = share(
        [piece for at in range(5, 9) for piece in cut(bias_sum[at : at + 1], model // 2)]
    ).reshape(model // 2)
    ada_t[...] = ada[...].T
    tall = model // 8
    share_at = pl.ds(pl.multiple_of(seq * 9 * 128, 128), 9 * 128)
    d_w_ada[...] = jnp.dot(
        ada_t[pl.ds(pl.multiple_of(rows * tall, 8), tall), :],
        item[:, share_at],
        precision=PRECISE,
        preferred_element_type=F32,
    )
    near = item[pl.ds(pl.multiple_of(rows // 2 * 8, 8), 8), :]
    total = jnp.zeros((1, 6 * model), F32)
    for j in range(8):
        wanted = jnp.where(seg_s[0, j % 4 * here] == seq, 1.0, 0.0)
        wanted = jnp.where(rows % 2 == j // 4, wanted, 0.0)
        total = total + near[j : j + 1] * wanted
    high = total.astype(BF16)
    low = (total - high.astype(F32)).astype(BF16)
    both = jnp.concatenate(
        [high.astype(F32), low.astype(F32), jnp.zeros((6, 6 * model), F32)], axis=0
    ).astype(BF16)
    d_ada = jnp.sum(dot_t(both, w_ada[...]), axis=0, keepdims=True)
    all_steps = step[0].astype(F32)
    my_step = jnp.zeros((1, model), F32)
    for j in range(4):
        my_step = my_step + all_steps[j : j + 1] * jnp.where(seq == j, 1.0, 0.0)
    gate = 1.0 / (1.0 + jnp.exp(-my_step))
    d_step[0] = d_ada * gate * (1.0 + my_step * (1.0 - gate))
    odd = seq % 2 == 1

    def place(full, mixed, first):
        even = mixed[:, :HEAD] if first else mixed[:, HEAD:]
        other = mixed[:, HEAD:] if first else mixed[:, :HEAD]
        return jnp.where(
            odd,
            jnp.concatenate([other, full], axis=1),
            jnp.concatenate([full, even], axis=1),
        )

    width = model // 2
    d_w_down[...] = jnp.concatenate([done[0], done[1]], axis=0).T
    d_w_up[:, :width] = done[2]
    d_w_up[:, width:] = done[3]
    cross, last = done[4], done[7]
    d_w_cq[...] = place(cross[:, :128], cross[:, 256:], True)
    d_w_co[...] = place(cross[:, 128:256], cross[:, 256:], False)
    d_w_ckv[...] = done[5]
    d_w_qkv[...] = place(
        jnp.concatenate([done[6], last[:, :128]], axis=1), last[:, 128:256], True
    )
    d_w_out[...] = place(last[:, 256:], last[:, 128:256], False)


def smem(count):
    return [pl.BlockSpec(memory_space=pltpu.SMEM)] * count


def per_device(
    frames, text_tokens, step_embed, segments, cotangent,
    w_ada, b_ada, w_qkv, w_out, g_cross, w_cq, w_ckv, w_co, w_up, b_up, w_down, b_down,
):
    seq_count = lax.axis_size("seq")
    rows_count = lax.axis_size("rows")
    here, model = frames.shape[1:]
    length = segments.shape[1]
    hidden = w_up.shape[1]
    assert (length // ITEMS) % here == 0
    text_rows, text_kept, step_rows = 128, 80, 16

    def like(shape, dtype=BF16):
        return jax.ShapeDtypeStruct(shape, dtype)

    square = like((here, model))
    dma = pltpu.SemaphoreType.DMA
    vmem = pltpu.VMEM
    (
        output, act, gm_t, h3, gpre, h2, cross, gqc, gc, gkvc, attn, ga, gattn, gx1, query,
        kv, h_all, lse, mods, text_part, early, text_mine,
    ) = pl.pallas_call(
        forward_kernel,
        out_shape=(
            square, like((here, hidden)), like((model, here)), square, like((here, hidden)),
            square, square, square, square, like((text_rows, 2 * model)), square, square,
            square, like((here, model), F32), square, like((length, 2 * model)),
            like((length, model)), like((here, 128), F32), like((8, model), F32),
            like((text_rows, model)), like((16, model), F32), like((text_rows, model)),
        ),
        in_specs=in_any(1) + in_vmem(3) + smem(1) + in_vmem(1)
        + in_any(1) + in_vmem(1) + in_any(2) + in_vmem(1) + in_any(4) + in_vmem(1)
        + in_any(1) + in_vmem(1),
        out_specs=tuple(in_vmem(22)),
        scratch_shapes=[
            vmem((seq_count, here, model), BF16),
            vmem(w_ada.shape, BF16), vmem(w_qkv.shape, BF16), vmem(w_out.shape, BF16),
            vmem(w_cq.shape, BF16), vmem(w_ckv.shape, BF16), vmem(w_co.shape, BF16),
            vmem(w_up.shape, BF16), vmem(w_down.shape, BF16),
            vmem((HEADS, here, text_rows), F32),
            vmem((here, model), F32), vmem((here, model), F32),
            vmem((step_rows, 6 * model), F32),
            vmem((1, hidden), F32),
            dma((9,)), dma((4,)), dma((4,)),
        ],
        compiler_params=pltpu.CompilerParams(
            collective_id=0, has_side_effects=True, vmem_limit_bytes=VMEM_MOST
        ),
        name="forward_layer",
    )(
        frames, cotangent, text_tokens, step_embed, segments, segments,
        w_ada, b_ada, w_qkv, w_out, g_cross, w_cq, w_ckv, w_co, w_up, b_up, w_down, b_down,
    )

    tall, width = model // rows_count, model // 2
    table = (2, 4, 2, 2)
    done, d_frames, d_text, e_all, l_all = pl.pallas_call(
        backward_kernel,
        out_shape=(
            like((CHUNKS, tall, width), F32), like((here, model), F32),
            like((text_kept, model), F32), like(table + (16, model)),
            like(table + (16, 128)),
        ),
        in_specs=in_vmem(15) + smem(1) + in_vmem(1) + in_any(8),
        out_specs=tuple(in_vmem(5)),
        scratch_shapes=[
            vmem((CHUNKS,) + table + (tall, width), BF16),
            vmem((2, 4, 2, 2, tall, width), BF16),
            vmem((CHUNKS, 2, 2, 2, tall, width), BF16),
            vmem((CHUNKS, 2, 2, tall, width), BF16),
            vmem((CHUNKS, 3, tall, width), BF16),
            vmem((3, here, model), BF16),
            vmem((length, 3 * model), BF16),
            vmem((3, here, model), BF16),
            vmem((2, 2, text_kept, model), BF16),
            vmem((16, 128), F32),
            vmem((here, model), BF16), vmem((here, model), F32), vmem((here, model), BF16),
            vmem((length, 2 * model), BF16), vmem((length, model), BF16),
            vmem((here, 128), F32), vmem((here, model), BF16), vmem(w_qkv.shape, BF16),
            dma((8,)),
            dma((CHUNKS,)), dma((CHUNKS,)),
            dma((CHUNKS, 2)), dma((CHUNKS, 2)),
            dma((CHUNKS, 2)), dma((CHUNKS, 2)),
            dma((CHUNKS, 3)), dma((CHUNKS, 3)),
            dma((3,)), dma((3,)), dma((6,)), dma((6,)), dma((6,)), dma((6,)),
            dma((2,)), dma((2,)), pltpu.SemaphoreType.REGULAR,
        ],
        compiler_params=pltpu.CompilerParams(
            collective_id=1, has_side_effects=True, vmem_limit_bytes=VMEM_MOST
        ),
        name="backward_layer",
    )(
        act, gm_t, h3, gpre, h2, cross, gqc, gc, gkvc, attn, ga, mods, text_part, early,
        text_mine, segments, segments, gattn, gx1, query, kv, h_all, lse, frames, w_qkv,
    )

    def shard(*shape):
        return like(shape, F32)

    seq_share = model // seq_count
    return pl.pallas_call(
        finish_kernel,
        out_shape=(
            like((1, here, model)), shard(1, here, model), shard(1, TXT, model),
            shard(1, 1, model), shard(tall, 6 * seq_share), shard(6 * tall),
            shard(tall, 3 * seq_share), shard(tall, seq_share), shard(tall),
            shard(tall, seq_share), shard(tall, 2 * seq_share), shard(tall, seq_share),
            shard(tall, hidden // seq_count), shard(hidden // rows_count),
            shard(hidden // rows_count, seq_share), shard(tall),
        ),
        in_specs=in_vmem(7) + smem(1) + in_vmem(1),
        out_specs=tuple(in_vmem(16)),
        scratch_shapes=[
            vmem((32, 6 * model), F32), vmem((32, model), F32), vmem((model, 32), F32),
        ],
        compiler_params=pltpu.CompilerParams(vmem_limit_bytes=VMEM_MOST),
        name="finish_layer",
    )(done, d_frames, d_text, output, e_all, l_all, step_embed, segments, w_ada)


def solution(mesh):
    row_seq = P("rows", "seq", None)
    in_specs = (
        row_seq, P("rows", None, None), P("rows", None, None), P("rows", None), row_seq,
    ) + (P(),) * 12
    out_specs = (row_seq,) * 4 + (
        P("rows", "seq"), P("rows"), P("rows", "seq"), P("rows", "seq"), P("rows"),
        P("rows", "seq"), P("rows", "seq"), P("rows", "seq"), P("rows", "seq"), P("rows"),
        P("rows", "seq"), P("rows"),
    )
    fused = mesh.shape["rows"] == 8 and mesh.shape["seq"] == 4
    return jax.shard_map(
        per_device if fused else per_device_plain, mesh=mesh, in_specs=in_specs, out_specs=out_specs, check_vma=False
    )
```

```python
import functools

import jax
import jax.numpy as jnp
from jax import lax
from jax.experimental import pallas as pl
from jax.experimental.pallas import tpu as pltpu
from jax.sharding import PartitionSpec as P

HEADS = 12
HEAD = 64
TXT = 77
ITEMS = 4

EPSILON = 1e-06
NEG_FILL = -1e30
PRECISE = lax.Precision.HIGHEST
F32 = jnp.float32
BF16 = jnp.bfloat16
MESH = pl.DeviceIdType.MESH
CHUNKS = 8
VMEM_MOST = 67_043_328


def dot(left, right):
    return jnp.dot(left, right, preferred_element_type=F32)


def dot_t(left, right):
    return lax.dot_general(left, right, (((1,), (1,)), ((), ())), preferred_element_type=F32)


def t_dot(left, right):
    return lax.dot_general(left, right, (((0,), (0,)), ((), ())), preferred_element_type=F32)


def norm_parts(values):
    center = values - jnp.mean(values, axis=-1, keepdims=True)
    inverse = lax.rsqrt(jnp.mean(center * center, axis=-1, keepdims=True) + EPSILON)
    return center * inverse, inverse


def norm_back(normed, inverse, upstream):
    return inverse * (
        upstream
        - jnp.mean(upstream, axis=-1, keepdims=True)
        - normed * jnp.mean(upstream * normed, axis=-1, keepdims=True)
    )


def gelu_tanh(values):
    return jax.nn.gelu(values, approximate=True)


def split_heads(matrix):
    return matrix.reshape(matrix.shape[0], HEADS, HEAD)


def scores_of(queries, keyset, allowed):
    raw = jnp.einsum(
        "qhd,khd->hqk", split_heads(queries), split_heads(keyset), preferred_element_type=F32
    )
    raw = raw * HEAD ** (-0.5)
    return raw if allowed is None else jnp.where(allowed[None, None, :], raw, NEG_FILL)


def attend_forward(queries, keyset, valueset, allowed):
    scores = scores_of(queries, keyset, allowed)
    top_score = jnp.max(scores, axis=-1, keepdims=True)
    exp_scores = jnp.exp(scores - top_score)
    totals = jnp.sum(exp_scores, axis=-1, keepdims=True)
    probs_low = (exp_scores / totals).astype(BF16)
    mixed = jnp.einsum(
        "hqk,khd->qhd", probs_low, split_heads(valueset), preferred_element_type=F32
    )
    return mixed.reshape(queries.shape).astype(BF16), top_score + jnp.log(totals)


def attend_backward(queries, keyset, valueset, allowed, log_total, upstream):
    probs = jnp.exp(scores_of(queries, keyset, allowed) - log_total)
    up_heads = split_heads(upstream)
    grad_probs = jnp.einsum(
        "qhd,khd->hqk", up_heads, split_heads(valueset), preferred_element_type=F32
    )
    inner = jnp.sum(probs * grad_probs, axis=-1, keepdims=True)
    grad_scores = (probs * (grad_probs - inner)).astype(BF16)
    grad_query = jnp.einsum(
        "hqk,khd->qhd", grad_scores, split_heads(keyset), preferred_element_type=F32
    )
    grad_key = jnp.einsum(
        "hqk,qhd->khd", grad_scores, split_heads(queries), preferred_element_type=F32
    )
    grad_value = jnp.einsum(
        "hqk,qhd->khd", probs.astype(BF16), up_heads, preferred_element_type=F32
    )
    return (
        (grad_query.reshape(queries.shape) * HEAD ** (-0.5)).astype(BF16),
        (grad_key.reshape(keyset.shape) * HEAD ** (-0.5)).astype(BF16),
        grad_value.reshape(valueset.shape).astype(BF16),
    )


def scatter_plain(matrix):
    part = lax.psum_scatter(matrix.astype(BF16), "rows", scatter_dimension=0, tiled=True)
    part = lax.psum_scatter(part, "seq", scatter_dimension=1, tiled=True)
    return part.astype(F32)


def per_device_plain(
    frames, text_tokens, step_embed, segments, cotangent,
    w_ada, b_ada, w_qkv, w_out, g_cross, w_cq, w_ckv, w_co, w_up, b_up, w_down, b_down,
):
    seq_count = lax.axis_size("seq")
    rows_count = lax.axis_size("rows")
    seq_index = lax.axis_index("seq")
    rows_index = lax.axis_index("rows")
    frames, text_tokens, step_embed = frames[0], text_tokens[0], step_embed[0]
    segments, cotangent = segments[0], cotangent[0]
    here, model = frames.shape
    length = segments.shape[0]
    assert (length // ITEMS) % here == 0
    block_slots = segments[::here]
    slot = lax.dynamic_index_in_dim(block_slots, seq_index, 0, keepdims=False)
    allowed = segments == slot
    text_mine = lax.dynamic_slice_in_dim(text_tokens, slot * TXT, TXT, axis=0)

    frames_all = lax.all_gather(frames, "seq", axis=0, tiled=True)
    ada_in = jax.nn.silu(step_embed.astype(F32)).astype(BF16)
    item_mod = dot(ada_in, w_ada) + b_ada.astype(F32)
    mine = lax.dynamic_slice_in_dim(item_mod, slot, 1, axis=0)
    shift_a, scale_a, gate_a, shift_b, scale_b, gate_b = jnp.split(mine, 6, axis=-1)

    normed_all, inverse_all = norm_parts(frames_all.astype(F32))
    hot = (block_slots[:, None] == jnp.arange(ITEMS)[None, :]).astype(F32)
    block_mod = jnp.dot(hot, item_mod[:, : 2 * model], precision=PRECISE)
    frame_mod = jnp.repeat(block_mod, here, axis=0)
    h_all = (normed_all * (1.0 + frame_mod[:, model:]) + frame_mod[:, :model]).astype(BF16)
    frames_f32 = frames.astype(F32)
    normed_0, inverse_0 = norm_parts(frames_f32)
    h_one = (normed_0 * (1.0 + scale_a) + shift_a).astype(BF16)
    query_a = dot(h_one, w_qkv[:, :model]).astype(BF16)
    kv_all = dot(h_all, w_qkv[:, model:]).astype(BF16)
    key_all, value_all = kv_all[:, :model], kv_all[:, model:]
    attn_low, lse_self = attend_forward(query_a, key_all, value_all, allowed)
    branch_a = dot(attn_low, w_out)
    x_one = frames_f32 + gate_a * branch_a
    gain = g_cross.astype(F32)[None]
    normed_1, inverse_1 = norm_parts(x_one)
    h_two = (normed_1 * gain).astype(BF16)
    query_c = dot(h_two, w_cq).astype(BF16)
    text_kv = dot(text_mine, w_ckv).astype(BF16)
    key_c, value_c = text_kv[:, :model], text_kv[:, model:]
    cross_low, lse_cross = attend_forward(query_c, key_c, value_c, None)
    x_two = x_one + dot(cross_low, w_co)
    normed_2, inverse_2 = norm_parts(x_two)
    h_three = (normed_2 * (1.0 + scale_b) + shift_b).astype(BF16)
    pre_act = dot(h_three, w_up) + b_up.astype(F32)
    act_low = gelu_tanh(pre_act).astype(BF16)
    branch_m = dot(act_low, w_down) + b_down.astype(F32)
    output = (x_two + gate_b * branch_m).astype(BF16)

    grad_out = cotangent.astype(F32)
    grad_m = (gate_b * grad_out).astype(BF16)
    grad_act = dot_t(grad_m, w_down)
    unused_act, gelu_back = jax.vjp(gelu_tanh, pre_act)
    grad_pre = gelu_back(grad_act)[0].astype(BF16)
    up_three = dot_t(grad_pre, w_up)
    grad_x2 = grad_out + norm_back(normed_2, inverse_2, up_three * (1.0 + scale_b))
    grad_c = grad_x2.astype(BF16)
    grad_cross = dot_t(grad_c, w_co).astype(BF16)
    grad_qc, grad_kc, grad_vc = attend_backward(
        query_c, key_c, value_c, None, lse_cross, grad_cross
    )
    grad_kvc = jnp.concatenate([grad_kc, grad_vc], axis=-1)
    up_two = dot_t(grad_qc, w_cq)
    grad_x1 = grad_x2 + norm_back(normed_1, inverse_1, up_two * gain)
    grad_a = (gate_a * grad_x1).astype(BF16)
    grad_attn = dot_t(grad_a, w_out).astype(BF16)
    grad_qa, grad_ka, grad_va = attend_backward(
        query_a, key_all, value_all, allowed, lse_self, grad_attn
    )
    grad_kva = jnp.concatenate([grad_ka, grad_va], axis=-1)
    up_kv = dot_t(grad_kva, w_qkv[:, model:]).astype(BF16)
    up_one = dot_t(grad_qa, w_qkv[:, :model]) + lax.psum_scatter(
        up_kv, "seq", scatter_dimension=0, tiled=True
    ).astype(F32)
    d_frames = grad_x1 + norm_back(normed_0, inverse_0, up_one * (1.0 + scale_a))

    small = jnp.concatenate(
        [
            jnp.sum(up_one, axis=0),
            jnp.sum(up_one * normed_0, axis=0),
            jnp.sum(grad_x1 * branch_a, axis=0),
            jnp.sum(up_three, axis=0),
            jnp.sum(up_three * normed_2, axis=0),
            jnp.sum(grad_out * branch_m, axis=0),
            jnp.sum(up_two * normed_1, axis=0),
            jnp.sum(grad_pre.astype(F32), axis=0),
            jnp.sum(grad_m.astype(F32), axis=0),
            lax.dynamic_index_in_dim(ada_in, slot, 0, keepdims=False).astype(F32),
        ]
    )
    small_all = lax.all_gather(small, ("rows", "seq"), axis=0, tiled=False)
    small_all = small_all.reshape(rows_count * seq_count, -1)
    item_all = small_all[:, : 6 * model]
    bias_all = small_all[:, 6 * model : -model]
    ada_all = small_all[:, -model:]

    def share(table, count, index):
        size = table.shape[-1] // count
        return lax.dynamic_slice_in_dim(table, index * size, size, axis=-1)

    def bias_sum(table):
        return jnp.sum(share(table, rows_count, rows_index), axis=0)

    d_b_ada = bias_sum(item_all)
    d_g_cross = bias_sum(bias_all[:, :model])
    d_b_up = bias_sum(bias_all[:, model:-model])
    d_b_down = bias_sum(bias_all[:, -model:])
    d_w_ada = lax.dot_general(
        share(ada_all, rows_count, rows_index),
        share(item_all, seq_count, seq_index),
        (((0,), (0,)), ((), ())),
        precision=PRECISE,
        preferred_element_type=F32,
    )
    item_share = ITEMS // seq_count
    row_items = lax.dynamic_slice_in_dim(item_all, rows_index * seq_count, seq_count, axis=0)
    owned = seq_index * item_share + jnp.arange(item_share)
    pick = (owned[:, None] == block_slots[None, :]).astype(F32)
    item_mine = jnp.dot(pick, row_items, precision=PRECISE)
    d_ada = lax.dot_general(
        item_mine, w_ada.astype(F32), (((1,), (1,)), ((), ())), precision=PRECISE
    )
    my_step = lax.dynamic_slice_in_dim(
        step_embed, seq_index * item_share, item_share, axis=0
    ).astype(F32)
    unused_step, silu_back = jax.vjp(jax.nn.silu, my_step)
    d_step = silu_back(d_ada)[0]
    text_part = dot_t(grad_kvc, w_ckv).astype(BF16)
    text_full = lax.dynamic_update_slice_in_dim(
        jnp.zeros(text_tokens.shape, BF16), text_part, slot * TXT, axis=0
    )
    d_text = lax.psum_scatter(text_full, "seq", scatter_dimension=0, tiled=True).astype(F32)

    d_w_down = scatter_plain(t_dot(act_low, grad_m))
    d_w_up = scatter_plain(t_dot(h_three, grad_pre))
    d_w_cq = scatter_plain(t_dot(h_two, grad_qc))
    d_w_co = scatter_plain(t_dot(cross_low, grad_c))
    d_w_ckv = scatter_plain(t_dot(text_mine, grad_kvc))
    d_w_out = scatter_plain(t_dot(attn_low, grad_a))
    d_w_qkv = scatter_plain(
        jnp.concatenate([t_dot(h_one, grad_qa), t_dot(h_all, grad_kva)], axis=1)
    )
    return (
        output[None], d_frames[None], d_text[None], d_step[None],
        d_w_ada, d_b_ada, d_w_qkv, d_w_out, d_g_cross, d_w_cq, d_w_ckv, d_w_co,
        d_w_up, d_b_up, d_w_down, d_b_down,
    )


def remote(src, dst, send, recv, peer):
    return pltpu.make_async_remote_copy(
        src_ref=src, dst_ref=dst, send_sem=send, recv_sem=recv,
        device_id=peer, device_id_type=MESH,
    )


def enter(peers):
    barrier = pltpu.get_barrier_semaphore()
    for peer in peers:
        pl.semaphore_signal(barrier, inc=1, device_id=peer, device_id_type=MESH)
    pl.semaphore_wait(barrier, len(peers))


def low_half(shape):
    return lax.broadcasted_iota(jnp.int32, shape, len(shape) - 1) < HEAD


def pick_half(pair, half):
    lower = low_half(pair.shape)
    return jnp.where(lower if half == 0 else ~lower, pair, jnp.zeros_like(pair))


def join_halves(first, second):
    return jnp.where(low_half(first.shape), first, second)


def lanes(index, count=1):
    return pl.ds(pl.multiple_of(index * 128, 128), 128 * count)


def col_sum(values):
    return jnp.sum(values, axis=0, keepdims=True)


def softmax_rows(scores):
    top = jnp.max(scores, axis=-1, keepdims=True)
    raised = jnp.exp(scores - top)
    total = jnp.sum(raised, axis=-1, keepdims=True)
    return raised / total, top + jnp.log(total)


def forward_kernel(
    frames, cot, text, step, seg_s, seg,
    w_ada, b_ada, w_qkv, w_out, g_cross, w_cq, w_ckv, w_co, w_up, b_up, w_down, b_down,
    output, act, gm_t, h3, gpre, h2, cross, gqc, gc, gkvc, attn, ga, gattn, gx1, query,
    kv, h_all, lse, mods, text_part, early, text_mine,
    fr, ada_v, qkv_v, out_v, cq_v, ckv_v, co_v, up_v, down_v, prob_c, acc_m, acc_u,
    item, up_bias, local, send, recv,
):
    seq = lax.axis_index("seq")
    y, x = seq // 2, seq % 2
    x_id, y_id, d_id = y * 2 + 1 - x, (1 - y) * 2 + x, (1 - y) * 2 + 1 - x
    x_peer, y_peer = {"seq": x_id}, {"seq": y_id}
    frames = frames.at[0]
    here, model = frames.shape
    part = here // 2
    slot = seg_s[0, seq * here]
    mask = seg[...] == slot
    loads = [
        pltpu.make_async_copy(src, dst, local.at[i])
        for i, (src, dst) in enumerate(
            [
                (frames, fr.at[seq]), (w_ada, ada_v), (w_qkv, qkv_v), (w_out, out_v),
                (w_ckv, ckv_v), (w_cq, cq_v), (w_co, co_v), (w_up, up_v), (w_down, down_v),
            ]
        )
    ]
    for i in (0, 1):
        loads[i].start()
    enter([x_peer, y_peer])
    to_x = remote(frames, fr.at[seq], send.at[0], recv.at[0], x_peer)
    to_y = remote(frames, fr.at[seq], send.at[1], recv.at[1], y_peer)
    to_x.start()
    to_y.start()
    loads[2].start()
    loads[4].start()

    def row(at):
        return mods[at : at + 1, :]

    step_f32 = jnp.concatenate(
        [step[0].astype(F32), jnp.zeros((item.shape[0] - ITEMS, model), F32)], axis=0
    )
    ada = (step_f32 / (1.0 + jnp.exp(-step_f32))).astype(BF16)
    loads[1].wait()
    item[...] = dot(ada, ada_v[...]) + b_ada[...].astype(F32)[None]
    for i in (3, 5, 6, 7, 8):
        loads[i].start()
    slot_row = lax.broadcasted_iota(jnp.int32, (item.shape[0], model), 0)
    chosen_mine = (slot_row == slot).astype(F32)
    for part_at in range(6):
        mods[part_at : part_at + 1, :] = col_sum(
            item[:, part_at * model : (part_at + 1) * model] * chosen_mine
        )
    early[10:11, :] = col_sum(ada.astype(F32) * chosen_mine)
    up_bias[...] = b_up[...].astype(F32)[None]

    def take(block):
        chosen = (slot_row == seg_s[0, block * here]).astype(F32)
        shift = col_sum(item[:, :model] * chosen)
        scale = col_sum(item[:, model : 2 * model] * chosen)
        normed, unused = norm_parts(fr[block].astype(F32))
        rows_at = pl.ds(pl.multiple_of(block * here, here), here)
        h_block = (normed * (1.0 + scale) + shift).astype(BF16)
        h_all[rows_at, :] = h_block
        kv[rows_at, :] = dot(h_block, qkv_v[:, model:]).astype(BF16)
        return h_block

    loads[0].wait()
    loads[2].wait()
    h_one = take(seq)
    query[...] = dot(h_one, qkv_v[:, :model]).astype(BF16)
    loads[4].wait()
    picked = (text_mine.shape[0], text.shape[1])
    text_at = lax.broadcasted_iota(jnp.int32, picked, 0)
    token = lax.broadcasted_iota(jnp.int32, picked, 1)
    hot = jnp.where((token == text_at + TXT * slot) & (text_at < TXT), 1.0, 0.0).astype(BF16)
    text_mine[...] = dot(hot, text[0]).astype(BF16)
    text_kv = dot(text_mine[...], ckv_v[...]).astype(BF16)
    gkvc[...] = text_kv
    to_x.wait_recv()
    fwd_y = remote(
        fr.at[x_id, pl.ds(0, part)], fr.at[x_id, pl.ds(0, part)], send.at[2], recv.at[2], y_peer
    )
    fwd_y.start()
    to_y.wait_recv()
    fwd_x = remote(
        fr.at[y_id, pl.ds(part, part)], fr.at[y_id, pl.ds(part, part)],
        send.at[3], recv.at[3], x_peer,
    )
    fwd_x.start()
    take(x_id)
    take(y_id)
    fwd_y.wait_recv()
    fwd_x.wait_recv()
    take(d_id)

    lse[...] = jnp.zeros_like(lse)
    lane_of = lax.broadcasted_iota(jnp.int32, lse.shape, 1)

    @pl.loop(0, HEADS // 2)
    def _(p):
        at = lanes(p)
        value_at = lanes(p + HEADS // 2)
        pair = query[:, at] * jnp.asarray(HEAD ** (-0.5), BF16)
        outs = []
        for half in range(2):
            scores = dot_t(pick_half(pair, half), kv[:, at])
            scores = jnp.where(mask, scores, NEG_FILL)
            probs, log_total = softmax_rows(scores)
            lse[...] = jnp.where(lane_of == 2 * p + half, log_total, lse[...])
            outs.append(dot(probs.astype(BF16), kv[:, value_at]))
        attn[:, at] = join_halves(*outs).astype(BF16)

    loads[3].wait()
    branch_a = dot(attn[...], out_v[...])
    x_one = frames_f32(fr[seq]) + row(2) * branch_a
    gx1[...] = branch_a
    gain = g_cross[...].astype(F32)[None]
    normed_1, inverse_1 = norm_parts(x_one)
    h2[...] = (normed_1 * gain).astype(BF16)
    loads[5].wait()
    query_c = dot(h2[...], cq_v[...]).astype(BF16)
    gqc[...] = query_c

    text_rows = text_mine.shape[0]
    key_lane = lax.broadcasted_iota(jnp.int32, (here, text_rows), 1)

    @pl.loop(0, HEADS // 2, unroll=True)
    def _(p):
        at = lanes(p)
        value_at = lanes(p + HEADS // 2)
        pair = gqc[:, at] * jnp.asarray(HEAD ** (-0.5), BF16)
        outs = []
        for half in range(2):
            scores = dot_t(pick_half(pair, half), gkvc[:, at])
            probs, unused = softmax_rows(jnp.where(key_lane < TXT, scores, NEG_FILL))
            prob_c[2 * p + half] = probs
            outs.append(dot(probs.astype(BF16), gkvc[:, value_at]))
        cross[:, at] = join_halves(*outs).astype(BF16)

    loads[6].wait()
    x_two = x_one + dot(cross[...], co_v[...])
    normed_2, inverse_2 = norm_parts(x_two)
    h3[...] = (normed_2 * (1.0 + row(4)) + row(3)).astype(BF16)
    grad_out = cot[0].astype(F32)
    grad_m = row(5) * grad_out
    gm_low = grad_m.astype(BF16)
    gm_t[...] = gm_low.astype(F32).T.astype(BF16)
    early[9:10, :] = col_sum(gm_low.astype(F32))
    gc[...] = gm_low
    acc_m[...] = jnp.zeros_like(acc_m)
    acc_u[...] = jnp.zeros_like(acc_u)
    loads[7].wait()
    loads[8].wait()
    slab = model // 2

    @pl.loop(0, w_up.shape[1] // slab)
    def _(j):
        at = pl.ds(pl.multiple_of(j * slab, slab), slab)
        pre = dot(h3[...], up_v[:, at]) + up_bias[:, at]
        inner = GELU_SCALE * (pre + 0.044715 * pre * pre * pre)
        tanh = jnp.tanh(inner)
        act_low = (0.5 * pre * (1.0 + tanh)).astype(BF16)
        act[:, at] = act_low
        acc_m[...] += dot(act_low, down_v[at, :])
        slope = 0.5 * (1.0 + tanh) + 0.5 * pre * (1.0 - tanh * tanh) * (
            GELU_SCALE * (1.0 + 3.0 * 0.044715 * pre * pre)
        )
        grad_pre = (dot_t(gc[...], down_v[at, :]) * slope).astype(BF16)
        gpre[:, at] = grad_pre
        acc_u[...] += dot_t(grad_pre, up_v[:, at])

    for quarter in range(4):
        at = slice(quarter * model, (quarter + 1) * model)
        early[5 + quarter : 6 + quarter, :] = col_sum(gpre[:, at].astype(F32))
    branch_m = acc_m[...] + b_down[...].astype(F32)[None]
    output[...] = (x_two + row(5) * branch_m).astype(BF16)
    early[3:4, :] = col_sum(grad_out * branch_m)
    up_three = acc_u[...]
    early[1:2, :] = col_sum(up_three)
    early[2:3, :] = col_sum(up_three * normed_2)
    grad_x2 = grad_out + norm_back(normed_2, inverse_2, up_three * (1.0 + row(4)))
    acc_m[...] = grad_x2
    gc[...] = grad_x2.astype(BF16)
    ga[...] = dot_t(gc[...], co_v[...]).astype(BF16)

    @pl.loop(0, HEADS // 2, unroll=True)
    def _(p):
        at = lanes(p)
        value_at = lanes(p + HEADS // 2)
        key_pair, value_pair = gkvc[:, at], gkvc[:, value_at]
        query_pair, up_pair = gqc[:, at], ga[:, at]
        d_q, d_k, d_v = [], [], []
        for half in range(2):
            probs = prob_c[2 * p + half]
            grad_probs = dot_t(pick_half(up_pair, half), value_pair)
            inner = jnp.sum(probs * grad_probs, axis=-1, keepdims=True)
            grad_scores = (probs * (grad_probs - inner)).astype(BF16)
            d_q.append(dot(grad_scores, key_pair))
            d_k.append(t_dot(grad_scores, query_pair))
            d_v.append(t_dot(probs.astype(BF16), up_pair))
        gqc[:, at] = (join_halves(*d_q) * HEAD ** (-0.5)).astype(BF16)
        gkvc[:, at] = (join_halves(*d_k) * HEAD ** (-0.5)).astype(BF16)
        gkvc[:, value_at] = join_halves(*d_v).astype(BF16)

    text_part[...] = dot_t(gkvc[...], ckv_v[...]).astype(BF16)
    up_two = dot_t(gqc[...], cq_v[...])
    early[4:5, :] = col_sum(up_two * normed_1)
    grad_x1 = acc_m[...] + norm_back(normed_1, inverse_1, up_two * gain)
    early[0:1, :] = col_sum(grad_x1 * gx1[...])
    early[11:16, :] = jnp.zeros((5, model), F32)
    gx1[...] = grad_x1
    ga[...] = (row(2) * grad_x1).astype(BF16)
    gattn[...] = dot_t(ga[...], out_v[...]).astype(BF16)
    for copy in (to_x, to_y, fwd_x, fwd_y):
        copy.wait_send()


def frames_f32(block):
    return block.astype(F32)


GELU_SCALE = 0.7978845608028654


ORDER = (2, 0, 3, 1, 4, 5, 6, 7)
DEEP = (0, 1)


def backward_kernel(
    act, gm_t, h3, gpre, h2, cross, gqc, gc, gkvc, attn, ga, mods, text_part, early, text,
    seg_s, seg, gattn_h, gx1_h, query_h, kv_h, h_all_h, lse_h, frames_h, w_qkv_h,
    out, d_frames, d_text, e_all, l_all,
    G, R0, R1, R2, R3, R4, dqkv, up_low, T, late,
    gattn, gx1, query, kv, h_all, lse, frames, w_qkv, local,
    s0, r0, s1, r1, s2, r2, s3, r3, s4, r4, se, re, sl, rl, st, rt, free,
):
    seq = lax.axis_index("seq")
    rows = lax.axis_index("rows")
    y, x = seq // 2, seq % 2
    z, c = rows // 2, rows % 2
    core_peer = {"rows": z * 2 + (1 - c)}
    x_id, y_id = y * 2 + 1 - x, (1 - y) * 2 + x
    x_peer, y_peer = {"seq": x_id}, {"seq": y_id}
    z_peers = [{"rows": lax.rem(z + d, 4) * 2 + c} for d in (1, 2, 3)]
    zh, zl = z // 2, z % 2
    near_peer = {"rows": (zh * 2 + 1 - zl) * 2 + c}
    far_peer = {"rows": ((1 - zh) * 2 + zl) * 2 + c}
    loads = [
        pltpu.make_async_copy(src, dst, local.at[i])
        for i, (src, dst) in enumerate(
            [
                (query_h, query), (kv_h, kv), (gattn_h, gattn), (lse_h, lse),
                (w_qkv_h, w_qkv), (h_all_h, h_all), (gx1_h, gx1), (frames_h.at[0], frames),
            ]
        )
    ]
    for load in loads:
        load.start()
    enter([core_peer, x_peer, y_peer] + z_peers)

    tall, width = G.shape[-2:]
    here, model = frames.shape
    mask = seg[...] == seg_s[0, seq * here]

    def gather_copies(table, send, recv):
        mine = table.at[c, z, y, x]
        pair = table.at[c, z, y]
        plane = table.at[c, z]
        return (
            [remote(mine, mine, send.at[0], recv.at[0], x_peer)],
            [remote(pair, pair, send.at[1], recv.at[1], y_peer)],
            [
                remote(plane, plane, send.at[1 + d], recv.at[1 + d], z_peers[d - 1])
                for d in (1, 2, 3)
            ],
            [remote(table.at[c], table.at[c], send.at[5], recv.at[5], core_peer)],
        )

    early_steps = gather_copies(e_all, se, re)
    late_steps = gather_copies(l_all, sl, rl)
    text_steps = (
        [remote(T.at[y, x], T.at[y, x], st.at[0], rt.at[0], x_peer)],
        [remote(T.at[y], T.at[y], st.at[1], rt.at[1], y_peer)],
    )

    def advance(steps, at):
        if at:
            for copy in steps[at - 1]:
                copy.wait_recv()
        if at < len(steps):
            for copy in steps[at]:
                copy.start()

    def put(k, s, block):
        low = block.astype(BF16)
        for zz in range(4):
            for cc in range(2):
                at = (zz * 2 + cc) * tall
                G[k, cc, zz, s // 2, s % 2] = low[at : at + tall]

    def put_lanes(k, s, lane, block):
        low = block.astype(BF16)
        for zz in range(4):
            for cc in range(2):
                at = (zz * 2 + cc) * tall
                G[k, cc, zz, s // 2, s % 2, :, lane : lane + 128] = low[at : at + tall]

    def shared(s, first_left, first, second_left, second):
        parity = s % 2
        half_of = (~low_half(first.shape)).astype(jnp.int32)
        first = jnp.where(half_of == parity, first, jnp.zeros_like(first))
        turned = pltpu.roll(second.astype(F32), HEAD, 1)
        half_of = (~low_half(turned.shape)).astype(jnp.int32)
        turned = jnp.where(half_of == parity, 0.0, turned).astype(BF16)
        return t_dot(first_left, first) + t_dot(second_left, turned)

    def compute(k):
        @pl.loop(0, 4)
        def _(s):
            full = s + (s + 1) // 2
            split = 1 + 3 * (s // 2)
            wide = 4 * s + (s + 1) // 2
            if k < 2:
                left = gm_t[pl.ds(pl.multiple_of(s * 2 * tall + k * tall, 16), tall), :]
                for r in range(8):
                    G[k, r % 2, r // 2, s // 2, s % 2] = dot(
                        left, act[:, r * width : (r + 1) * width]
                    ).astype(BF16)
            elif k < 4:
                put(k, s, t_dot(h3[...], gpre[:, lanes(s * 6 + (k - 2) * 3, 3)]))
            elif k == 4:
                put_lanes(k, s, 0, t_dot(h2[...], gqc[:, lanes(full)]))
                put_lanes(k, s, 128, t_dot(cross[...], gc[:, lanes(full)]))
                put_lanes(
                    k, s, 256,
                    shared(s, h2[...], gqc[:, lanes(split)], cross[...], gc[:, lanes(split)]),
                )
            elif k == 5:
                put(k, s, t_dot(text[...], gkvc[:, lanes(s * 3, 3)]))
            elif k == 6:
                put(k, s, t_dot(h_all[...], dqkv[:, lanes(wide, 3)]))
            else:
                put_lanes(k, s, 0, t_dot(h_all[...], dqkv[:, lanes(wide + 3)]))
                put_lanes(
                    k, s, 128,
                    shared(
                        s, h_all[...], dqkv[:, lanes(4 + 9 * (s // 2))],
                        attn[...], ga[:, lanes(split)],
                    ),
                )
                put_lanes(k, s, 256, t_dot(attn[...], ga[:, lanes(full)]))

    def core_copy(k):
        return remote(G.at[k, 1 - c], R0.at[ORDER.index(k) % 2], s0.at[k], r0.at[k], core_peer)

    def first_copies(k):
        return (
            remote(G.at[k, c, 0:2, :, 1 - x], R1.at[k, 0], s1.at[k, 0], r1.at[k, 0], x_peer),
            remote(G.at[k, c, 2:4, 1 - y], R1.at[k, 1], s1.at[k, 1], r1.at[k, 1], y_peer),
        )

    def second_copies(k):
        return (
            remote(G.at[k, c, 0:2, 1 - y, x], R2.at[k, 0], s2.at[k, 0], r2.at[k, 0], y_peer),
            remote(G.at[k, c, 2:4, y, 1 - x], R2.at[k, 1], s2.at[k, 1], r2.at[k, 1], x_peer),
        )

    def z_copies(k):
        return [
            remote(
                G.at[k, c, lax.rem(z + d, 4), y, x], R3.at[k, d - 1],
                s3.at[k, d - 1], r3.at[k, d - 1], z_peers[d - 1],
            )
            for d in (1, 2, 3)
        ]

    def near_copies(k):
        return [
            remote(
                G.at[k, c, h * 2 + 1 - zl], R1.at[k, h], s3.at[k, h], r3.at[k, h], near_peer
            )
            for h in range(2)
        ]

    def far_copy(k):
        return remote(
            G.at[k, c, (1 - zh) * 2 + zl], R2.at[k], s3.at[k, 2], r3.at[k, 2], far_peer
        )

    def pair_copies(k):
        if k % 2 == 0:
            return [
                remote(
                    G.at[k, c, z, other, 1 - x], R3.at[k, other],
                    s1.at[k, other], r1.at[k, other], x_peer,
                )
                for other in range(2)
            ]
        return [
            remote(
                G.at[k, c, z, 1 - y, other], R3.at[k, other],
                s1.at[k, other], r1.at[k, other], y_peer,
            )
            for other in range(2)
        ]

    def last_copy(k):
        if k % 2 == 0:
            return remote(
                G.at[k, c, z, 1 - y, x], R3.at[k, 2], s2.at[k, 0], r2.at[k, 0], y_peer
            )
        return remote(G.at[k, c, z, y, 1 - x], R3.at[k, 2], s2.at[k, 0], r2.at[k, 0], x_peer)

    def add(one, two):
        return (one.astype(F32) + two.astype(F32)).astype(BF16)

    def deep1(k):
        core_add(k)
        for copy in near_copies(k):
            copy.start()

    def deep2(k):
        for copy in near_copies(k):
            copy.wait_recv()
        for h in range(2):
            for yy in range(2):
                for xx in range(2):
                    at = h * 2 + zl
                    G[k, c, at, yy, xx] = add(G[k, c, at, yy, xx], R1[k, h, yy, xx])
        far_copy(k).start()

    def deep3(k):
        far_copy(k).wait_recv()
        for yy in range(2):
            for xx in range(2):
                G[k, c, z, yy, xx] = add(G[k, c, z, yy, xx], R2[k, yy, xx])
        for copy in pair_copies(k):
            copy.start()

    def deep4(k):
        for copy in pair_copies(k):
            copy.wait_recv()
        for other in range(2):
            if k % 2 == 0:
                G[k, c, z, other, x] = add(G[k, c, z, other, x], R3[k, other])
            else:
                G[k, c, z, y, other] = add(G[k, c, z, y, other], R3[k, other])
        last_copy(k).start()

    def deep5(k):
        last_copy(k).wait_recv()
        out[k] = G[k, c, z, y, x].astype(F32) + R3[k, 2].astype(F32)

    def deep_copies(k):
        return near_copies(k) + [far_copy(k)] + pair_copies(k) + [last_copy(k)]

    def phase0(k):
        compute(k)
        if ORDER.index(k) >= 2:
            pl.semaphore_wait(free, 1)
        core_copy(k).start()

    def core_add(k):
        core_copy(k).wait_recv()

        @pl.loop(0, 4)
        def _(zz):
            for yy in range(2):
                for xx in range(2):
                    G[k, c, zz, yy, xx] = add(G[k, c, zz, yy, xx], R0[ORDER.index(k) % 2, zz, yy, xx])

        if ORDER.index(k) < CHUNKS - 2:
            pl.semaphore_signal(free, inc=1, device_id=core_peer, device_id_type=MESH)

    def phase1(k):
        core_add(k)
        for copy in first_copies(k):
            copy.start()

    def phase2(k):
        for copy in first_copies(k):
            copy.wait_recv()
        for zz in range(2):
            for other in range(2):
                G[k, c, zz, other, x] = add(G[k, c, zz, other, x], R1[k, 0, zz, other])
                G[k, c, 2 + zz, y, other] = add(G[k, c, 2 + zz, y, other], R1[k, 1, zz, other])
        for copy in second_copies(k):
            copy.start()

    def phase3(k):
        for copy in second_copies(k):
            copy.wait_recv()
        for zz in range(2):
            G[k, c, zz, y, x] = add(G[k, c, zz, y, x], R2[k, 0, zz])
            G[k, c, 2 + zz, y, x] = add(G[k, c, 2 + zz, y, x], R2[k, 1, zz])
        for copy in z_copies(k):
            copy.start()

    def phase4(k):
        for copy in z_copies(k):
            copy.wait_recv()
        total = G[k, c, z, y, x].astype(F32)
        for d in range(3):
            total = total + R3[k, d].astype(F32)
        out[k] = total

    e_all[c, z, y, x] = early[...].astype(BF16)
    T[y, x] = text_part[: T.shape[2], :]
    phase0(2)
    phase0(0)
    phase1(2)
    advance(early_steps, 0)
    advance(text_steps, 0)
    phase0(3)
    deep1(0)
    phase0(1)
    phase1(3)
    phase0(4)
    deep1(1)
    advance(early_steps, 1)
    advance(text_steps, 1)
    phase0(5)
    phase1(4)
    phase1(5)
    advance(early_steps, 2)

    own = pl.ds(pl.multiple_of(seq * here, here), here)
    dqkv[:, :model] = jnp.zeros((dqkv.shape[0], model), BF16)
    lane_of = lax.broadcasted_iota(jnp.int32, lse.shape, 1)
    for load in loads:
        load.wait()

    @pl.loop(0, HEADS // 2)
    def _(p):
        at = lanes(p)
        key_at = lanes(p + HEADS // 2)
        value_at = lanes(p + HEADS)
        key_pair, value_pair = kv[:, at], kv[:, key_at]
        query_pair, up_pair = query[:, at], gattn[:, at]
        scaled = query_pair * jnp.asarray(HEAD ** (-0.5), BF16)
        d_q, d_k, d_v = [], [], []
        for half in range(2):
            scores = dot_t(pick_half(scaled, half), key_pair)
            log_total = jnp.sum(
                jnp.where(lane_of == 2 * p + half, lse[...], 0.0), axis=-1, keepdims=True
            )
            scores = jnp.where(mask, scores, NEG_FILL)
            probs = jnp.exp(scores - log_total)
            grad_probs = dot_t(pick_half(up_pair, half), value_pair)
            inner = jnp.sum(probs * grad_probs, axis=-1, keepdims=True)
            grad_scores = (probs * (grad_probs - inner)).astype(BF16)
            d_q.append(dot(grad_scores, key_pair))
            d_k.append(t_dot(grad_scores, query_pair))
            d_v.append(t_dot(probs.astype(BF16), up_pair))
        dqkv[own, at] = (join_halves(*d_q) * HEAD ** (-0.5)).astype(BF16)
        dqkv[:, key_at] = (join_halves(*d_k) * HEAD ** (-0.5)).astype(BF16)
        dqkv[:, value_at] = join_halves(*d_v).astype(BF16)

    def up_block(block):
        rows_at = pl.ds(pl.multiple_of(block * here, here), here)
        return dot_t(dqkv[rows_at, model:], w_qkv[:, model:])

    part = here // 2
    up_first = (
        remote(up_low.at[:, 1 - x, :part], R4.at[0:2], s4.at[0], r4.at[0], x_peer),
        remote(up_low.at[1 - y, :, part:], R4.at[2:4], s4.at[1], r4.at[1], y_peer),
    )
    up_second = (
        remote(up_low.at[1 - y, x, :part], R4.at[4], s4.at[2], r4.at[2], y_peer),
        remote(up_low.at[y, 1 - x, part:], R4.at[5], s4.at[3], r4.at[3], x_peer),
    )
    deep2(0)
    for block in range(4):
        up_low[block // 2, block % 2] = up_block(block).astype(BF16)
    for copy in up_first:
        copy.start()
    phase0(6)
    phase2(2)
    deep2(1)
    phase0(7)
    phase1(6)
    phase2(3)
    phase1(7)
    phase3(2)
    deep3(0)
    for copy in up_first:
        copy.wait_recv()
    for i in range(2):
        up_low[i, x, :part] = add(up_low[i, x, :part], R4[i])
        up_low[y, i, part:] = add(up_low[y, i, part:], R4[2 + i])
    for copy in up_second:
        copy.start()
    advance(early_steps, 3)
    advance(text_steps, 2)
    phase2(4)
    phase3(3)
    deep3(1)
    deep4(0)
    phase2(5)
    phase3(4)
    deep4(1)
    deep5(0)
    for copy in up_second:
        copy.wait_recv()
    up_one = dot_t(dqkv[own, :model], w_qkv[:, :model]) + up_low[y, x].astype(F32)
    up_one = up_one + jnp.concatenate([R4[4], R4[5]], axis=0).astype(F32)
    normed, inverse = norm_parts(frames[...].astype(F32))
    for i, total in enumerate((col_sum(up_one), col_sum(up_one * normed))):
        for j in range(model // 128):
            at = i * (model // 128) + j
            late[at : at + 1, :] = total[:, j * 128 : (j + 1) * 128]
    late[2 * (model // 128) :, :] = jnp.zeros((16 - 2 * (model // 128), 128), F32)
    d_frames[...] = gx1[...] + norm_back(normed, inverse, up_one * (1.0 + mods[1:2, :]))
    l_all[c, z, y, x] = late[...].astype(BF16)
    advance(late_steps, 0)
    total = jnp.zeros(d_text.shape, F32)
    for i in range(4):
        total = total + T[i // 2, i % 2].astype(F32) * jnp.where(
            seg_s[0, i * here] == seq, 1.0, 0.0
        )
    d_text[...] = total
    phase2(6)
    phase3(5)
    advance(late_steps, 1)
    deep5(1)
    phase2(7)
    phase3(6)
    advance(late_steps, 2)
    phase3(7)
    advance(late_steps, 3)

    @pl.loop(len(DEEP), CHUNKS)
    def _(k):
        phase4(k)

    advance(early_steps, 4)
    advance(late_steps, 4)
    for k in range(CHUNKS):
        core_copy(k).wait_send()
    for k in DEEP:
        for copy in deep_copies(k):
            copy.wait_send()

    @pl.loop(len(DEEP), CHUNKS)
    def _(k):
        for copy in (*first_copies(k), *second_copies(k), *z_copies(k)):
            copy.wait_send()

    for copy in (*up_first, *up_second):
        copy.wait_send()
    for steps in (early_steps, late_steps, text_steps):
        for step in steps:
            for copy in step:
                copy.wait_send()


def in_vmem(count):
    return [pl.BlockSpec(memory_space=pltpu.VMEM)] * count


def in_any(count):
    return [pl.BlockSpec(memory_space=pl.ANY)] * count


def finish_kernel(
    done, d_frames_in, d_text_in, output_in, e_all, l_all, step, seg_s, w_ada,
    output, d_frames, d_text, d_step, d_w_ada, d_b_ada, d_w_qkv, d_w_out, d_g_cross,
    d_w_cq, d_w_ckv, d_w_co, d_w_up, d_b_up, d_w_down, d_b_down,
    item, ada, ada_t,
):
    seq = lax.axis_index("seq")
    rows = lax.axis_index("rows")
    here, model = output_in.shape
    parts = model // 128
    output[0] = output_in[...]
    d_frames[0] = d_frames_in[...]
    d_text[:, 0, :] = d_text_in[: d_text.shape[0], :]
    bias_sum = jnp.zeros((16, model), F32)
    for r in range(8):
        for s in range(4):
            entry = e_all[r % 2, r // 2, s // 2, s % 2].astype(F32)
            tail = l_all[r % 2, r // 2, s // 2, s % 2].astype(F32)
            bias_sum = bias_sum + entry
            at = slice(r * 4 + s, r * 4 + s + 1)
            ada[at, :] = entry[10:11]
            for j in range(4):
                item[at, (2 + j) * model : (3 + j) * model] = entry[j : j + 1]
            for j in range(2 * parts):
                item[at, j * 128 : (j + 1) * 128] = tail[j : j + 1]
    item_sum = jnp.sum(item[...], axis=0, keepdims=True)

    def share(pieces):
        total = jnp.zeros_like(pieces[0])
        for r, piece in enumerate(pieces):
            total = total + jnp.where(rows == r, piece, jnp.zeros_like(piece))
        return total

    def cut(row, size):
        return [row[:, at * size : (at + 1) * size] for at in range(row.shape[1] // size)]

    d_b_ada[...] = share(cut(item_sum, 6 * model // 8)).reshape(6 * model // 8)
    d_g_cross[...] = share(cut(bias_sum[4:5], model // 8)).reshape(model // 8)
    d_b_down[...] = share(cut(bias_sum[9:10], model // 8)).reshape(model // 8)
    d_b_up[...] = share(
        [piece for at in range(5, 9) for piece in cut(bias_sum[at : at + 1], model // 2)]
    ).reshape(model // 2)
    ada_t[...] = ada[...].T
    tall = model // 8
    share_at = pl.ds(pl.multiple_of(seq * 9 * 128, 128), 9 * 128)
    d_w_ada[...] = jnp.dot(
        ada_t[pl.ds(pl.multiple_of(rows * tall, 8), tall), :],
        item[:, share_at],
        precision=PRECISE,
        preferred_element_type=F32,
    )
    near = item[pl.ds(pl.multiple_of(rows // 2 * 8, 8), 8), :]
    total = jnp.zeros((1, 6 * model), F32)
    for j in range(8):
        wanted = jnp.where(seg_s[0, j % 4 * here] == seq, 1.0, 0.0)
        wanted = jnp.where(rows % 2 == j // 4, wanted, 0.0)
        total = total + near[j : j + 1] * wanted
    high = total.astype(BF16)
    low = (total - high.astype(F32)).astype(BF16)
    both = jnp.concatenate(
        [high.astype(F32), low.astype(F32), jnp.zeros((6, 6 * model), F32)], axis=0
    ).astype(BF16)
    d_ada = jnp.sum(dot_t(both, w_ada[...]), axis=0, keepdims=True)
    all_steps = step[0].astype(F32)
    my_step = jnp.zeros((1, model), F32)
    for j in range(4):
        my_step = my_step + all_steps[j : j + 1] * jnp.where(seq == j, 1.0, 0.0)
    gate = 1.0 / (1.0 + jnp.exp(-my_step))
    d_step[0] = d_ada * gate * (1.0 + my_step * (1.0 - gate))
    odd = seq % 2 == 1

    def place(full, mixed, first):
        even = mixed[:, :HEAD] if first else mixed[:, HEAD:]
        other = mixed[:, HEAD:] if first else mixed[:, :HEAD]
        return jnp.where(
            odd,
            jnp.concatenate([other, full], axis=1),
            jnp.concatenate([full, even], axis=1),
        )

    width = model // 2
    d_w_down[: model // 8] = done[0]
    d_w_down[model // 8 :] = done[1]
    d_w_up[:, :width] = done[2]
    d_w_up[:, width:] = done[3]
    cross, last = done[4], done[7]
    d_w_cq[...] = place(cross[:, :128], cross[:, 256:], True)
    d_w_co[...] = place(cross[:, 128:256], cross[:, 256:], False)
    d_w_ckv[...] = done[5]
    d_w_qkv[...] = place(
        jnp.concatenate([done[6], last[:, :128]], axis=1), last[:, 128:256], True
    )
    d_w_out[...] = place(last[:, 256:], last[:, 128:256], False)


def smem(count):
    return [pl.BlockSpec(memory_space=pltpu.SMEM)] * count


def per_device(
    frames, text_tokens, step_embed, segments, cotangent,
    w_ada, b_ada, w_qkv, w_out, g_cross, w_cq, w_ckv, w_co, w_up, b_up, w_down, b_down,
):
    seq_count = lax.axis_size("seq")
    rows_count = lax.axis_size("rows")
    here, model = frames.shape[1:]
    length = segments.shape[1]
    hidden = w_up.shape[1]
    assert (length // ITEMS) % here == 0
    text_rows, text_kept, step_rows = 128, 80, 16

    def like(shape, dtype=BF16):
        return jax.ShapeDtypeStruct(shape, dtype)

    square = like((here, model))
    dma = pltpu.SemaphoreType.DMA
    vmem = pltpu.VMEM
    (
        output, act, gm_t, h3, gpre, h2, cross, gqc, gc, gkvc, attn, ga, gattn, gx1, query,
        kv, h_all, lse, mods, text_part, early, text_mine,
    ) = pl.pallas_call(
        forward_kernel,
        out_shape=(
            square, like((here, hidden)), like((model, here)), square, like((here, hidden)),
            square, square, square, square, like((text_rows, 2 * model)), square, square,
            square, like((here, model), F32), square, like((length, 2 * model)),
            like((length, model)), like((here, 128), F32), like((8, model), F32),
            like((text_rows, model)), like((16, model), F32), like((text_rows, model)),
        ),
        in_specs=in_any(1) + in_vmem(3) + smem(1) + in_vmem(1)
        + in_any(1) + in_vmem(1) + in_any(2) + in_vmem(1) + in_any(4) + in_vmem(1)
        + in_any(1) + in_vmem(1),
        out_specs=tuple(in_vmem(22)),
        scratch_shapes=[
            vmem((seq_count, here, model), BF16),
            vmem(w_ada.shape, BF16), vmem(w_qkv.shape, BF16), vmem(w_out.shape, BF16),
            vmem(w_cq.shape, BF16), vmem(w_ckv.shape, BF16), vmem(w_co.shape, BF16),
            vmem(w_up.shape, BF16), vmem(w_down.shape, BF16),
            vmem((HEADS, here, text_rows), F32),
            vmem((here, model), F32), vmem((here, model), F32),
            vmem((step_rows, 6 * model), F32),
            vmem((1, hidden), F32),
            dma((9,)), dma((4,)), dma((4,)),
        ],
        compiler_params=pltpu.CompilerParams(
            collective_id=0, has_side_effects=True, vmem_limit_bytes=VMEM_MOST
        ),
        name="forward_layer",
    )(
        frames, cotangent, text_tokens, step_embed, segments, segments,
        w_ada, b_ada, w_qkv, w_out, g_cross, w_cq, w_ckv, w_co, w_up, b_up, w_down, b_down,
    )

    tall, width = model // rows_count, model // 2
    table = (2, 4, 2, 2)
    done, d_frames, d_text, e_all, l_all = pl.pallas_call(
        backward_kernel,
        out_shape=(
            like((CHUNKS, tall, width), F32), like((here, model), F32),
            like((text_kept, model), F32), like(table + (16, model)),
            like(table + (16, 128)),
        ),
        in_specs=in_vmem(15) + smem(1) + in_vmem(1) + in_any(8),
        out_specs=tuple(in_vmem(5)),
        scratch_shapes=[
            vmem((CHUNKS,) + table + (tall, width), BF16),
            vmem((2, 4, 2, 2, tall, width), BF16),
            vmem((CHUNKS, 2, 2, 2, tall, width), BF16),
            vmem((CHUNKS, 2, 2, tall, width), BF16),
            vmem((CHUNKS, 3, tall, width), BF16),
            vmem((6, here // 2, model), BF16),
            vmem((length, 3 * model), BF16),
            vmem((2, 2, here, model), BF16),
            vmem((2, 2, text_kept, model), BF16),
            vmem((16, 128), F32),
            vmem((here, model), BF16), vmem((here, model), F32), vmem((here, model), BF16),
            vmem((length, 2 * model), BF16), vmem((length, model), BF16),
            vmem((here, 128), F32), vmem((here, model), BF16), vmem(w_qkv.shape, BF16),
            dma((8,)),
            dma((CHUNKS,)), dma((CHUNKS,)),
            dma((CHUNKS, 2)), dma((CHUNKS, 2)),
            dma((CHUNKS, 2)), dma((CHUNKS, 2)),
            dma((CHUNKS, 3)), dma((CHUNKS, 3)),
            dma((4,)), dma((4,)), dma((6,)), dma((6,)), dma((6,)), dma((6,)),
            dma((2,)), dma((2,)), pltpu.SemaphoreType.REGULAR,
        ],
        compiler_params=pltpu.CompilerParams(
            collective_id=1, has_side_effects=True, vmem_limit_bytes=VMEM_MOST
        ),
        name="backward_layer",
    )(
        act, gm_t, h3, gpre, h2, cross, gqc, gc, gkvc, attn, ga, mods, text_part, early,
        text_mine, segments, segments, gattn, gx1, query, kv, h_all, lse, frames, w_qkv,
    )

    def shard(*shape):
        return like(shape, F32)

    seq_share = model // seq_count
    results = pl.pallas_call(
        finish_kernel,
        out_shape=(
            like((1, here, model)), shard(1, here, model), shard(TXT, 1, model),
            shard(1, 1, model), shard(tall, 6 * seq_share), shard(6 * tall),
            shard(tall, 3 * seq_share), shard(tall, seq_share), shard(tall),
            shard(tall, seq_share), shard(tall, 2 * seq_share), shard(tall, seq_share),
            shard(tall, hidden // seq_count), shard(hidden // rows_count),
            shard(seq_share, hidden // rows_count), shard(tall),
        ),
        in_specs=in_vmem(7) + smem(1) + in_vmem(1),
        out_specs=tuple(in_vmem(16)),
        scratch_shapes=[
            vmem((32, 6 * model), F32), vmem((32, model), F32), vmem((model, 32), F32),
        ],
        compiler_params=pltpu.CompilerParams(vmem_limit_bytes=VMEM_MOST),
        name="finish_layer",
    )(done, d_frames, d_text, output, e_all, l_all, step_embed, segments, w_ada)
    results = list(results)
    results[2] = results[2].transpose(1, 0, 2)
    results[14] = results[14].T
    return tuple(results)


def solution(mesh):
    row_seq = P("rows", "seq", None)
    in_specs = (
        row_seq, P("rows", None, None), P("rows", None, None), P("rows", None), row_seq,
    ) + (P(),) * 12
    out_specs = (row_seq,) * 4 + (
        P("rows", "seq"), P("rows"), P("rows", "seq"), P("rows", "seq"), P("rows"),
        P("rows", "seq"), P("rows", "seq"), P("rows", "seq"), P("rows", "seq"), P("rows"),
        P("rows", "seq"), P("rows"),
    )
    fused = mesh.shape["rows"] == 8 and mesh.shape["seq"] == 4
    return jax.shard_map(
        per_device if fused else per_device_plain, mesh=mesh, in_specs=in_specs, out_specs=out_specs, check_vma=False
    )
```

```python
import functools

import jax
import jax.numpy as jnp
from jax import lax
from jax.experimental import pallas as pl
from jax.experimental.pallas import tpu as pltpu
from jax.sharding import PartitionSpec as P

HEADS = 12
HEAD = 64
TXT = 77
ITEMS = 4

EPSILON = 1e-06
NEG_FILL = -1e30
PRECISE = lax.Precision.HIGHEST
F32 = jnp.float32
BF16 = jnp.bfloat16
MESH = pl.DeviceIdType.MESH
CHUNKS = 8
VMEM_MOST = 67_043_328


def dot(left, right):
    return jnp.dot(left, right, preferred_element_type=F32)


def dot_t(left, right):
    return lax.dot_general(left, right, (((1,), (1,)), ((), ())), preferred_element_type=F32)


def t_dot(left, right):
    return lax.dot_general(left, right, (((0,), (0,)), ((), ())), preferred_element_type=F32)


def norm_parts(values):
    center = values - jnp.mean(values, axis=-1, keepdims=True)
    inverse = lax.rsqrt(jnp.mean(center * center, axis=-1, keepdims=True) + EPSILON)
    return center * inverse, inverse


def norm_back(normed, inverse, upstream):
    return inverse * (
        upstream
        - jnp.mean(upstream, axis=-1, keepdims=True)
        - normed * jnp.mean(upstream * normed, axis=-1, keepdims=True)
    )


def gelu_tanh(values):
    return jax.nn.gelu(values, approximate=True)


def split_heads(matrix):
    return matrix.reshape(matrix.shape[0], HEADS, HEAD)


def scores_of(queries, keyset, allowed):
    raw = jnp.einsum(
        "qhd,khd->hqk", split_heads(queries), split_heads(keyset), preferred_element_type=F32
    )
    raw = raw * HEAD ** (-0.5)
    return raw if allowed is None else jnp.where(allowed[None, None, :], raw, NEG_FILL)


def attend_forward(queries, keyset, valueset, allowed):
    scores = scores_of(queries, keyset, allowed)
    top_score = jnp.max(scores, axis=-1, keepdims=True)
    exp_scores = jnp.exp(scores - top_score)
    totals = jnp.sum(exp_scores, axis=-1, keepdims=True)
    probs_low = (exp_scores / totals).astype(BF16)
    mixed = jnp.einsum(
        "hqk,khd->qhd", probs_low, split_heads(valueset), preferred_element_type=F32
    )
    return mixed.reshape(queries.shape).astype(BF16), top_score + jnp.log(totals)


def attend_backward(queries, keyset, valueset, allowed, log_total, upstream):
    probs = jnp.exp(scores_of(queries, keyset, allowed) - log_total)
    up_heads = split_heads(upstream)
    grad_probs = jnp.einsum(
        "qhd,khd->hqk", up_heads, split_heads(valueset), preferred_element_type=F32
    )
    inner = jnp.sum(probs * grad_probs, axis=-1, keepdims=True)
    grad_scores = (probs * (grad_probs - inner)).astype(BF16)
    grad_query = jnp.einsum(
        "hqk,khd->qhd", grad_scores, split_heads(keyset), preferred_element_type=F32
    )
    grad_key = jnp.einsum(
        "hqk,qhd->khd", grad_scores, split_heads(queries), preferred_element_type=F32
    )
    grad_value = jnp.einsum(
        "hqk,qhd->khd", probs.astype(BF16), up_heads, preferred_element_type=F32
    )
    return (
        (grad_query.reshape(queries.shape) * HEAD ** (-0.5)).astype(BF16),
        (grad_key.reshape(keyset.shape) * HEAD ** (-0.5)).astype(BF16),
        grad_value.reshape(valueset.shape).astype(BF16),
    )


def scatter_plain(matrix):
    part = lax.psum_scatter(matrix.astype(BF16), "rows", scatter_dimension=0, tiled=True)
    part = lax.psum_scatter(part, "seq", scatter_dimension=1, tiled=True)
    return part.astype(F32)


def per_device_plain(
    frames, text_tokens, step_embed, segments, cotangent,
    w_ada, b_ada, w_qkv, w_out, g_cross, w_cq, w_ckv, w_co, w_up, b_up, w_down, b_down,
):
    seq_count = lax.axis_size("seq")
    rows_count = lax.axis_size("rows")
    seq_index = lax.axis_index("seq")
    rows_index = lax.axis_index("rows")
    frames, text_tokens, step_embed = frames[0], text_tokens[0], step_embed[0]
    segments, cotangent = segments[0], cotangent[0]
    here, model = frames.shape
    length = segments.shape[0]
    assert (length // ITEMS) % here == 0
    block_slots = segments[::here]
    slot = lax.dynamic_index_in_dim(block_slots, seq_index, 0, keepdims=False)
    allowed = segments == slot
    text_mine = lax.dynamic_slice_in_dim(text_tokens, slot * TXT, TXT, axis=0)

    frames_all = lax.all_gather(frames, "seq", axis=0, tiled=True)
    ada_in = jax.nn.silu(step_embed.astype(F32)).astype(BF16)
    item_mod = dot(ada_in, w_ada) + b_ada.astype(F32)
    mine = lax.dynamic_slice_in_dim(item_mod, slot, 1, axis=0)
    shift_a, scale_a, gate_a, shift_b, scale_b, gate_b = jnp.split(mine, 6, axis=-1)

    normed_all, inverse_all = norm_parts(frames_all.astype(F32))
    hot = (block_slots[:, None] == jnp.arange(ITEMS)[None, :]).astype(F32)
    block_mod = jnp.dot(hot, item_mod[:, : 2 * model], precision=PRECISE)
    frame_mod = jnp.repeat(block_mod, here, axis=0)
    h_all = (normed_all * (1.0 + frame_mod[:, model:]) + frame_mod[:, :model]).astype(BF16)
    frames_f32 = frames.astype(F32)
    normed_0, inverse_0 = norm_parts(frames_f32)
    h_one = (normed_0 * (1.0 + scale_a) + shift_a).astype(BF16)
    query_a = dot(h_one, w_qkv[:, :model]).astype(BF16)
    kv_all = dot(h_all, w_qkv[:, model:]).astype(BF16)
    key_all, value_all = kv_all[:, :model], kv_all[:, model:]
    attn_low, lse_self = attend_forward(query_a, key_all, value_all, allowed)
    branch_a = dot(attn_low, w_out)
    x_one = frames_f32 + gate_a * branch_a
    gain = g_cross.astype(F32)[None]
    normed_1, inverse_1 = norm_parts(x_one)
    h_two = (normed_1 * gain).astype(BF16)
    query_c = dot(h_two, w_cq).astype(BF16)
    text_kv = dot(text_mine, w_ckv).astype(BF16)
    key_c, value_c = text_kv[:, :model], text_kv[:, model:]
    cross_low, lse_cross = attend_forward(query_c, key_c, value_c, None)
    x_two = x_one + dot(cross_low, w_co)
    normed_2, inverse_2 = norm_parts(x_two)
    h_three = (normed_2 * (1.0 + scale_b) + shift_b).astype(BF16)
    pre_act = dot(h_three, w_up) + b_up.astype(F32)
    act_low = gelu_tanh(pre_act).astype(BF16)
    branch_m = dot(act_low, w_down) + b_down.astype(F32)
    output = (x_two + gate_b * branch_m).astype(BF16)

    grad_out = cotangent.astype(F32)
    grad_m = (gate_b * grad_out).astype(BF16)
    grad_act = dot_t(grad_m, w_down)
    unused_act, gelu_back = jax.vjp(gelu_tanh, pre_act)
    grad_pre = gelu_back(grad_act)[0].astype(BF16)
    up_three = dot_t(grad_pre, w_up)
    grad_x2 = grad_out + norm_back(normed_2, inverse_2, up_three * (1.0 + scale_b))
    grad_c = grad_x2.astype(BF16)
    grad_cross = dot_t(grad_c, w_co).astype(BF16)
    grad_qc, grad_kc, grad_vc = attend_backward(
        query_c, key_c, value_c, None, lse_cross, grad_cross
    )
    grad_kvc = jnp.concatenate([grad_kc, grad_vc], axis=-1)
    up_two = dot_t(grad_qc, w_cq)
    grad_x1 = grad_x2 + norm_back(normed_1, inverse_1, up_two * gain)
    grad_a = (gate_a * grad_x1).astype(BF16)
    grad_attn = dot_t(grad_a, w_out).astype(BF16)
    grad_qa, grad_ka, grad_va = attend_backward(
        query_a, key_all, value_all, allowed, lse_self, grad_attn
    )
    grad_kva = jnp.concatenate([grad_ka, grad_va], axis=-1)
    up_kv = dot_t(grad_kva, w_qkv[:, model:]).astype(BF16)
    up_one = dot_t(grad_qa, w_qkv[:, :model]) + lax.psum_scatter(
        up_kv, "seq", scatter_dimension=0, tiled=True
    ).astype(F32)
    d_frames = grad_x1 + norm_back(normed_0, inverse_0, up_one * (1.0 + scale_a))

    small = jnp.concatenate(
        [
            jnp.sum(up_one, axis=0),
            jnp.sum(up_one * normed_0, axis=0),
            jnp.sum(grad_x1 * branch_a, axis=0),
            jnp.sum(up_three, axis=0),
            jnp.sum(up_three * normed_2, axis=0),
            jnp.sum(grad_out * branch_m, axis=0),
            jnp.sum(up_two * normed_1, axis=0),
            jnp.sum(grad_pre.astype(F32), axis=0),
            jnp.sum(grad_m.astype(F32), axis=0),
            lax.dynamic_index_in_dim(ada_in, slot, 0, keepdims=False).astype(F32),
        ]
    )
    small_all = lax.all_gather(small, ("rows", "seq"), axis=0, tiled=False)
    small_all = small_all.reshape(rows_count * seq_count, -1)
    item_all = small_all[:, : 6 * model]
    bias_all = small_all[:, 6 * model : -model]
    ada_all = small_all[:, -model:]

    def share(table, count, index):
        size = table.shape[-1] // count
        return lax.dynamic_slice_in_dim(table, index * size, size, axis=-1)

    def bias_sum(table):
        return jnp.sum(share(table, rows_count, rows_index), axis=0)

    d_b_ada = bias_sum(item_all)
    d_g_cross = bias_sum(bias_all[:, :model])
    d_b_up = bias_sum(bias_all[:, model:-model])
    d_b_down = bias_sum(bias_all[:, -model:])
    d_w_ada = lax.dot_general(
        share(ada_all, rows_count, rows_index),
        share(item_all, seq_count, seq_index),
        (((0,), (0,)), ((), ())),
        precision=PRECISE,
        preferred_element_type=F32,
    )
    item_share = ITEMS // seq_count
    row_items = lax.dynamic_slice_in_dim(item_all, rows_index * seq_count, seq_count, axis=0)
    owned = seq_index * item_share + jnp.arange(item_share)
    pick = (owned[:, None] == block_slots[None, :]).astype(F32)
    item_mine = jnp.dot(pick, row_items, precision=PRECISE)
    d_ada = lax.dot_general(
        item_mine, w_ada.astype(F32), (((1,), (1,)), ((), ())), precision=PRECISE
    )
    my_step = lax.dynamic_slice_in_dim(
        step_embed, seq_index * item_share, item_share, axis=0
    ).astype(F32)
    unused_step, silu_back = jax.vjp(jax.nn.silu, my_step)
    d_step = silu_back(d_ada)[0]
    text_part = dot_t(grad_kvc, w_ckv).astype(BF16)
    text_full = lax.dynamic_update_slice_in_dim(
        jnp.zeros(text_tokens.shape, BF16), text_part, slot * TXT, axis=0
    )
    d_text = lax.psum_scatter(text_full, "seq", scatter_dimension=0, tiled=True).astype(F32)

    d_w_down = scatter_plain(t_dot(act_low, grad_m))
    d_w_up = scatter_plain(t_dot(h_three, grad_pre))
    d_w_cq = scatter_plain(t_dot(h_two, grad_qc))
    d_w_co = scatter_plain(t_dot(cross_low, grad_c))
    d_w_ckv = scatter_plain(t_dot(text_mine, grad_kvc))
    d_w_out = scatter_plain(t_dot(attn_low, grad_a))
    d_w_qkv = scatter_plain(
        jnp.concatenate([t_dot(h_one, grad_qa), t_dot(h_all, grad_kva)], axis=1)
    )
    return (
        output[None], d_frames[None], d_text[None], d_step[None],
        d_w_ada, d_b_ada, d_w_qkv, d_w_out, d_g_cross, d_w_cq, d_w_ckv, d_w_co,
        d_w_up, d_b_up, d_w_down, d_b_down,
    )


def remote(src, dst, send, recv, peer):
    return pltpu.make_async_remote_copy(
        src_ref=src, dst_ref=dst, send_sem=send, recv_sem=recv,
        device_id=peer, device_id_type=MESH,
    )


def enter(peers):
    barrier = pltpu.get_barrier_semaphore()
    for peer in peers:
        pl.semaphore_signal(barrier, inc=1, device_id=peer, device_id_type=MESH)
    pl.semaphore_wait(barrier, len(peers))


def low_half(shape):
    return lax.broadcasted_iota(jnp.int32, shape, len(shape) - 1) < HEAD


def pick_half(pair, half):
    lower = low_half(pair.shape)
    return jnp.where(lower if half == 0 else ~lower, pair, jnp.zeros_like(pair))


def join_halves(first, second):
    return jnp.where(low_half(first.shape), first, second)


def lanes(index, count=1):
    return pl.ds(pl.multiple_of(index * 128, 128), 128 * count)


def col_sum(values):
    return jnp.sum(values, axis=0, keepdims=True)


def softmax_rows(scores):
    top = jnp.max(scores, axis=-1, keepdims=True)
    raised = jnp.exp(scores - top)
    total = jnp.sum(raised, axis=-1, keepdims=True)
    return raised / total, top + jnp.log(total)


def forward_kernel(
    frames, cot, text, step, seg_s, seg,
    w_ada, b_ada, w_qkv, w_out, g_cross, w_cq, w_ckv, w_co, w_up, b_up, w_down, b_down,
    output, act, gm_t, h3, gpre, h2, cross, gqc, gkvc, attn, query,
    kv, h_all, lse, mods, early, text_mine, branch, x_one, x_two, acc_u, prob_c,
    fr, ada_v, qkv_v, out_v, cq_v, ckv_v, co_v, up_v, down_v, gm, acc_m,
    item, up_bias, local, send, recv,
):
    seq = lax.axis_index("seq")
    y, x = seq // 2, seq % 2
    x_id, y_id, d_id = y * 2 + 1 - x, (1 - y) * 2 + x, (1 - y) * 2 + 1 - x
    x_peer, y_peer = {"seq": x_id}, {"seq": y_id}
    frames = frames.at[0]
    here, model = frames.shape
    part = here // 2
    slot = seg_s[0, seq * here]
    mask = seg[...] == slot
    loads = [
        pltpu.make_async_copy(src, dst, local.at[i])
        for i, (src, dst) in enumerate(
            [
                (frames, fr.at[seq]), (w_ada, ada_v), (w_qkv, qkv_v), (w_out, out_v),
                (w_ckv, ckv_v), (w_cq, cq_v), (w_co, co_v), (w_up, up_v), (w_down, down_v),
            ]
        )
    ]
    for i in (0, 1):
        loads[i].start()
    enter([x_peer, y_peer])
    to_x = remote(frames, fr.at[seq], send.at[0], recv.at[0], x_peer)
    to_y = remote(frames, fr.at[seq], send.at[1], recv.at[1], y_peer)
    to_x.start()
    to_y.start()
    loads[2].start()
    loads[4].start()

    def row(at):
        return mods[at : at + 1, :]

    step_f32 = jnp.concatenate(
        [step[0].astype(F32), jnp.zeros((item.shape[0] - ITEMS, model), F32)], axis=0
    )
    ada = (step_f32 / (1.0 + jnp.exp(-step_f32))).astype(BF16)
    loads[1].wait()
    item[...] = dot(ada, ada_v[...]) + b_ada[...].astype(F32)[None]
    for i in (3, 5, 6, 7, 8):
        loads[i].start()
    slot_row = lax.broadcasted_iota(jnp.int32, (item.shape[0], model), 0)
    chosen_mine = (slot_row == slot).astype(F32)
    for part_at in range(6):
        mods[part_at : part_at + 1, :] = col_sum(
            item[:, part_at * model : (part_at + 1) * model] * chosen_mine
        )
    early[10:11, :] = col_sum(ada.astype(F32) * chosen_mine)
    up_bias[...] = b_up[...].astype(F32)[None]

    def take(block):
        chosen = (slot_row == seg_s[0, block * here]).astype(F32)
        shift = col_sum(item[:, :model] * chosen)
        scale = col_sum(item[:, model : 2 * model] * chosen)
        normed, unused = norm_parts(fr[block].astype(F32))
        rows_at = pl.ds(pl.multiple_of(block * here, here), here)
        h_block = (normed * (1.0 + scale) + shift).astype(BF16)
        h_all[rows_at, :] = h_block
        kv[rows_at, :] = dot(h_block, qkv_v[:, model:]).astype(BF16)
        return h_block

    loads[0].wait()
    loads[2].wait()
    h_one = take(seq)
    query[...] = dot(h_one, qkv_v[:, :model]).astype(BF16)
    loads[4].wait()
    picked = (text_mine.shape[0], text.shape[1])
    text_at = lax.broadcasted_iota(jnp.int32, picked, 0)
    token = lax.broadcasted_iota(jnp.int32, picked, 1)
    hot = jnp.where((token == text_at + TXT * slot) & (text_at < TXT), 1.0, 0.0).astype(BF16)
    text_mine[...] = dot(hot, text[0]).astype(BF16)
    text_kv = dot(text_mine[...], ckv_v[...]).astype(BF16)
    gkvc[...] = text_kv
    to_x.wait_recv()
    fwd_y = remote(
        fr.at[x_id, pl.ds(0, part)], fr.at[x_id, pl.ds(0, part)], send.at[2], recv.at[2], y_peer
    )
    fwd_y.start()
    to_y.wait_recv()
    fwd_x = remote(
        fr.at[y_id, pl.ds(part, part)], fr.at[y_id, pl.ds(part, part)],
        send.at[3], recv.at[3], x_peer,
    )
    fwd_x.start()
    take(x_id)
    take(y_id)
    fwd_y.wait_recv()
    fwd_x.wait_recv()
    take(d_id)

    lse[...] = jnp.zeros_like(lse)
    lane_of = lax.broadcasted_iota(jnp.int32, lse.shape, 1)

    @pl.loop(0, HEADS // 2)
    def _(p):
        at = lanes(p)
        value_at = lanes(p + HEADS // 2)
        pair = query[:, at] * jnp.asarray(HEAD ** (-0.5), BF16)
        outs = []
        for half in range(2):
            scores = dot_t(pick_half(pair, half), kv[:, at])
            scores = jnp.where(mask, scores, NEG_FILL)
            probs, log_total = softmax_rows(scores)
            lse[...] = jnp.where(lane_of == 2 * p + half, log_total, lse[...])
            outs.append(dot(probs.astype(BF16), kv[:, value_at]))
        attn[:, at] = join_halves(*outs).astype(BF16)

    loads[3].wait()
    branch_a = dot(attn[...], out_v[...])
    x_one[...] = frames_f32(fr[seq]) + row(2) * branch_a
    branch[...] = branch_a
    gain = g_cross[...].astype(F32)[None]
    normed_1, unused = norm_parts(x_one[...])
    h2[...] = (normed_1 * gain).astype(BF16)
    loads[5].wait()
    query_c = dot(h2[...], cq_v[...]).astype(BF16)
    gqc[...] = query_c

    text_rows = text_mine.shape[0]
    key_lane = lax.broadcasted_iota(jnp.int32, (here, text_rows), 1)

    @pl.loop(0, HEADS // 2, unroll=True)
    def _(p):
        at = lanes(p)
        value_at = lanes(p + HEADS // 2)
        pair = gqc[:, at] * jnp.asarray(HEAD ** (-0.5), BF16)
        outs = []
        for half in range(2):
            scores = dot_t(pick_half(pair, half), gkvc[:, at])
            probs, unused = softmax_rows(jnp.where(key_lane < TXT, scores, NEG_FILL))
            low = probs.astype(BF16)
            prob_c[2 * p + half] = low
            outs.append(dot(low, gkvc[:, value_at]))
        cross[:, at] = join_halves(*outs).astype(BF16)

    loads[6].wait()
    x_two[...] = x_one[...] + dot(cross[...], co_v[...])
    normed_2, unused = norm_parts(x_two[...])
    h3[...] = (normed_2 * (1.0 + row(4)) + row(3)).astype(BF16)
    grad_out = cot[0].astype(F32)
    grad_m = row(5) * grad_out
    gm_low = grad_m.astype(BF16)
    gm_t[...] = gm_low.astype(F32).T.astype(BF16)
    early[9:10, :] = col_sum(gm_low.astype(F32))
    gm[...] = gm_low
    acc_m[...] = jnp.zeros_like(acc_m)
    acc_u[...] = jnp.zeros_like(acc_u)
    loads[7].wait()
    loads[8].wait()
    slab = model // 2

    @pl.loop(0, w_up.shape[1] // slab)
    def _(j):
        at = pl.ds(pl.multiple_of(j * slab, slab), slab)
        pre = dot(h3[...], up_v[:, at]) + up_bias[:, at]
        inner = GELU_SCALE * (pre + 0.044715 * pre * pre * pre)
        tanh = jnp.tanh(inner)
        act_low = (0.5 * pre * (1.0 + tanh)).astype(BF16)
        act[:, at] = act_low
        acc_m[...] += dot(act_low, down_v[at, :])
        slope = 0.5 * (1.0 + tanh) + 0.5 * pre * (1.0 - tanh * tanh) * (
            GELU_SCALE * (1.0 + 3.0 * 0.044715 * pre * pre)
        )
        grad_pre = (dot_t(gm[...], down_v[at, :]) * slope).astype(BF16)
        gpre[:, at] = grad_pre
        acc_u[...] += dot_t(grad_pre, up_v[:, at])

    for quarter in range(4):
        at = slice(quarter * model, (quarter + 1) * model)
        early[5 + quarter : 6 + quarter, :] = col_sum(gpre[:, at].astype(F32))
    branch_m = acc_m[...] + b_down[...].astype(F32)[None]
    output[...] = (x_two[...] + row(5) * branch_m).astype(BF16)
    early[3:4, :] = col_sum(grad_out * branch_m)
    up_three = acc_u[...]
    early[1:2, :] = col_sum(up_three)
    early[2:3, :] = col_sum(up_three * normed_2)
    early[0:1, :] = jnp.zeros((1, model), F32)
    early[4:5, :] = jnp.zeros((1, model), F32)
    early[11:16, :] = jnp.zeros((5, model), F32)
    for copy in (to_x, to_y, fwd_x, fwd_y):
        copy.wait_send()


def frames_f32(block):
    return block.astype(F32)


GELU_SCALE = 0.7978845608028654


ORDER = (1, 0, 2, 3, 4, 5, 6, 7)
DEEP = (0, 4)
FLAT = (1, 2, 3, 5, 6, 7)


def backward_kernel(
    act, gm_t, h3, gpre, h2, cross, attn, mods, early, text, g_cross,
    seg_s, seg, query_h, kv_h, h_all_h, lse_h, frames_h, w_qkv_h,
    gqc_h, gkvc_h, cot_h, branch_h, x_one_h, x_two_h, up_h, prob_h, w_co, w_cq, w_out, w_ckv,
    out, d_frames, d_text, e_all, l_all,
    G, R0, R1, R2, R3, R4, dqkv, up_low, T, late,
    gattn, gx1, kv, h_all, lse, w_qkv, local,
    gqc, gkvc, gc, ga, branch, x_one, x_two, prob_c,
    s0, r0, s1, r1, s2, r2, s3, r3, s4, r4, se, re, sl, rl, st, rt, free,
):
    seq = lax.axis_index("seq")
    rows = lax.axis_index("rows")
    y, x = seq // 2, seq % 2
    z, c = rows // 2, rows % 2
    core_peer = {"rows": z * 2 + (1 - c)}
    x_id, y_id = y * 2 + 1 - x, (1 - y) * 2 + x
    x_peer, y_peer = {"seq": x_id}, {"seq": y_id}
    z_peers = [{"rows": lax.rem(z + d, 4) * 2 + c} for d in (1, 2, 3)]
    zh, zl = z // 2, z % 2
    near_peer = {"rows": (zh * 2 + 1 - zl) * 2 + c}
    far_peer = {"rows": ((1 - zh) * 2 + zl) * 2 + c}
    here, model = gc.shape
    first_loads = [
        (up_h, d_frames), (x_two_h, x_two), (cot_h.at[0], gattn),
        (w_co, dqkv.at[:model, :model]), (gkvc_h, gkvc), (gqc_h, gqc), (prob_h, prob_c),
        (w_cq, dqkv.at[:model, model : 2 * model]), (x_one_h, x_one), (branch_h, branch),
        (w_ckv, w_qkv.at[:, : 2 * model]), (w_out, dqkv.at[:model, 2 * model :]),
        (kv_h, kv), (lse_h, lse), (h_all_h, h_all),
        (query_h, gqc), (frames_h.at[0], gc), (w_qkv_h, w_qkv),
    ]
    loads = [
        pltpu.make_async_copy(src, dst, local.at[i]) for i, (src, dst) in enumerate(first_loads)
    ]
    last_load = loads.pop()
    frames_load = loads.pop()
    query_load = loads.pop()
    for load in loads:
        load.start()
    enter([core_peer, x_peer, y_peer] + z_peers)

    tall, width = G.shape[-2:]
    mask = seg[...] == seg_s[0, seq * here]

    def gather_copies(table, send, recv):
        mine, line, sheet = table.at[c, z, y, x], table.at[c, :, y, x], table.at[c, :, y]
        return (
            [
                remote(mine, mine, send.at[d - 1], recv.at[d - 1], z_peers[d - 1])
                for d in (1, 2, 3)
            ],
            [remote(line, line, send.at[3], recv.at[3], x_peer)],
            [remote(sheet, sheet, send.at[4], recv.at[4], y_peer)],
            [remote(table.at[c], table.at[c], send.at[5], recv.at[5], core_peer)],
        )

    early_steps = gather_copies(e_all, se, re)
    late_steps = gather_copies(l_all, sl, rl)
    text_steps = (
        [remote(T.at[y, x], T.at[y, x], st.at[0], rt.at[0], x_peer)],
        [remote(T.at[y], T.at[y], st.at[1], rt.at[1], y_peer)],
    )

    def advance(steps, at):
        if at:
            for copy in steps[at - 1]:
                copy.wait_recv()
        if at < len(steps):
            for copy in steps[at]:
                copy.start()

    def put(k, s, block):
        low = block.astype(BF16)
        for zz in range(4):
            for cc in range(2):
                at = (zz * 2 + cc) * tall
                G[k, cc, zz, s // 2, s % 2] = low[at : at + tall]

    def put_lanes(k, s, lane, block):
        low = block.astype(BF16)
        for zz in range(4):
            for cc in range(2):
                at = (zz * 2 + cc) * tall
                G[k, cc, zz, s // 2, s % 2, :, lane : lane + 128] = low[at : at + tall]

    def shared(s, first_left, first, second_left, second):
        parity = s % 2
        half_of = (~low_half(first.shape)).astype(jnp.int32)
        first = jnp.where(half_of == parity, first, jnp.zeros_like(first))
        turned = pltpu.roll(second.astype(F32), HEAD, 1)
        half_of = (~low_half(turned.shape)).astype(jnp.int32)
        turned = jnp.where(half_of == parity, 0.0, turned).astype(BF16)
        return t_dot(first_left, first) + t_dot(second_left, turned)

    def compute(k):
        @pl.loop(0, 4)
        def _(s):
            full = s + (s + 1) // 2
            split = 1 + 3 * (s // 2)
            wide = 4 * s + (s + 1) // 2
            if k < 2:
                left = gm_t[pl.ds(pl.multiple_of(s * 2 * tall + k * tall, 16), tall), :]
                for r in range(8):
                    G[k, r % 2, r // 2, s // 2, s % 2] = dot(
                        left, act[:, r * width : (r + 1) * width]
                    ).astype(BF16)
            elif k < 4:
                put(k, s, t_dot(h3[...], gpre[:, lanes(s * 6 + (k - 2) * 3, 3)]))
            elif k == 4:
                put_lanes(k, s, 0, t_dot(h2[...], gqc[:, lanes(full)]))
                put_lanes(k, s, 128, t_dot(cross[...], gc[:, lanes(full)]))
                put_lanes(
                    k, s, 256,
                    shared(s, h2[...], gqc[:, lanes(split)], cross[...], gc[:, lanes(split)]),
                )
            elif k == 5:
                put(k, s, t_dot(text[...], gkvc[:, lanes(s * 3, 3)]))
            elif k == 6:
                put(k, s, t_dot(h_all[...], dqkv[:, lanes(wide, 3)]))
            else:
                put_lanes(k, s, 0, t_dot(h_all[...], dqkv[:, lanes(wide + 3)]))
                put_lanes(
                    k, s, 128,
                    shared(
                        s, h_all[...], dqkv[:, lanes(4 + 9 * (s // 2))],
                        attn[...], ga[:, lanes(split)],
                    ),
                )
                put_lanes(k, s, 256, t_dot(attn[...], ga[:, lanes(full)]))

    def core_copy(k):
        return remote(G.at[k, 1 - c], R0.at[ORDER.index(k) % 2], s0.at[k], r0.at[k], core_peer)

    def first_copies(k):
        return (
            remote(G.at[k, c, 0:2, :, 1 - x], R1.at[k, 0], s1.at[k, 0], r1.at[k, 0], x_peer),
            remote(G.at[k, c, 2:4, 1 - y], R1.at[k, 1], s1.at[k, 1], r1.at[k, 1], y_peer),
        )

    def second_copies(k):
        return (
            remote(G.at[k, c, 0:2, 1 - y, x], R2.at[k, 0], s2.at[k, 0], r2.at[k, 0], y_peer),
            remote(G.at[k, c, 2:4, y, 1 - x], R2.at[k, 1], s2.at[k, 1], r2.at[k, 1], x_peer),
        )

    def z_near(k):
        return [
            remote(
                G.at[k, c, h * 2 + 1 - zl, y, x], R3.at[k, h],
                s3.at[k, h], r3.at[k, h], near_peer,
            )
            for h in range(2)
        ]

    def z_far(k):
        return remote(
            G.at[k, c, (1 - zh) * 2 + zl, y, x], R3.at[k, 2], s3.at[k, 2], r3.at[k, 2], far_peer
        )

    def near_copies(k):
        return [
            remote(
                G.at[k, c, h * 2 + 1 - zl], R1.at[k, h], s3.at[k, h], r3.at[k, h], near_peer
            )
            for h in range(2)
        ]

    def far_copy(k):
        return remote(
            G.at[k, c, (1 - zh) * 2 + zl], R2.at[k], s3.at[k, 2], r3.at[k, 2], far_peer
        )

    def pair_copies(k):
        if k == 0:
            return [
                remote(
                    G.at[k, c, z, other, 1 - x], R3.at[k, other],
                    s1.at[k, other], r1.at[k, other], x_peer,
                )
                for other in range(2)
            ]
        return [
            remote(
                G.at[k, c, z, 1 - y, other], R3.at[k, other],
                s1.at[k, other], r1.at[k, other], y_peer,
            )
            for other in range(2)
        ]

    def last_copy(k):
        if k == 0:
            return remote(
                G.at[k, c, z, 1 - y, x], R3.at[k, 2], s2.at[k, 0], r2.at[k, 0], y_peer
            )
        return remote(G.at[k, c, z, y, 1 - x], R3.at[k, 2], s2.at[k, 0], r2.at[k, 0], x_peer)

    def add(one, two):
        return (one.astype(F32) + two.astype(F32)).astype(BF16)

    def deep1(k):
        core_add(k)
        for copy in near_copies(k):
            copy.start()

    def deep2(k):
        for copy in near_copies(k):
            copy.wait_recv()
        for h in range(2):
            for yy in range(2):
                for xx in range(2):
                    at = h * 2 + zl
                    G[k, c, at, yy, xx] = add(G[k, c, at, yy, xx], R1[k, h, yy, xx])
        far_copy(k).start()

    def deep3(k):
        far_copy(k).wait_recv()
        for yy in range(2):
            for xx in range(2):
                G[k, c, z, yy, xx] = add(G[k, c, z, yy, xx], R2[k, yy, xx])
        for copy in pair_copies(k):
            copy.start()

    def deep4(k):
        for copy in pair_copies(k):
            copy.wait_recv()
        for other in range(2):
            if k == 0:
                G[k, c, z, other, x] = add(G[k, c, z, other, x], R3[k, other])
            else:
                G[k, c, z, y, other] = add(G[k, c, z, y, other], R3[k, other])
        last_copy(k).start()

    def deep5(k):
        last_copy(k).wait_recv()
        out[k] = G[k, c, z, y, x].astype(F32) + R3[k, 2].astype(F32)

    def deep_copies(k):
        return near_copies(k) + [far_copy(k)] + pair_copies(k) + [last_copy(k)]

    def phase0(k):
        compute(k)
        if ORDER.index(k) >= 2:
            pl.semaphore_wait(free, 1)
        core_copy(k).start()

    def core_add(k):
        core_copy(k).wait_recv()

        @pl.loop(0, 4)
        def _(zz):
            for yy in range(2):
                for xx in range(2):
                    G[k, c, zz, yy, xx] = add(G[k, c, zz, yy, xx], R0[ORDER.index(k) % 2, zz, yy, xx])

        if ORDER.index(k) < CHUNKS - 2:
            pl.semaphore_signal(free, inc=1, device_id=core_peer, device_id_type=MESH)

    def phase1(k):
        core_add(k)
        for copy in first_copies(k):
            copy.start()

    def phase2(k):
        for copy in first_copies(k):
            copy.wait_recv()
        for zz in range(2):
            for other in range(2):
                G[k, c, zz, other, x] = add(G[k, c, zz, other, x], R1[k, 0, zz, other])
                G[k, c, 2 + zz, y, other] = add(G[k, c, 2 + zz, y, other], R1[k, 1, zz, other])
        for copy in second_copies(k):
            copy.start()

    def phase3(k):
        for copy in second_copies(k):
            copy.wait_recv()
        for zz in range(2):
            G[k, c, zz, y, x] = add(G[k, c, zz, y, x], R2[k, 0, zz])
            G[k, c, 2 + zz, y, x] = add(G[k, c, 2 + zz, y, x], R2[k, 1, zz])
        for copy in z_near(k):
            copy.start()

    def phase4(k):
        for copy in z_near(k):
            copy.wait_recv()
        for h in range(2):
            at = h * 2 + zl
            G[k, c, at, y, x] = add(G[k, c, at, y, x], R3[k, h])
        z_far(k).start()

    def phase5(k):
        z_far(k).wait_recv()
        out[k] = G[k, c, z, y, x].astype(F32) + R3[k, 2].astype(F32)

    phase0(1)
    phase0(0)
    phase1(1)
    phase0(2)
    deep1(0)
    phase0(3)
    phase1(2)
    phase1(3)
    for load in loads:
        load.wait()

    def row(at):
        return mods[at : at + 1, :]

    co_v, cq_v = dqkv.at[:model, :model], dqkv.at[:model, model : 2 * model]
    out_v, ckv_v = dqkv.at[:model, 2 * model :], w_qkv.at[:, : 2 * model]
    normed_2, inverse_2 = norm_parts(x_two[...])
    gx1[...] = gattn[...].astype(F32) + norm_back(
        normed_2, inverse_2, d_frames[...] * (1.0 + row(4))
    )
    gc[...] = gx1[...].astype(BF16)
    ga[...] = dot_t(gc[...], co_v[...]).astype(BF16)

    @pl.loop(0, HEADS // 2, unroll=True)
    def _(p):
        at = lanes(p)
        value_at = lanes(p + HEADS // 2)
        key_pair, value_pair = gkvc[:, at], gkvc[:, value_at]
        query_pair, up_pair = gqc[:, at], ga[:, at]
        d_q, d_k, d_v = [], [], []
        for half in range(2):
            low = prob_c[2 * p + half]
            probs = low.astype(F32)
            grad_probs = dot_t(pick_half(up_pair, half), value_pair)
            inner = jnp.sum(probs * grad_probs, axis=-1, keepdims=True)
            grad_scores = (probs * (grad_probs - inner)).astype(BF16)
            d_q.append(dot(grad_scores, key_pair))
            d_k.append(t_dot(grad_scores, query_pair))
            d_v.append(t_dot(low, up_pair))
        gqc[:, at] = (join_halves(*d_q) * HEAD ** (-0.5)).astype(BF16)
        gkvc[:, at] = (join_halves(*d_k) * HEAD ** (-0.5)).astype(BF16)
        gkvc[:, value_at] = join_halves(*d_v).astype(BF16)

    phase2(1)
    T[y, x] = dot_t(gkvc[: T.shape[2], :], ckv_v[...]).astype(BF16)
    last_load.start()
    advance(text_steps, 0)
    normed_1, inverse_1 = norm_parts(x_one[...])
    up_two = dot_t(gqc[...], cq_v[...])
    grad_x1 = gx1[...] + norm_back(normed_1, inverse_1, up_two * g_cross[...].astype(F32)[None])
    gx1[...] = grad_x1
    ga[...] = (row(2) * grad_x1).astype(BF16)
    gattn[...] = dot_t(ga[...], out_v[...]).astype(BF16)
    row_of = lax.broadcasted_iota(jnp.int32, early.shape, 0)
    whole = jnp.where(row_of == 0, col_sum(grad_x1 * branch[...]), early[...])
    whole = jnp.where(row_of == 4, col_sum(up_two * normed_1), whole)
    e_all[c, z, y, x] = whole.astype(BF16)
    advance(early_steps, 0)
    phase0(4)
    frames_load.start()
    query_load.start()
    phase0(5)
    deep1(4)
    phase1(5)
    phase2(2)
    deep2(0)
    advance(early_steps, 1)
    advance(text_steps, 1)
    phase2(3)

    query_load.wait()
    own = pl.ds(pl.multiple_of(seq * here, here), here)
    dqkv[:, :model] = jnp.zeros((dqkv.shape[0], model), BF16)
    lane_of = lax.broadcasted_iota(jnp.int32, lse.shape, 1)
    @pl.loop(0, HEADS // 2)
    def _(p):
        at = lanes(p)
        key_at = lanes(p + HEADS // 2)
        value_at = lanes(p + HEADS)
        key_pair, value_pair = kv[:, at], kv[:, key_at]
        query_pair, up_pair = gqc[:, at], gattn[:, at]
        scaled = query_pair * jnp.asarray(HEAD ** (-0.5), BF16)
        d_q, d_k, d_v = [], [], []
        for half in range(2):
            scores = dot_t(pick_half(scaled, half), key_pair)
            log_total = jnp.sum(
                jnp.where(lane_of == 2 * p + half, lse[...], 0.0), axis=-1, keepdims=True
            )
            scores = jnp.where(mask, scores, NEG_FILL)
            probs = jnp.exp(scores - log_total)
            grad_probs = dot_t(pick_half(up_pair, half), value_pair)
            inner = jnp.sum(probs * grad_probs, axis=-1, keepdims=True)
            grad_scores = (probs * (grad_probs - inner)).astype(BF16)
            d_q.append(dot(grad_scores, key_pair))
            d_k.append(t_dot(grad_scores, query_pair))
            d_v.append(t_dot(probs.astype(BF16), up_pair))
        dqkv[own, at] = (join_halves(*d_q) * HEAD ** (-0.5)).astype(BF16)
        dqkv[:, key_at] = (join_halves(*d_k) * HEAD ** (-0.5)).astype(BF16)
        dqkv[:, value_at] = join_halves(*d_v).astype(BF16)

    def up_block(block):
        rows_at = pl.ds(pl.multiple_of(block * here, here), here)
        return dot_t(dqkv[rows_at, model:], w_qkv[:, model:])

    part = here // 2
    up_first = (
        remote(up_low.at[:, 1 - x, :part], R4.at[0:2], s4.at[0], r4.at[0], x_peer),
        remote(up_low.at[1 - y, :, part:], R4.at[2:4], s4.at[1], r4.at[1], y_peer),
    )
    up_second = (
        remote(up_low.at[1 - y, x, :part], R4.at[4], s4.at[2], r4.at[2], y_peer),
        remote(up_low.at[y, 1 - x, part:], R4.at[5], s4.at[3], r4.at[3], x_peer),
    )
    last_load.wait()
    advance(early_steps, 2)
    for block in range(4):
        up_low[block // 2, block % 2] = up_block(block).astype(BF16)
    for copy in up_first:
        copy.start()
    phase0(6)
    phase3(1)
    deep3(0)
    phase0(7)
    phase1(6)
    deep2(4)
    phase1(7)
    phase3(2)
    phase4(1)
    phase2(5)
    phase3(3)
    phase4(2)
    for copy in up_first:
        copy.wait_recv()
    for i in range(2):
        up_low[i, x, :part] = add(up_low[i, x, :part], R4[i])
        up_low[y, i, part:] = add(up_low[y, i, part:], R4[2 + i])
    for copy in up_second:
        copy.start()
    advance(early_steps, 3)
    advance(text_steps, 2)
    deep4(0)
    deep3(4)
    phase4(3)
    phase3(5)
    deep5(0)
    phase2(6)
    deep4(4)
    for copy in up_second:
        copy.wait_recv()
    up_one = dot_t(dqkv[own, :model], w_qkv[:, :model]) + up_low[y, x].astype(F32)
    up_one = up_one + jnp.concatenate([R4[4], R4[5]], axis=0).astype(F32)
    frames_load.wait()
    normed, inverse = norm_parts(gc[...].astype(F32))
    for i, total in enumerate((col_sum(up_one), col_sum(up_one * normed))):
        for j in range(model // 128):
            at = i * (model // 128) + j
            late[at : at + 1, :] = total[:, j * 128 : (j + 1) * 128]
    late[2 * (model // 128) :, :] = jnp.zeros((16 - 2 * (model // 128), 128), F32)
    d_frames[...] = gx1[...] + norm_back(normed, inverse, up_one * (1.0 + mods[1:2, :]))
    l_all[c, z, y, x] = late[...].astype(BF16)
    advance(late_steps, 0)
    total = jnp.zeros(d_text.shape, F32)
    for i in range(4):
        total = total + T[i // 2, i % 2].astype(F32) * jnp.where(
            seg_s[0, i * here] == seq, 1.0, 0.0
        )
    d_text[...] = total
    phase4(5)
    phase3(6)
    advance(late_steps, 1)
    phase2(7)
    deep5(4)
    phase4(6)
    advance(late_steps, 2)
    phase3(7)
    advance(late_steps, 3)
    for k in FLAT[:-2]:
        phase5(k)
    phase4(7)
    for k in FLAT[-2:]:
        phase5(k)
    advance(early_steps, 4)
    advance(late_steps, 4)
    for k in range(CHUNKS):
        core_copy(k).wait_send()
    for k in DEEP:
        for copy in deep_copies(k):
            copy.wait_send()

    for k in FLAT:
        for copy in (*first_copies(k), *second_copies(k), *z_near(k), z_far(k)):
            copy.wait_send()

    for copy in (*up_first, *up_second):
        copy.wait_send()
    for steps in (early_steps, late_steps, text_steps):
        for step in steps:
            for copy in step:
                copy.wait_send()


def in_vmem(count):
    return [pl.BlockSpec(memory_space=pltpu.VMEM)] * count


def in_any(count):
    return [pl.BlockSpec(memory_space=pl.ANY)] * count


def finish_kernel(
    done, d_frames_in, d_text_in, output_in, e_all, l_all, step, seg_s, w_ada,
    output, d_frames, d_text, d_step, d_w_ada, d_b_ada, d_w_qkv, d_w_out, d_g_cross,
    d_w_cq, d_w_ckv, d_w_co, d_w_up, d_b_up, d_w_down, d_b_down,
    item, ada, ada_t,
):
    seq = lax.axis_index("seq")
    rows = lax.axis_index("rows")
    here, model = output_in.shape
    parts = model // 128
    output[0] = output_in[...]
    d_frames[0] = d_frames_in[...]
    d_text[:, 0, :] = d_text_in[: d_text.shape[0], :]
    bias_sum = jnp.zeros((16, model), F32)
    for r in range(8):
        for s in range(4):
            entry = e_all[r % 2, r // 2, s // 2, s % 2].astype(F32)
            tail = l_all[r % 2, r // 2, s // 2, s % 2].astype(F32)
            bias_sum = bias_sum + entry
            at = slice(r * 4 + s, r * 4 + s + 1)
            ada[at, :] = entry[10:11]
            for j in range(4):
                item[at, (2 + j) * model : (3 + j) * model] = entry[j : j + 1]
            for j in range(2 * parts):
                item[at, j * 128 : (j + 1) * 128] = tail[j : j + 1]
    item_sum = jnp.sum(item[...], axis=0, keepdims=True)

    def share(pieces):
        total = jnp.zeros_like(pieces[0])
        for r, piece in enumerate(pieces):
            total = total + jnp.where(rows == r, piece, jnp.zeros_like(piece))
        return total

    def cut(row, size):
        return [row[:, at * size : (at + 1) * size] for at in range(row.shape[1] // size)]

    d_b_ada[...] = share(cut(item_sum, 6 * model // 8)).reshape(6 * model // 8)
    d_g_cross[...] = share(cut(bias_sum[4:5], model // 8)).reshape(model // 8)
    d_b_down[...] = share(cut(bias_sum[9:10], model // 8)).reshape(model // 8)
    d_b_up[...] = share(
        [piece for at in range(5, 9) for piece in cut(bias_sum[at : at + 1], model // 2)]
    ).reshape(model // 2)
    ada_t[...] = ada[...].T
    tall = model // 8
    share_at = pl.ds(pl.multiple_of(seq * 9 * 128, 128), 9 * 128)
    d_w_ada[...] = jnp.dot(
        ada_t[pl.ds(pl.multiple_of(rows * tall, 8), tall), :],
        item[:, share_at],
        precision=PRECISE,
        preferred_element_type=F32,
    )
    near = item[pl.ds(pl.multiple_of(rows // 2 * 8, 8), 8), :]
    total = jnp.zeros((1, 6 * model), F32)
    for j in range(8):
        wanted = jnp.where(seg_s[0, j % 4 * here] == seq, 1.0, 0.0)
        wanted = jnp.where(rows % 2 == j // 4, wanted, 0.0)
        total = total + near[j : j + 1] * wanted
    high = total.astype(BF16)
    low = (total - high.astype(F32)).astype(BF16)
    both = jnp.concatenate(
        [high.astype(F32), low.astype(F32), jnp.zeros((6, 6 * model), F32)], axis=0
    ).astype(BF16)
    d_ada = jnp.sum(dot_t(both, w_ada[...]), axis=0, keepdims=True)
    all_steps = step[0].astype(F32)
    my_step = jnp.zeros((1, model), F32)
    for j in range(4):
        my_step = my_step + all_steps[j : j + 1] * jnp.where(seq == j, 1.0, 0.0)
    gate = 1.0 / (1.0 + jnp.exp(-my_step))
    d_step[0] = d_ada * gate * (1.0 + my_step * (1.0 - gate))
    odd = seq % 2 == 1

    def place(full, mixed, first):
        even = mixed[:, :HEAD] if first else mixed[:, HEAD:]
        other = mixed[:, HEAD:] if first else mixed[:, :HEAD]
        return jnp.where(
            odd,
            jnp.concatenate([other, full], axis=1),
            jnp.concatenate([full, even], axis=1),
        )

    width = model // 2
    d_w_down[: model // 8] = done[0]
    d_w_down[model // 8 :] = done[1]
    d_w_up[:, :width] = done[2]
    d_w_up[:, width:] = done[3]
    cross, last = done[4], done[7]
    d_w_cq[...] = place(cross[:, :128], cross[:, 256:], True)
    d_w_co[...] = place(cross[:, 128:256], cross[:, 256:], False)
    d_w_ckv[...] = done[5]
    d_w_qkv[...] = place(
        jnp.concatenate([done[6], last[:, :128]], axis=1), last[:, 128:256], True
    )
    d_w_out[...] = place(last[:, 256:], last[:, 128:256], False)


def smem(count):
    return [pl.BlockSpec(memory_space=pltpu.SMEM)] * count


def per_device(
    frames, text_tokens, step_embed, segments, cotangent,
    w_ada, b_ada, w_qkv, w_out, g_cross, w_cq, w_ckv, w_co, w_up, b_up, w_down, b_down,
):
    seq_count = lax.axis_size("seq")
    rows_count = lax.axis_size("rows")
    here, model = frames.shape[1:]
    length = segments.shape[1]
    hidden = w_up.shape[1]
    assert (length // ITEMS) % here == 0
    text_rows, text_kept, step_rows = 128, 80, 16

    def like(shape, dtype=BF16):
        return jax.ShapeDtypeStruct(shape, dtype)

    square = like((here, model))
    dma = pltpu.SemaphoreType.DMA
    vmem = pltpu.VMEM
    wide = like((here, model), F32)
    (
        output, act, gm_t, h3, gpre, h2, cross, gqc, gkvc, attn, query,
        kv, h_all, lse, mods, early, text_mine, branch, x_one, x_two, up_three, prob_c,
    ) = pl.pallas_call(
        forward_kernel,
        out_shape=(
            square, like((here, hidden)), like((model, here)), square, like((here, hidden)),
            square, square, square, like((text_rows, 2 * model)), square, square,
            like((length, 2 * model)), like((length, model)), like((here, 128), F32),
            like((8, model), F32), like((16, model), F32), like((text_rows, model)),
            wide, wide, wide, wide, like((HEADS, here, text_rows)),
        ),
        in_specs=in_any(1) + in_vmem(3) + smem(1) + in_vmem(1)
        + in_any(1) + in_vmem(1) + in_any(2) + in_vmem(1) + in_any(4) + in_vmem(1)
        + in_any(1) + in_vmem(1),
        out_specs=tuple(in_vmem(22)),
        scratch_shapes=[
            vmem((seq_count, here, model), BF16),
            vmem(w_ada.shape, BF16), vmem(w_qkv.shape, BF16), vmem(w_out.shape, BF16),
            vmem(w_cq.shape, BF16), vmem(w_ckv.shape, BF16), vmem(w_co.shape, BF16),
            vmem(w_up.shape, BF16), vmem(w_down.shape, BF16),
            vmem((here, model), BF16), vmem((here, model), F32),
            vmem((step_rows, 6 * model), F32),
            vmem((1, hidden), F32),
            dma((9,)), dma((4,)), dma((4,)),
        ],
        compiler_params=pltpu.CompilerParams(
            collective_id=0, has_side_effects=True, vmem_limit_bytes=VMEM_MOST
        ),
        name="forward_layer",
    )(
        frames, cotangent, text_tokens, step_embed, segments, segments,
        w_ada, b_ada, w_qkv, w_out, g_cross, w_cq, w_ckv, w_co, w_up, b_up, w_down, b_down,
    )

    tall, width = model // rows_count, model // 2
    table = (2, 4, 2, 2)
    done, d_frames, d_text, e_all, l_all = pl.pallas_call(
        backward_kernel,
        out_shape=(
            like((CHUNKS, tall, width), F32), like((here, model), F32),
            like((text_kept, model), F32), like(table + (16, model)),
            like(table + (16, 128)),
        ),
        in_specs=in_vmem(11) + smem(1) + in_vmem(1) + in_any(18),
        out_specs=tuple(in_vmem(5)),
        scratch_shapes=[
            vmem((CHUNKS,) + table + (tall, width), BF16),
            vmem((2, 4, 2, 2, tall, width), BF16),
            vmem((CHUNKS, 2, 2, 2, tall, width), BF16),
            vmem((CHUNKS, 2, 2, tall, width), BF16),
            vmem((CHUNKS, 3, tall, width), BF16),
            vmem((6, here // 2, model), BF16),
            vmem((length, 3 * model), BF16),
            vmem((2, 2, here, model), BF16),
            vmem((2, 2, text_kept, model), BF16),
            vmem((16, 128), F32),
            vmem((here, model), BF16), vmem((here, model), F32),
            vmem((length, 2 * model), BF16), vmem((length, model), BF16),
            vmem((here, 128), F32), vmem(w_qkv.shape, BF16),
            dma((18,)),
            vmem((here, model), BF16), vmem((text_rows, 2 * model), BF16),
            vmem((here, model), BF16), vmem((here, model), BF16),
            vmem((here, model), F32), vmem((here, model), F32), vmem((here, model), F32),
            vmem((HEADS, here, text_rows), BF16),
            dma((CHUNKS,)), dma((CHUNKS,)),
            dma((CHUNKS, 2)), dma((CHUNKS, 2)),
            dma((CHUNKS, 2)), dma((CHUNKS, 2)),
            dma((CHUNKS, 3)), dma((CHUNKS, 3)),
            dma((4,)), dma((4,)), dma((6,)), dma((6,)), dma((6,)), dma((6,)),
            dma((2,)), dma((2,)), pltpu.SemaphoreType.REGULAR,
        ],
        compiler_params=pltpu.CompilerParams(
            collective_id=1, has_side_effects=True, vmem_limit_bytes=VMEM_MOST
        ),
        name="backward_layer",
    )(
        act, gm_t, h3, gpre, h2, cross, attn, mods, early, text_mine, g_cross,
        segments, segments, query, kv, h_all, lse, frames, w_qkv,
        gqc, gkvc, cotangent, branch, x_one, x_two, up_three, prob_c, w_co, w_cq, w_out, w_ckv,
    )

    def shard(*shape):
        return like(shape, F32)

    seq_share = model // seq_count
    results = pl.pallas_call(
        finish_kernel,
        out_shape=(
            like((1, here, model)), shard(1, here, model), shard(TXT, 1, model),
            shard(1, 1, model), shard(tall, 6 * seq_share), shard(6 * tall),
            shard(tall, 3 * seq_share), shard(tall, seq_share), shard(tall),
            shard(tall, seq_share), shard(tall, 2 * seq_share), shard(tall, seq_share),
            shard(tall, hidden // seq_count), shard(hidden // rows_count),
            shard(seq_share, hidden // rows_count), shard(tall),
        ),
        in_specs=in_vmem(7) + smem(1) + in_vmem(1),
        out_specs=tuple(in_vmem(16)),
        scratch_shapes=[
            vmem((32, 6 * model), F32), vmem((32, model), F32), vmem((model, 32), F32),
        ],
        compiler_params=pltpu.CompilerParams(vmem_limit_bytes=VMEM_MOST),
        name="finish_layer",
    )(done, d_frames, d_text, output, e_all, l_all, step_embed, segments, w_ada)
    results = list(results)
    results[2] = results[2].transpose(1, 0, 2)
    results[14] = results[14].T
    return tuple(results)


def solution(mesh):
    row_seq = P("rows", "seq", None)
    in_specs = (
        row_seq, P("rows", None, None), P("rows", None, None), P("rows", None), row_seq,
    ) + (P(),) * 12
    out_specs = (row_seq,) * 4 + (
        P("rows", "seq"), P("rows"), P("rows", "seq"), P("rows", "seq"), P("rows"),
        P("rows", "seq"), P("rows", "seq"), P("rows", "seq"), P("rows", "seq"), P("rows"),
        P("rows", "seq"), P("rows"),
    )
    fused = mesh.shape["rows"] == 8 and mesh.shape["seq"] == 4
    return jax.shard_map(
        per_device if fused else per_device_plain, mesh=mesh, in_specs=in_specs, out_specs=out_specs, check_vma=False
    )
```
